32 devices in a mesh: dp: 4 (over z), row: 4 (over x, core), col: 2 (over y).
Axes of the slice: x: 2, y: 2, z: 4, core: 2. Of those that a mesh axis runs over, the one named last changes fastest.
Arguments:
- inputs: bfloat16 [2, 32768, 768], P(None, ('dp', 'row', 'col')), may hold values from -6 to 6
- qkv_weight: bfloat16 [768, 2304], P('row', 'col'), may hold values from -0.3125 to 0.3125
- out_weight: bfloat16 [768, 768], P('row', 'col'), may hold values from -0.625 to 0.625
- up_weight: bfloat16 [768, 3072], P('row', 'col'), may hold values from -0.21875 to 0.21875
- down_weight: bfloat16 [3072, 768], P('row', 'col'), may hold values from -0.15625 to 0.15625
- vectors: float32 [768, 8], replicated, may hold values from -1 to 2
- up_bias: float32 [3072], replicated, may hold values from -1.2 to 1.2
- cont_lengths: int32 [2, 16, 8], P(None, ('dp', 'row')), may hold values from 1 to 128
- out_cotangent: bfloat16 [2, 32768, 768], P(None, ('dp', 'row', 'col')), may hold values from -6 to 6
Outputs:
- outputs: bfloat16 [2, 32768, 768], P(None, ('dp', 'row', 'col'))
- input_grad: bfloat16 [2, 32768, 768], P(None, ('dp', 'row', 'col'))
- qkv_grad: float32 [768, 2304], P('row', 'col')
- out_grad: float32 [768, 768], P('row', 'col')
- up_grad: float32 [768, 3072], P('row', 'col')
- down_grad: float32 [3072, 768], P('row', 'col')
- vector_grad: float32 [768, 8], P(('row', 'col'))
- up_bias_grad: float32 [3072], P(('row', 'col'))
The draws below stay inside these ranges and needn't reach their ends.
All inputs are finite; a program needn't handle non-finite values.
Results may differ from the reference program's by a relative error of at most 0.017.
Values may be sent and summed in bfloat16 or wider, within the bound.
A program may use at most 256 MiB of HBM per device.

```python
import jax
import jax.numpy as jnp
from jax import lax

D = 768
H = 12
DH = 64
FF = 3072
PROMPT = 1024
CLEN = 128
MICRO = 2
CONTS = 8
GROUPS = 16
TOKENS = 32768


def draw_vectors(key, part):
    noise = jax.random.truncated_normal(key, -4.0, 4.0, (D, 8), jnp.float32)
    centre = jnp.array([0.0, 0.0, 0.0, 1.0, 0.0, 0.0, 1.0, 0.0], jnp.float32)
    spread = jnp.array([0.2, 0.2, 0.2, 0.1, 0.2, 0.2, 0.1, 0.2], jnp.float32)
    return centre + spread * noise


def plant(values, rng, low, largest):
    longest = values.shape.index(max(values.shape))
    spots = []
    for shift in (0, 1):
        where = [jax.random.randint(jax.random.fold_in(rng, axis), (), 0, length) for axis, length in enumerate(values.shape)]
        where[longest] = (where[longest] + shift) % values.shape[longest]
        spots.append(tuple(where))
    return values.at[spots[0]].set(low).at[spots[1]].set(largest)


def block_levels(rng, dims, split, least, top_value):
    level, own = 1.0, jax.random.fold_in(rng, 6)
    for position, parts in split:
        heights = jnp.exp(jax.random.uniform(jax.random.fold_in(own, position), (parts,), jnp.float32, least / len(split), top_value / len(split)))
        level = level * jnp.repeat(heights, dims[position] // parts).reshape([-1 if axis == position else 1 for axis in range(len(dims))])
    return level


def gaussian(rng, shape, scale, bound, cuts=(), kind=jnp.bfloat16):
    values = jax.random.normal(rng, shape, jnp.float32) * scale
    if len(cuts) > 0:
        values = block_levels(rng, shape, cuts, -0.22, 0.18) * values
    return jnp.clip(values, min=-bound, max=bound).astype(kind)


def setup_inputs(seed: int = 0) -> dict:
    key_of = jax.random.split(jax.random.key(seed), 10)
    inputs = gaussian(key_of[0], (MICRO, TOKENS, D), 1.0, 6.0, ((1, 32),))
    qkv_weight = gaussian(key_of[1], (D, 3 * D), (D // 2) ** -0.5, 0.3125, ((0, 4), (1, 2)))
    out_weight = gaussian(key_of[2], (D, D), (D // 8) ** -0.5, 0.625, ((0, 4), (1, 2)))
    up_weight = gaussian(key_of[3], (D, FF), D ** -0.5, 0.21875, ((0, 4), (1, 2)))
    down_weight = gaussian(key_of[4], (FF, D), (FF // 2) ** -0.5, 0.15625, ((0, 4), (1, 2)))
    vectors = draw_vectors(jax.random.fold_in(key_of[9], 71), 0)
    up_bias = gaussian(key_of[6], (FF,), 0.2, 1.2, (), jnp.float32)
    cont_lengths = plant(jax.random.randint(key_of[7], (MICRO, GROUPS, CONTS), 1, CLEN + 1), jax.random.fold_in(key_of[7], 1), 1, CLEN).astype(jnp.int32)
    out_cotangent = gaussian(key_of[8], (MICRO, TOKENS, D), 1.0, 6.0, ((1, 32),))
    return {"inputs": inputs, "qkv_weight": qkv_weight, "out_weight": out_weight, "up_weight": up_weight, "down_weight": down_weight, "vectors": vectors, "up_bias": up_bias, "cont_lengths": cont_lengths, "out_cotangent": out_cotangent}


@jax.custom_vjp
def low(v):
    return lax.optimization_barrier(v.astype(jnp.bfloat16)).astype(jnp.float32)

@jax.custom_vjp
def low_back(v):
    return v

def low_keep(v):
    return (low(v), None)

def low_pass(kept, grad):
    return (grad,)

def back_keep(v):
    return (v, None)

def back_low(kept, grad):
    return (low(grad),)
low.defvjp(low_keep, low_pass)
low_back.defvjp(back_keep, back_low)
EPSILON = 1e-05

def product(left, right):
    return jnp.dot(left, right, precision=lax.Precision.HIGHEST, preferred_element_type=jnp.float32)

def layer_norm(value, gain, shift):
    average = lax.optimization_barrier(jnp.mean(value, axis=-1, keepdims=True))
    centred = value - average
    spread = lax.optimization_barrier(jnp.mean(centred * centred, axis=-1, keepdims=True))
    return centred * lax.rsqrt(spread + EPSILON) * gain + shift

def regroup(value):
    half = PROMPT // 2
    return jnp.concatenate([value[:half], value[PROMPT:PROMPT + half], value[half:PROMPT], value[PROMPT + half:]], axis=0)

def group_layer(tokens, lengths, qkv_matrix, out_matrix, up_matrix, down_matrix, vector_table, bias_table):
    highest = lax.Precision.HIGHEST
    scale = DH ** (-0.5)
    shift = jnp.concatenate([vector_table[:, 0], jnp.zeros((D,), jnp.float32), vector_table[:, 1]])
    qkv = low(low_back(product(tokens, qkv_matrix)) + shift)
    queries = qkv[:, :D].reshape(2 * PROMPT, H, DH)
    keys = qkv[:, D:2 * D].reshape(2 * PROMPT, H, DH)
    values = qkv[:, 2 * D:].reshape(2 * PROMPT, H, DH)
    prompt_queries = queries[:PROMPT]
    prompt_keys = keys[:PROMPT]
    prompt_values = values[:PROMPT]
    reply_queries = queries[PROMPT:].reshape(CONTS, CLEN, H, DH)
    reply_keys = keys[PROMPT:].reshape(CONTS, CLEN, H, DH)
    reply_values = values[PROMPT:].reshape(CONTS, CLEN, H, DH)
    prompt_scores = low_back(jnp.einsum('qhd,khd->hqk', prompt_queries, prompt_keys, precision=highest) * scale)
    prompt_probs = low(jax.nn.softmax(prompt_scores, axis=-1))
    prompt_out = jnp.einsum('hqk,khd->qhd', prompt_probs, prompt_values, precision=highest)
    wide = jnp.einsum('cqhd,khd->chqk', reply_queries, prompt_keys, precision=highest)
    narrow = jnp.einsum('cqhd,ckhd->chqk', reply_queries, reply_keys, precision=highest)
    reply_scores = low_back(jnp.concatenate([wide, narrow], axis=-1) * scale)
    place = jnp.arange(CLEN, dtype=jnp.int32)
    causal = place[None, :] <= place[:, None]
    inside = place[None, :] < lengths[:, None]
    allowed_near = jnp.logical_and(causal[None, None, :, :], inside[:, None, None, :])
    allowed = jnp.concatenate([jnp.ones((CONTS, 1, CLEN, PROMPT), dtype=jnp.bool_), allowed_near], axis=-1)
    masked = jnp.where(allowed, reply_scores, -jnp.inf)
    reply_probs = low(jax.nn.softmax(masked, axis=-1))
    reply_out = jnp.einsum('chqk,khd->cqhd', reply_probs[..., :PROMPT], prompt_values, precision=highest)
    reply_out = reply_out + jnp.einsum('chqk,ckhd->cqhd', reply_probs[..., PROMPT:], reply_values, precision=highest)
    joined = jnp.concatenate([prompt_out.reshape(PROMPT, D), reply_out.reshape(CONTS * CLEN, D)], axis=0)
    attended = low(low_back(joined))
    branch = low_back(product(attended, out_matrix)) + vector_table[:, 2]
    hidden = layer_norm(tokens + branch, vector_table[:, 3], vector_table[:, 4])
    pre_act = low_back(product(low(hidden), up_matrix)) + bias_table
    act_low = low(jax.nn.gelu(pre_act, approximate=False))
    second = hidden + low_back(product(act_low, down_matrix)) + vector_table[:, 5]
    return layer_norm(second, vector_table[:, 6], vector_table[:, 7])

def reference(inputs, qkv_weight, out_weight, up_weight, down_weight, vectors, up_bias, cont_lengths, out_cotangent):
    params = (qkv_weight.astype(jnp.float32), out_weight.astype(jnp.float32), up_weight.astype(jnp.float32), down_weight.astype(jnp.float32), vectors, up_bias)
    total_groups = MICRO * GROUPS
    token_groups = inputs.reshape(total_groups, 2 * PROMPT, D)
    grad_groups = out_cotangent.reshape(total_groups, 2 * PROMPT, D)
    length_groups = cont_lengths.reshape(total_groups, CONTS)

    def one_group(totals, items):
        tokens, cotangent, lengths = items

        def forward(token_values, qkv_matrix, out_matrix, up_matrix, down_matrix, vector_table, bias_table):
            return group_layer(token_values, lengths, qkv_matrix, out_matrix, up_matrix, down_matrix, vector_table, bias_table)
        ordered = regroup(tokens.astype(jnp.float32))
        result, pullback = jax.vjp(forward, ordered, params[0], params[1], params[2], params[3], params[4], params[5])
        grads = pullback(regroup(cotangent.astype(jnp.float32)))
        totals = tuple((total + grad for total, grad in zip(totals, grads[1:])))
        return (totals, (regroup(result).astype(jnp.bfloat16), regroup(grads[0]).astype(jnp.bfloat16)))
    start = tuple((jnp.zeros(param.shape, jnp.float32) for param in params))
    totals, (results, input_grads) = lax.scan(one_group, start, (token_groups, grad_groups, length_groups))
    return (results.reshape(MICRO, TOKENS, D), input_grads.reshape(MICRO, TOKENS, D), totals[0], totals[1], totals[2], totals[3], totals[4], totals[5])
```

```python
import functools
import math

import jax
import jax.numpy as jnp
from jax import lax
from jax.experimental import pallas as pl
from jax.experimental.pallas import tpu as pltpu
from jax.sharding import PartitionSpec as P

H = 12
CLEN = 128
LANES = 128
EPSILON = 1e-05
LOG2E = math.log2(math.e)
LOW = jnp.bfloat16
FULL = jnp.float32
cat = jnp.concatenate


def nt(left, right):
    return lax.dot_general(left, right, (((1,), (1,)), ((), ())), preferred_element_type=FULL)


def nn(left, right):
    return lax.dot_general(left, right, (((1,), (0,)), ((), ())), preferred_element_type=FULL)


def tn(left, right):
    return lax.dot_general(left, right, (((0,), (0,)), ((), ())), preferred_element_type=FULL)


def only(pick, value):
    return jnp.where(pick, value, jnp.zeros_like(value))


def attend_kernel(own_ref, other_ref, mask_ref, out_ref, lse_ref, *, head, scale):
    rows = own_ref.shape[1]
    half = rows // 2
    heads = LANES // head
    queries = own_ref[0, :, :LANES]
    own_keys = own_ref[0, :, LANES : 2 * LANES] * jnp.asarray(scale, LOW)
    own_values = own_ref[0, :, 2 * LANES :]
    keys = cat([own_keys[:half], other_ref[0, :, :LANES] * jnp.asarray(scale, LOW)], axis=0)
    near = own_keys[half:]
    values_t = cat([own_values[:half], other_ref[0, :, LANES:]], axis=0).T
    near_values_t = own_values[half:].T
    lane = lax.broadcasted_iota(jnp.int32, (1, LANES), 1) // head
    spans = [(start, start + CLEN) for start in range(0, half, CLEN)]
    picked = lax.broadcasted_iota(jnp.int32, (8, LANES), 0) == lane
    chooser = jnp.where(picked, 1.0, 0.0).astype(LOW)

    def with_ones(value):
        return cat([value, jnp.ones((16, value.shape[1]), LOW)], axis=0)

    def squares(value):
        return nt(chooser, value * value)

    def run(exact):
        flags = []
        if not exact:
            largest = jnp.maximum(
                jnp.max(squares(keys), axis=1, keepdims=True),
                jnp.max(squares(near), axis=1, keepdims=True),
            )
            bound = jnp.sqrt(squares(queries) * largest) * LOG2E
        for part in range(2):
            span = slice(part * half, (part + 1) * half)
            query = queries[span]
            outs = []
            for h in range(heads):
                pick = lane == h
                lines = slice(h * head, (h + 1) * head)
                scores = nt(only(pick, keys), query)
                if part:
                    near_keys = only(pick, near)
                    local = cat([nt(near_keys[a:b], query[a:b]) for a, b in spans], axis=1)
                    local = local + mask_ref[0]
                if exact:
                    top = jnp.max(scores, axis=0, keepdims=True)
                    if part:
                        top = jnp.maximum(top, jnp.max(local, axis=0, keepdims=True))
                    top = top * LOG2E
                else:
                    top = bound[h : h + 1, span]
                weights = jnp.exp2(scores * LOG2E - top).astype(LOW)
                mixed = nn(with_ones(values_t[lines]), weights)
                if part:
                    weights = jnp.exp2(local * LOG2E - top).astype(LOW)
                    value = with_ones(near_values_t[lines])
                    mixed = mixed + cat(
                        [nn(value[:, a:b], weights[:, a:b]) for a, b in spans], axis=1
                    )
                total = mixed[head : head + 1]
                fine = jnp.logical_and(total > 1e-25, total < 1e30)
                flags.append(jnp.where(fine, 0.0, 1.0))
                outs.append(mixed[:head] / total)
                lse_ref[0, 0, h : h + 1, span] = top + jnp.log2(total)
            out_ref[0, span] = cat(outs, axis=0).T.astype(LOW)
        return jnp.max(sum(flags[1:], flags[0]))

    bad = run(False)

    @pl.when(bad > 0.5)
    def _():
        run(True)


def attend(own, other, mask, head):
    batch, rows, columns = own.shape
    steps = columns // (3 * LANES)
    heads = LANES // head
    work = batch * rows * (rows + CLEN) * steps * LANES

    def spec(count, width):
        return pl.BlockSpec((1, count, width), lambda m, p: (m, 0, p))

    return pl.pallas_call(
        functools.partial(attend_kernel, head=head, scale=head**-0.5),
        grid=(batch, steps),
        in_specs=[
            spec(rows, 3 * LANES),
            spec(rows // 2, 2 * LANES),
            pl.BlockSpec((1,) + mask.shape[1:], lambda m, p: (m, 0, 0)),
        ],
        out_specs=[
            spec(rows, LANES),
            pl.BlockSpec((1, 1, heads, rows), lambda m, p: (m, p, 0, 0)),
        ],
        out_shape=[
            jax.ShapeDtypeStruct((batch, rows, steps * LANES), LOW),
            jax.ShapeDtypeStruct((batch, steps, heads, rows), FULL),
        ],
        cost_estimate=pl.CostEstimate(
            flops=16 * work, bytes_accessed=own.size * 4, transcendentals=work // head
        ),
        name="attend",
    )(own, other, mask)


def attend_back_kernel(
    own_ref, other_ref, mask_ref, out_ref, grad_ref, lse_ref, own_grad_ref, other_grad_ref,
    *, head, scale,
):
    rows = own_ref.shape[1]
    half = rows // 2
    heads = LANES // head
    own_keys = own_ref[0, :, LANES : 2 * LANES] * jnp.asarray(scale, LOW)
    own_values = own_ref[0, :, 2 * LANES :]
    keys = cat([own_keys[:half], other_ref[0, :, :LANES] * jnp.asarray(scale, LOW)], axis=0)
    near = own_keys[half:]
    values = cat([own_values[:half], other_ref[0, :, LANES:]], axis=0)
    near_values = own_values[half:]
    keys_t = keys.T
    near_t = near.T
    lane = lax.broadcasted_iota(jnp.int32, (1, LANES), 1) // head
    spans = [(start, start + CLEN) for start in range(0, half, CLEN)]
    totals = [None, None, None, None]

    def add(place, value):
        totals[place] = value if totals[place] is None else totals[place] + value

    for part in range(2):
        span = slice(part * half, (part + 1) * half)
        query = own_ref[0, span, :LANES]
        grad = grad_ref[0, span]
        dots = (grad.astype(FULL) * out_ref[0, span].astype(FULL)).T
        query_grads = []
        for h in range(heads):
            pick = lane == h
            lines = slice(h * head, (h + 1) * head)
            lse = lse_ref[0, 0, h : h + 1, span]
            delta = jnp.sum(dots[lines], axis=0, keepdims=True)
            query_h = only(pick, query)
            grad_h = only(pick, grad)
            probs = jnp.exp2(nt(only(pick, keys), query) * LOG2E - lse)
            slopes = (probs * (nt(only(pick, values), grad) - delta)).astype(LOW)
            probs = probs.astype(LOW)
            query_grad = nn(keys_t[lines], slopes)
            add(0, nn(slopes, query_h))
            add(1, nn(probs, grad_h))
            if part:
                near_h = only(pick, near)
                near_values_h = only(pick, near_values)
                local = cat([nt(near_h[a:b], query[a:b]) for a, b in spans], axis=1)
                dlocal = cat([nt(near_values_h[a:b], grad[a:b]) for a, b in spans], axis=1)
                probs = jnp.exp2((local + mask_ref[0]) * LOG2E - lse)
                slopes = (probs * (dlocal - delta)).astype(LOW)
                probs = probs.astype(LOW)
                query_grad = query_grad + cat(
                    [nn(near_t[lines, a:b], slopes[:, a:b]) for a, b in spans], axis=1
                )
                add(2, cat([nn(slopes[:, a:b], query_h[a:b]) for a, b in spans], axis=0))
                add(3, cat([nn(probs[:, a:b], grad_h[a:b]) for a, b in spans], axis=0))
            query_grads.append(query_grad)
        own_grad_ref[0, span, :LANES] = cat(query_grads, axis=0).T.astype(LOW)
    key_grad = (totals[0] * scale).astype(LOW)
    value_grad = totals[1].astype(LOW)
    own_grad_ref[0, :half, LANES : 2 * LANES] = key_grad[:half]
    own_grad_ref[0, :half, 2 * LANES :] = value_grad[:half]
    other_grad_ref[0, :, :LANES] = key_grad[half:]
    other_grad_ref[0, :, LANES:] = value_grad[half:]
    own_grad_ref[0, half:, LANES : 2 * LANES] = (totals[2] * scale).astype(LOW)
    own_grad_ref[0, half:, 2 * LANES :] = totals[3].astype(LOW)


def attend_back(own, other, mask, out, grad, lse, head):
    batch, rows, columns = own.shape
    steps = columns // (3 * LANES)
    work = batch * rows * (rows + CLEN) * steps * LANES

    def spec(count, width):
        return pl.BlockSpec((1, count, width), lambda m, p: (m, 0, p))

    return pl.pallas_call(
        functools.partial(attend_back_kernel, head=head, scale=head**-0.5),
        grid=(batch, steps),
        in_specs=[
            spec(rows, 3 * LANES),
            spec(rows // 2, 2 * LANES),
            pl.BlockSpec((1,) + mask.shape[1:], lambda m, p: (m, 0, 0)),
            spec(rows, LANES),
            spec(rows, LANES),
            pl.BlockSpec((1, 1) + lse.shape[2:], lambda m, p: (m, p, 0, 0)),
        ],
        out_specs=[spec(rows, 3 * LANES), spec(rows // 2, 2 * LANES)],
        out_shape=[
            jax.ShapeDtypeStruct(own.shape, LOW),
            jax.ShapeDtypeStruct(other.shape, LOW),
        ],
        cost_estimate=pl.CostEstimate(
            flops=40 * work, bytes_accessed=own.size * 10, transcendentals=work // head
        ),
        name="attend_back",
    )(own, other, mask, out, grad, lse)


def swapped(value, axis, mask):
    pairs = [(source, source ^ mask) for source in range(lax.axis_size(axis))]
    return lax.ppermute(value, axis, pairs)


def masks_of(axis):
    return [1 << bit for bit in range(lax.axis_size(axis).bit_length() - 1)]


def bit_of(axis, mask):
    return jnp.where(lax.axis_index(axis) & mask == 0, 0, 1)


def joined(value, axis, mask, dim):
    other = swapped(value, axis, mask)
    first = bit_of(axis, mask) == 0
    return jnp.stack([jnp.where(first, value, other), jnp.where(first, other, value)], axis=dim)


def gathered(block):
    for mask in masks_of("col"):
        block = joined(block, "col", mask, 1).reshape(block.shape[0], -1)
    depth, columns = block.shape
    value = block[None]
    for mask in masks_of("row")[::-1]:
        value = joined(value, "row", mask, 1).reshape(-1, depth, columns)
    return value.reshape(-1, columns)


def parted(value, axis, mask, dim):
    bit = bit_of(axis, mask)
    keep = lax.dynamic_index_in_dim(value, bit, dim, keepdims=False)
    send = lax.dynamic_index_in_dim(value, 1 - bit, dim, keepdims=False)
    return keep + swapped(send.astype(LOW), axis, mask).astype(FULL)


def scattered(total, shape):
    value = total.reshape(-1, shape[0], total.shape[1])
    for mask in masks_of("row"):
        value = parted(value.reshape(-1, 2, *value.shape[1:]), "row", mask, 1)
    value = value.reshape(shape[0], -1)
    for mask in masks_of("col")[::-1]:
        value = parted(value.reshape(shape[0], 2, -1), "col", mask, 1)
    return over_dp(value)


def over_dp(value):
    for mask in masks_of("dp"):
        low = value.astype(LOW)
        value = low.astype(FULL) + swapped(low, "dp", 2 * mask - 1).astype(FULL)
    return value


def normalize(value):
    average = jnp.mean(value, axis=-1, keepdims=True)
    centred = value - average
    spread = jnp.mean(centred * centred, axis=-1, keepdims=True)
    inverse = lax.rsqrt(spread + EPSILON)
    return (centred * inverse, inverse)


def normalize_back(grad_normed, normed, inverse):
    first = jnp.mean(grad_normed, axis=-1, keepdims=True)
    second = jnp.mean(grad_normed * normed, axis=-1, keepdims=True)
    return inverse * (grad_normed - first - normed * second)


def near_mask(lengths, half):
    place = jnp.arange(CLEN, dtype=jnp.int32)[:, None]
    query = jnp.arange(half, dtype=jnp.int32)[None, :]
    limit = jnp.repeat(lengths, CLEN, axis=1)[:, None, :]
    seen = jnp.logical_and((place <= query % CLEN)[None], place[None] < limit)
    return jnp.where(seen, 0.0, -jnp.inf).astype(FULL)


def local(
    inputs,
    qkv_weight,
    out_weight,
    up_weight,
    down_weight,
    vectors,
    up_bias,
    cont_lengths,
    out_cotangent,
):
    grid_rows = lax.axis_size("row")
    grid_cols = lax.axis_size("col")
    place = lax.axis_index("col")
    side = place % 2
    batch, rows, width = inputs.shape
    half = rows // 2
    head = width // H
    steps = width // LANES
    half_conts = cont_lengths.shape[2] // 2
    group_lengths = lax.dynamic_index_in_dim(cont_lengths, place // 2, 1, keepdims=False)
    lengths = lax.dynamic_slice_in_dim(group_lengths, side * half_conts, half_conts, 1)
    mask = near_mask(lengths, half)

    other_tokens = swapped(inputs[:, :half], "col", 1).reshape(batch * half, width)
    tokens = inputs.reshape(batch * rows, width)

    def by_step(matrix):
        lead = matrix.shape[0]
        shaped = matrix.reshape(lead, 3, steps, LANES)
        return shaped.transpose(0, 2, 1, 3)

    qkv_matrix = by_step(gathered(qkv_weight))
    pair_matrix = qkv_matrix[:, :, 1:].reshape(width, 2 * width)
    qkv_matrix = qkv_matrix.reshape(width, 3 * width)
    shift = by_step(
        cat([vectors[:, 0], jnp.zeros((width,), FULL), vectors[:, 1]])[None]
    )
    pair_shift = shift[:, :, 1:].reshape(1, 2 * width)
    shift = shift.reshape(1, 3 * width)
    own = (nn(tokens, qkv_matrix) + shift).astype(LOW).reshape(batch, rows, 3 * width)
    other = (nn(other_tokens, pair_matrix) + pair_shift).astype(LOW)
    other = other.reshape(batch, half, 2 * width)
    attended, lse = attend(own, other, mask, head)

    out_matrix = gathered(out_weight)
    up_matrix = gathered(up_weight)
    down_matrix = gathered(down_weight)
    attended = attended.reshape(batch * rows, width)
    first_sum = tokens.astype(FULL) + nn(attended, out_matrix) + vectors[:, 2]
    first_normed, first_inverse = normalize(first_sum)
    hidden = first_normed * vectors[:, 3] + vectors[:, 4]
    hidden_low = hidden.astype(LOW)
    pre_act = nn(hidden_low, up_matrix) + up_bias
    phi = 0.5 * lax.erfc(pre_act * (-(0.5**0.5)))
    slope = phi + pre_act * (jnp.exp(-0.5 * pre_act * pre_act) * ((2 * math.pi) ** -0.5))
    act_low = (pre_act * phi).astype(LOW)
    slope_low = slope.astype(LOW)
    second_sum = hidden + nn(act_low, down_matrix) + vectors[:, 5]
    second_normed, second_inverse = normalize(second_sum)
    result = (second_normed * vectors[:, 6] + vectors[:, 7]).astype(LOW)

    grad_out = out_cotangent.reshape(batch * rows, width).astype(FULL)
    grad_second = normalize_back(grad_out * vectors[:, 6], second_normed, second_inverse)
    grad_second_low = grad_second.astype(LOW)
    grad_pre = nt(grad_second_low, down_matrix) * slope_low.astype(FULL)
    grad_pre_low = grad_pre.astype(LOW)
    grad_hidden = grad_second + nt(grad_pre_low, up_matrix)
    grad_first = normalize_back(grad_hidden * vectors[:, 3], first_normed, first_inverse)
    grad_first_low = grad_first.astype(LOW)
    grad_attended = nt(grad_first_low, out_matrix).astype(LOW)
    down_grad = scattered(tn(act_low, grad_second_low), down_weight.shape)
    up_grad = scattered(tn(hidden_low, grad_pre_low), up_weight.shape)
    out_grad = scattered(tn(attended, grad_first_low), out_weight.shape)

    own_grad, other_grad = attend_back(
        own,
        other,
        mask,
        attended.reshape(batch, rows, width),
        grad_attended.reshape(batch, rows, width),
        lse,
        head,
    )
    own_grad = own_grad.reshape(batch * rows, 3 * width)
    other_grad = other_grad.reshape(batch * half, 2 * width)
    sent = nt(other_grad, pair_matrix).astype(LOW).reshape(batch, half, width)
    received = swapped(sent, "col", 1).astype(FULL)
    grad_tokens = (grad_first + nt(own_grad, qkv_matrix)).reshape(batch, rows, width)
    grad_tokens = cat([grad_tokens[:, :half] + received, grad_tokens[:, half:]], axis=1)
    grad_tokens = grad_tokens.astype(LOW)
    qkv_total = tn(tokens, own_grad).reshape(width, steps, 3, LANES)
    pair_total = tn(other_tokens, other_grad).reshape(width, steps, 2, LANES)
    qkv_total = cat([qkv_total[:, :, :1], qkv_total[:, :, 1:] + pair_total], axis=2)
    qkv_total = qkv_total.transpose(0, 2, 1, 3).reshape(width, 3 * width)
    qkv_grad = scattered(qkv_total, qkv_weight.shape)

    own_sum = jnp.sum(own_grad.astype(FULL), axis=0).reshape(steps, 3, LANES)
    other_sum = jnp.sum(other_grad.astype(FULL), axis=0).reshape(steps, 2, LANES)
    sums = [
        own_sum[:, 0].reshape(width),
        (own_sum[:, 2] + other_sum[:, 1]).reshape(width),
        jnp.sum(grad_first, axis=0),
        jnp.sum(grad_hidden * first_normed, axis=0),
        jnp.sum(grad_hidden, axis=0),
        jnp.sum(grad_second, axis=0),
        jnp.sum(grad_out * second_normed, axis=0),
        jnp.sum(grad_out, axis=0),
        jnp.sum(grad_pre, axis=0),
    ]
    sums = lax.psum(cat(sums), ("dp", "row", "col"))
    index = lax.axis_index("row") * grid_cols + place
    devices = grid_rows * grid_cols
    split = sums[: 8 * width].reshape(8, width)
    vector_grad = lax.dynamic_slice_in_dim(split, index * (width // devices), width // devices, 1).T
    bias = sums[8 * width :]
    count = bias.shape[0] // devices
    bias_grad = lax.dynamic_slice_in_dim(bias, index * count, count, 0)
    return (
        result.reshape(batch, rows, width),
        grad_tokens,
        qkv_grad,
        out_grad,
        up_grad,
        down_grad,
        vector_grad,
        bias_grad,
    )


def solution(mesh):
    everywhere = ("dp", "row", "col")
    tokens = P(None, everywhere, None)
    matrix = P("row", "col")
    return jax.shard_map(
        local,
        mesh=mesh,
        in_specs=(
            tokens, matrix, matrix, matrix, matrix, P(), P(), P(None, ("dp", "row"), None), tokens,
        ),
        out_specs=(
            tokens, tokens, matrix, matrix, matrix, matrix, P(("row", "col"), None), P(("row", "col")),
        ),
        check_vma=False,
    )
```

```python
import functools
import math

import jax
import jax.numpy as jnp
from jax import lax
from jax.experimental import pallas as pl
from jax.experimental.pallas import tpu as pltpu
from jax.sharding import PartitionSpec as P

H = 12
CLEN = 128
LANES = 128
EPSILON = 1e-05
LOG2E = math.log2(math.e)
LOW = jnp.bfloat16
FULL = jnp.float32
cat = jnp.concatenate


def nt(left, right):
    return lax.dot_general(left, right, (((1,), (1,)), ((), ())), preferred_element_type=FULL)


def nn(left, right):
    return lax.dot_general(left, right, (((1,), (0,)), ((), ())), preferred_element_type=FULL)


def tn(left, right):
    return lax.dot_general(left, right, (((0,), (0,)), ((), ())), preferred_element_type=FULL)


def only(pick, value):
    return jnp.where(pick, value, jnp.zeros_like(value))


def spread(order):
    listed = []
    for stage in range(len(order)):
        for code in range(1 << stage):
            listed.append((stage, tuple(order[i] for i in range(stage) if code >> i & 1)))
    return listed


def flipped(position, axis, mask):
    bit = position[axis] // mask % 2
    return {**position, axis: position[axis] + mask * (1 - 2 * bit)}


def place_of(position, crossed):
    for axis, mask in crossed:
        position = flipped(position, axis, mask)
    return position


def here(axes):
    return {axis: lax.axis_index(axis) for axis in axes}


def bits_of(axis, size):
    return [(axis, 1 << bit) for bit in range(size.bit_length() - 1)]


def greet(partners):
    barrier = pltpu.get_barrier_semaphore()
    for axis, mask in partners:
        target = flipped(here((axis,)), axis, mask)
        pl.semaphore_signal(barrier, inc=1, device_id=target, device_id_type=pl.DeviceIdType.MESH)
    pl.semaphore_wait(barrier, len(partners))


class Gather:
    def __init__(self, own, whole, order, sends, arrivals, base):
        self.own, self.whole, self.order = own, whole, order
        self.sends, self.arrivals, self.base = sends, arrivals, base
        self.copies = spread(order)
        self.position = here(("row", "col"))

    def slot(self, position):
        depth, columns = self.own.shape
        first = pl.multiple_of(position["row"] * depth, 16)
        start = pl.multiple_of(position["col"] * columns, LANES)
        return self.whole.at[pl.ds(first, depth), pl.ds(start, columns)]

    def copy(self, index):
        stage, crossed = self.copies[index]
        axis, mask = self.order[stage]
        slot = self.slot(place_of(self.position, crossed))
        return pltpu.make_async_remote_copy(
            src_ref=slot if crossed else self.own,
            dst_ref=slot,
            send_sem=self.sends.at[self.base + index],
            recv_sem=self.arrivals.at[self.base + index],
            device_id=flipped(here((axis,)), axis, mask),
            device_id_type=pl.DeviceIdType.MESH,
        )

    def arrival(self, index):
        stage, crossed = self.copies[index]
        axis, mask = self.order[stage]
        slot = self.slot(place_of(self.position, crossed + (self.order[stage],)))
        return pltpu.make_async_remote_copy(
            src_ref=slot,
            dst_ref=slot,
            send_sem=self.sends.at[self.base + index],
            recv_sem=self.arrivals.at[self.base + index],
            device_id=flipped(here((axis,)), axis, mask),
            device_id_type=pl.DeviceIdType.MESH,
        )

    def placing(self, semaphore):
        return pltpu.make_async_copy(self.own, self.slot(self.position), semaphore)

    def source(self, index):
        crossed = self.copies[index][1]
        last = self.order.index(crossed[-1])
        return self.copies.index((last, crossed[:-1]))

    def first(self):
        return [i for i, (stage, crossed) in enumerate(self.copies) if not crossed]

    def later(self):
        return [i for i, (stage, crossed) in enumerate(self.copies) if crossed]


def attend_step(q_ref, k_ref, v_ref, ok_ref, ov_ref, mask_ref, out_ref, lse_ref, *, head, exact):
    rows = q_ref.shape[1]
    half = rows // 2
    heads = LANES // head
    scale = jnp.asarray(head**-0.5, LOW)
    queries = q_ref[0]
    own_keys = k_ref[0] * scale
    own_values = v_ref[0]
    keys = cat([own_keys[:half], ok_ref[0] * scale], axis=0)
    near = own_keys[half:]
    values_t = cat([own_values[:half], ov_ref[0]], axis=0).T
    near_values_t = own_values[half:].T
    lane = lax.broadcasted_iota(jnp.int32, (1, LANES), 1) // head
    spans = [(start, start + CLEN) for start in range(0, half, CLEN)]
    picked = lax.broadcasted_iota(jnp.int32, (8, LANES), 0) == lane
    chooser = jnp.where(picked, 1.0, 0.0).astype(LOW)

    def with_ones(value):
        return cat([value, jnp.ones((16, value.shape[1]), LOW)], axis=0)

    def squares(value):
        return nt(chooser, value * value)

    flags = []
    if not exact:
        largest = jnp.maximum(
            jnp.max(squares(keys), axis=1, keepdims=True),
            jnp.max(squares(near), axis=1, keepdims=True),
        )
        bound = jnp.sqrt(squares(queries) * largest) * LOG2E
    for part in range(2):
        span = slice(part * half, (part + 1) * half)
        query = queries[span]
        outs = []
        for h in range(heads):
            pick = lane == h
            lines = slice(h * head, (h + 1) * head)
            scores = nt(only(pick, keys), query)
            if part:
                near_keys = only(pick, near)
                local = cat([nt(near_keys[a:b], query[a:b]) for a, b in spans], axis=1)
                local = local + mask_ref[0]
            if exact:
                top = jnp.max(scores, axis=0, keepdims=True)
                if part:
                    top = jnp.maximum(top, jnp.max(local, axis=0, keepdims=True))
                top = top * LOG2E
            else:
                top = bound[h : h + 1, span]
            weights = jnp.exp2(scores * LOG2E - top).astype(LOW)
            mixed = nn(with_ones(values_t[lines]), weights)
            if part:
                weights = jnp.exp2(local * LOG2E - top).astype(LOW)
                value = with_ones(near_values_t[lines])
                mixed = mixed + cat([nn(value[:, a:b], weights[:, a:b]) for a, b in spans], axis=1)
            total = mixed[head : head + 1]
            fine = jnp.logical_and(total > 1e-25, total < 1e30)
            flags.append(jnp.where(fine, 0.0, 1.0))
            outs.append(mixed[:head] / total)
            lse_ref[0, 0, h : h + 1, span] = top + jnp.log2(total)
        out_ref[0, span] = cat(outs, axis=0).T.astype(LOW)
    return sum(flags[1:], flags[0])


def attend_again_kernel(*refs, head):
    attend_step(*refs, head=head, exact=True)


def attend_kernel(
    q_ref, k_ref, v_ref, ok_ref, ov_ref, mask_ref, out_block, up_block, down_block,
    out_ref, lse_ref, flag_ref, out_whole, up_whole, down_whole,
    sends, arrivals, placed, *, head, grid,
):
    rows, columns = grid
    steps = pl.num_programs(1)
    step = pl.program_id(0) * steps + pl.program_id(1)
    final = 2 * steps - 1
    row_bits, col_bits = bits_of("row", rows), bits_of("col", columns)
    first_order = tuple(col_bits + row_bits[::-1])
    second_order = tuple(row_bits[:0:-1] + col_bits + row_bits[:1])
    per = len(spread(first_order))
    parts = [
        Gather(out_block, out_whole, first_order, sends, arrivals, 0),
        Gather(down_block, down_whole, first_order, sends, arrivals, per),
        Gather(up_block, up_whole, second_order, sends, arrivals, 2 * per),
    ]

    @pl.when(step == 0)
    def _():
        greet(row_bits + col_bits)
        for index in parts[0].first():
            for part in parts:
                part.copy(index).start()
        for number, part in enumerate(parts):
            part.placing(placed.at[number]).start()

    last = len(first_order) - 1
    events = {}
    for number, part in enumerate(parts):
        for index in part.later():
            stage, crossed = part.copies[index]
            if len(crossed) > 1 and number:
                when = final
            elif stage == last:
                when = (5, 8, 9)[number] + 2 * (len(crossed) > 1)
            else:
                when = (2, 6, 7)[number]
            events.setdefault(min(when, final), []).append((part, index))
    waited = set()
    for when in sorted(events):
        if when == final:
            continue

        @pl.when(step == when)
        def _(batch=events[when]):
            for part, index in batch:
                origin = part.source(index)
                if (part.base, origin) not in waited:
                    waited.add((part.base, origin))
                    part.arrival(origin).wait_recv()
                part.copy(index).start()

    flags = attend_step(
        q_ref, k_ref, v_ref, ok_ref, ov_ref, mask_ref, out_ref, lse_ref, head=head, exact=False
    )
    flag_ref[0, 0] = jnp.broadcast_to(flags, flag_ref.shape[2:])

    @pl.when(step == final)
    def _():
        for part, index in events.get(final, []):
            origin = part.source(index)
            if (part.base, origin) not in waited:
                waited.add((part.base, origin))
                part.arrival(origin).wait_recv()
            part.copy(index).start()
        for number, part in enumerate(parts):
            part.placing(placed.at[number]).wait()
            for index in range(per):
                if (part.base, index) not in waited:
                    part.arrival(index).wait_recv()
                part.copy(index).wait_send()


def attend_specs(own, other, mask):
    batch, rows, columns = own.shape
    steps = columns // (3 * LANES)

    def spec(count, offset):
        return pl.BlockSpec((1, count, LANES), lambda m, p: (m, 0, offset * steps + p))

    ins = [
        spec(rows, 0),
        spec(rows, 1),
        spec(rows, 2),
        spec(rows // 2, 0),
        spec(rows // 2, 1),
        pl.BlockSpec((1,) + mask.shape[1:], lambda m, p: (m, 0, 0)),
    ]
    return batch, rows, steps, spec, ins


def attend_again(own, other, mask, head):
    batch, rows, steps, spec, ins = attend_specs(own, other, mask)
    heads = LANES // head
    return pl.pallas_call(
        functools.partial(attend_again_kernel, head=head),
        grid=(batch, steps),
        in_specs=ins,
        out_specs=[spec(rows, 0), pl.BlockSpec((1, 1, heads, rows), lambda m, p: (m, p, 0, 0))],
        out_shape=[
            jax.ShapeDtypeStruct((batch, rows, steps * LANES), LOW),
            jax.ShapeDtypeStruct((batch, steps, heads, rows), FULL),
        ],
        name="attend_again",
    )(own, own, own, other, other, mask)


def attend(own, other, mask, blocks, grid, head):
    batch, rows, steps, spec, ins = attend_specs(own, other, mask)
    heads = LANES // head
    half = rows // 2
    anywhere = pl.BlockSpec(memory_space=pl.ANY)
    copies = 3 * (grid[0] * grid[1] - 1)
    work = batch * rows * (rows + CLEN) * steps * LANES
    wholes = [
        jax.ShapeDtypeStruct((block.shape[0] * grid[0], block.shape[1] * grid[1]), LOW)
        for block in blocks
    ]
    out, lse, flags, *wholes = pl.pallas_call(
        functools.partial(attend_kernel, head=head, grid=grid),
        grid=(batch, steps),
        in_specs=ins + [anywhere] * 3,
        out_specs=[
            spec(rows, 0),
            pl.BlockSpec((1, 1, heads, rows), lambda m, p: (m, p, 0, 0)),
            pl.BlockSpec((1, 1, 8, half), lambda m, p: (m, p, 0, 0)),
        ]
        + [anywhere] * 3,
        out_shape=[
            jax.ShapeDtypeStruct((batch, rows, steps * LANES), LOW),
            jax.ShapeDtypeStruct((batch, steps, heads, rows), FULL),
            jax.ShapeDtypeStruct((batch, steps, 8, half), FULL),
        ]
        + wholes,
        scratch_shapes=[
            pltpu.SemaphoreType.DMA((copies,)),
            pltpu.SemaphoreType.DMA((copies,)),
            pltpu.SemaphoreType.DMA((3,)),
        ],
        compiler_params=pltpu.CompilerParams(collective_id=1, has_side_effects=True),
        cost_estimate=pl.CostEstimate(
            flops=16 * work, bytes_accessed=own.size * 4, transcendentals=work // head
        ),
        name="attend",
    )(own, own, own, other, other, mask, *blocks)
    out, lse = lax.cond(
        jnp.max(flags) > 0.5,
        lambda: tuple(attend_again(own, other, mask, head)),
        lambda: (out, lse),
    )
    return out, lse, wholes


def begin_kernel(tokens_ref, block_ref, other_ref, whole_ref, sends, arrivals, placed, *, grid):
    rows, columns = grid
    row_bits, col_bits = bits_of("row", rows), bits_of("col", columns)
    order = tuple(col_bits + row_bits[::-1])
    part = Gather(block_ref, whole_ref, order, sends, arrivals, 0)
    per = len(part.copies)
    half = other_ref.shape[1]
    partner = flipped(here(("col",)), "col", 1)
    exchanges = [
        pltpu.make_async_remote_copy(
            src_ref=tokens_ref.at[m, pl.ds(0, half)],
            dst_ref=other_ref.at[m],
            send_sem=sends.at[per + m],
            recv_sem=arrivals.at[per + m],
            device_id=partner,
            device_id_type=pl.DeviceIdType.MESH,
        )
        for m in range(other_ref.shape[0])
    ]
    greet(row_bits + col_bits)
    for index in part.first():
        part.copy(index).start()
    for exchange in exchanges:
        exchange.start()
    part.placing(placed.at[0]).start()
    waited = set()
    for index in part.later():
        origin = part.source(index)
        if origin not in waited:
            waited.add(origin)
            part.arrival(origin).wait_recv()
        part.copy(index).start()
    for index in range(per):
        if index not in waited:
            part.arrival(index).wait_recv()
        part.copy(index).wait_send()
    part.placing(placed.at[0]).wait()
    for exchange in exchanges:
        exchange.wait()


def begin(tokens, block, grid):
    batch, rows, width = tokens.shape
    copies = grid[0] * grid[1] - 1 + batch
    anywhere = pl.BlockSpec(memory_space=pl.ANY)
    return pl.pallas_call(
        functools.partial(begin_kernel, grid=grid),
        in_specs=[anywhere] * 2,
        out_specs=[anywhere] * 2,
        out_shape=[
            jax.ShapeDtypeStruct((batch, rows // 2, width), LOW),
            jax.ShapeDtypeStruct((block.shape[0] * grid[0], block.shape[1] * grid[1]), LOW),
        ],
        scratch_shapes=[
            pltpu.SemaphoreType.DMA((copies,)),
            pltpu.SemaphoreType.DMA((copies,)),
            pltpu.SemaphoreType.DMA((1,)),
        ],
        compiler_params=pltpu.CompilerParams(collective_id=0, has_side_effects=True),
        name="begin",
    )(tokens, block)


def attend_back_kernel(
    q_ref, k_ref, v_ref, ok_ref, ov_ref, mask_ref, out_ref, grad_ref, lse_ref,
    own_grad_ref, other_grad_ref, own_scratch, other_scratch, stored, *, head, scale,
):
    rows = q_ref.shape[1]
    half = rows // 2
    heads = LANES // head
    steps = pl.num_programs(1)
    group, tile = pl.program_id(0), pl.program_id(1)
    step = group * steps + tile
    slot = step % 2

    def stores(group, tile, slot):
        copies = []
        for part in range(3):
            lanes = pl.ds(pl.multiple_of((part * steps + tile) * LANES, LANES), LANES)
            copies.append(
                pltpu.make_async_copy(
                    own_scratch.at[slot, part], own_grad_ref.at[group, :, lanes], stored.at[slot, part]
                )
            )
        for part in range(2):
            lanes = pl.ds(pl.multiple_of((part * steps + tile) * LANES, LANES), LANES)
            copies.append(
                pltpu.make_async_copy(
                    other_scratch.at[slot, part],
                    other_grad_ref.at[group, :, lanes],
                    stored.at[slot, 3 + part],
                )
            )
        return copies

    @pl.when(step >= 2)
    def _():
        for copy in stores((step - 2) // steps, (step - 2) % steps, slot):
            copy.wait()

    own_keys = k_ref[0] * jnp.asarray(scale, LOW)
    own_values = v_ref[0]
    keys = cat([own_keys[:half], ok_ref[0] * jnp.asarray(scale, LOW)], axis=0)
    near = own_keys[half:]
    values = cat([own_values[:half], ov_ref[0]], axis=0)
    near_values = own_values[half:]
    keys_t = keys.T
    near_t = near.T
    lane = lax.broadcasted_iota(jnp.int32, (1, LANES), 1) // head
    spans = [(start, start + CLEN) for start in range(0, half, CLEN)]
    totals = [None, None, None, None]

    def add(place, value):
        totals[place] = value if totals[place] is None else totals[place] + value

    for part in range(2):
        span = slice(part * half, (part + 1) * half)
        query = q_ref[0, span]
        grad = grad_ref[0, span]
        dots = (grad.astype(FULL) * out_ref[0, span].astype(FULL)).T
        query_grads = []
        for h in range(heads):
            pick = lane == h
            lines = slice(h * head, (h + 1) * head)
            lse = lse_ref[0, 0, h : h + 1, span]
            delta = jnp.sum(dots[lines], axis=0, keepdims=True)
            query_h = only(pick, query)
            grad_h = only(pick, grad)
            probs = jnp.exp2(nt(only(pick, keys), query) * LOG2E - lse)
            slopes = (probs * (nt(only(pick, values), grad) - delta)).astype(LOW)
            probs = probs.astype(LOW)
            query_grad = nn(keys_t[lines], slopes)
            add(0, nn(slopes, query_h))
            add(1, nn(probs, grad_h))
            if part:
                near_h = only(pick, near)
                near_values_h = only(pick, near_values)
                local = cat([nt(near_h[a:b], query[a:b]) for a, b in spans], axis=1)
                dlocal = cat([nt(near_values_h[a:b], grad[a:b]) for a, b in spans], axis=1)
                probs = jnp.exp2((local + mask_ref[0]) * LOG2E - lse)
                slopes = (probs * (dlocal - delta)).astype(LOW)
                probs = probs.astype(LOW)
                query_grad = query_grad + cat(
                    [nn(near_t[lines, a:b], slopes[:, a:b]) for a, b in spans], axis=1
                )
                add(2, cat([nn(slopes[:, a:b], query_h[a:b]) for a, b in spans], axis=0))
                add(3, cat([nn(probs[:, a:b], grad_h[a:b]) for a, b in spans], axis=0))
            query_grads.append(query_grad)
        own_scratch[slot, 0, span] = cat(query_grads, axis=0).T.astype(LOW)
    key_grad = (totals[0] * scale).astype(LOW)
    value_grad = totals[1].astype(LOW)
    own_scratch[slot, 1, :half] = key_grad[:half]
    own_scratch[slot, 2, :half] = value_grad[:half]
    own_scratch[slot, 1, half:] = (totals[2] * scale).astype(LOW)
    own_scratch[slot, 2, half:] = totals[3].astype(LOW)
    other_scratch[slot, 0] = key_grad[half:]
    other_scratch[slot, 1] = value_grad[half:]
    for copy in stores(group, tile, slot):
        copy.start()

    @pl.when(step == pl.num_programs(0) * steps - 1)
    def _():
        for copy in stores((step - 1) // steps, (step - 1) % steps, 1 - slot):
            copy.wait()
        for copy in stores(group, tile, slot):
            copy.wait()


def attend_back(own, other, mask, out, grad, lse, head):
    batch, rows, steps, spec, ins = attend_specs(own, other, mask)
    work = batch * rows * (rows + CLEN) * steps * LANES
    anywhere = pl.BlockSpec(memory_space=pl.ANY)
    return pl.pallas_call(
        functools.partial(attend_back_kernel, head=head, scale=head**-0.5),
        grid=(batch, steps),
        in_specs=ins
        + [
            spec(rows, 0),
            spec(rows, 0),
            pl.BlockSpec((1, 1) + lse.shape[2:], lambda m, p: (m, p, 0, 0)),
        ],
        out_specs=[anywhere] * 2,
        out_shape=[
            jax.ShapeDtypeStruct(own.shape, LOW),
            jax.ShapeDtypeStruct(other.shape, LOW),
        ],
        scratch_shapes=[
            pltpu.VMEM((2, 3, rows, LANES), LOW),
            pltpu.VMEM((2, 2, rows // 2, LANES), LOW),
            pltpu.SemaphoreType.DMA((2, 5)),
        ],
        cost_estimate=pl.CostEstimate(
            flops=40 * work, bytes_accessed=own.size * 10, transcendentals=work // head
        ),
        name="attend_back",
    )(own, own, own, other, other, mask, out, grad, lse)


def swapped(value, axis, mask):
    pairs = [(source, source ^ mask) for source in range(lax.axis_size(axis))]
    return lax.ppermute(value, axis, pairs)


def masks_of(axis):
    return [1 << bit for bit in range(lax.axis_size(axis).bit_length() - 1)]


def bit_of(axis, mask):
    return jnp.where(lax.axis_index(axis) & mask == 0, 0, 1)


def joined(value, axis, mask, dim):
    other = swapped(value, axis, mask)
    first = bit_of(axis, mask) == 0
    return jnp.stack([jnp.where(first, value, other), jnp.where(first, other, value)], axis=dim)


def gathered(block):
    for mask in masks_of("col"):
        block = joined(block, "col", mask, 1).reshape(block.shape[0], -1)
    depth, columns = block.shape
    value = block[None]
    for mask in masks_of("row")[::-1]:
        value = joined(value, "row", mask, 1).reshape(-1, depth, columns)
    return value.reshape(-1, columns)


def parted(value, axis, mask, dim):
    bit = bit_of(axis, mask)
    keep = lax.dynamic_index_in_dim(value, bit, dim, keepdims=False)
    send = lax.dynamic_index_in_dim(value, 1 - bit, dim, keepdims=False)
    return keep + swapped(send.astype(LOW), axis, mask).astype(FULL)


def scattered(total, shape):
    value = total.reshape(-1, shape[0], total.shape[1])
    for mask in masks_of("row"):
        value = parted(value.reshape(-1, 2, *value.shape[1:]), "row", mask, 1)
    value = value.reshape(shape[0], -1)
    for mask in masks_of("col")[::-1]:
        value = parted(value.reshape(shape[0], 2, -1), "col", mask, 1)
    return over_dp(value)


def over_dp(value):
    for mask in masks_of("dp"):
        low = value.astype(LOW)
        value = low.astype(FULL) + swapped(low, "dp", 2 * mask - 1).astype(FULL)
    return value


def normalize(value):
    average = jnp.mean(value, axis=-1, keepdims=True)
    centred = value - average
    spread = jnp.mean(centred * centred, axis=-1, keepdims=True)
    inverse = lax.rsqrt(spread + EPSILON)
    return (centred * inverse, inverse)


def normalize_back(grad_normed, normed, inverse):
    first = jnp.mean(grad_normed, axis=-1, keepdims=True)
    second = jnp.mean(grad_normed * normed, axis=-1, keepdims=True)
    return inverse * (grad_normed - first - normed * second)


def near_mask(lengths, half):
    place = jnp.arange(CLEN, dtype=jnp.int32)[:, None]
    query = jnp.arange(half, dtype=jnp.int32)[None, :]
    limit = jnp.repeat(lengths, CLEN, axis=1)[:, None, :]
    seen = jnp.logical_and((place <= query % CLEN)[None], place[None] < limit)
    return jnp.where(seen, 0.0, -jnp.inf).astype(FULL)


def local(
    inputs,
    qkv_weight,
    out_weight,
    up_weight,
    down_weight,
    vectors,
    up_bias,
    cont_lengths,
    out_cotangent,
):
    grid_rows = lax.axis_size("row")
    grid_cols = lax.axis_size("col")
    place = lax.axis_index("col")
    side = place % 2
    batch, rows, width = inputs.shape
    half = rows // 2
    head = width // H
    half_conts = cont_lengths.shape[2] // 2
    group_lengths = lax.dynamic_index_in_dim(cont_lengths, place // 2, 1, keepdims=False)
    lengths = lax.dynamic_slice_in_dim(group_lengths, side * half_conts, half_conts, 1)
    mask = near_mask(lengths, half)

    grid = (grid_rows, grid_cols)
    direct = out_weight.shape[1] % LANES == 0 and qkv_weight.shape[1] % LANES == 0
    blocks = (out_weight, up_weight, down_weight)
    tokens = inputs.reshape(batch * rows, width)
    if direct:
        other_tokens, qkv_matrix = begin(inputs, qkv_weight, grid)
    else:
        other_tokens = swapped(inputs[:, :half], "col", 1)
        qkv_matrix = gathered(qkv_weight)
    other_tokens = other_tokens.reshape(batch * half, width)
    pair_matrix = qkv_matrix[:, width:]
    shift = cat([vectors[:, 0], jnp.zeros((width,), FULL), vectors[:, 1]])
    pair_shift = shift[width:]
    own = (nn(tokens, qkv_matrix) + shift).astype(LOW).reshape(batch, rows, 3 * width)
    other = (nn(other_tokens, pair_matrix) + pair_shift).astype(LOW)
    other = other.reshape(batch, half, 2 * width)
    if direct:
        attended, lse, (out_matrix, up_matrix, down_matrix) = attend(
            own, other, mask, blocks, grid, head
        )
    else:
        attended, lse = attend_again(own, other, mask, head)
        out_matrix, up_matrix, down_matrix = (gathered(block) for block in blocks)
    attended = attended.reshape(batch * rows, width)
    first_sum = tokens.astype(FULL) + nn(attended, out_matrix) + vectors[:, 2]
    first_normed, first_inverse = normalize(first_sum)
    hidden = first_normed * vectors[:, 3] + vectors[:, 4]
    hidden_low = hidden.astype(LOW)
    pre_act = nn(hidden_low, up_matrix) + up_bias
    phi = 0.5 + 0.5 * lax.erf(pre_act * (0.5**0.5))
    slope = phi + pre_act * (jnp.exp(-0.5 * pre_act * pre_act) * ((2 * math.pi) ** -0.5))
    act_low = (pre_act * phi).astype(LOW)
    slope_low = slope.astype(LOW)
    second_sum = hidden + nn(act_low, down_matrix) + vectors[:, 5]
    second_normed, second_inverse = normalize(second_sum)
    result = (second_normed * vectors[:, 6] + vectors[:, 7]).astype(LOW)

    grad_out = out_cotangent.reshape(batch * rows, width).astype(FULL)
    grad_second = normalize_back(grad_out * vectors[:, 6], second_normed, second_inverse)
    grad_second_low = grad_second.astype(LOW)
    grad_pre = nt(grad_second_low, down_matrix) * slope_low.astype(FULL)
    grad_pre_low = grad_pre.astype(LOW)
    grad_hidden = grad_second + nt(grad_pre_low, up_matrix)
    grad_first = normalize_back(grad_hidden * vectors[:, 3], first_normed, first_inverse)
    grad_first_low = grad_first.astype(LOW)
    grad_attended = nt(grad_first_low, out_matrix).astype(LOW)
    down_grad = scattered(tn(act_low, grad_second_low), down_weight.shape)
    up_grad = scattered(tn(hidden_low, grad_pre_low), up_weight.shape)
    out_grad = scattered(tn(attended, grad_first_low), out_weight.shape)

    own_grad, other_grad = attend_back(
        own,
        other,
        mask,
        attended.reshape(batch, rows, width),
        grad_attended.reshape(batch, rows, width),
        lse,
        head,
    )
    own_grad = own_grad.reshape(batch * rows, 3 * width)
    other_grad = other_grad.reshape(batch * half, 2 * width)
    sent = nt(other_grad, pair_matrix).astype(LOW).reshape(batch, half, width)
    received = swapped(sent, "col", 1).astype(FULL)
    grad_tokens = (grad_first + nt(own_grad, qkv_matrix)).reshape(batch, rows, width)
    grad_tokens = cat([grad_tokens[:, :half] + received, grad_tokens[:, half:]], axis=1)
    grad_tokens = grad_tokens.astype(LOW)
    qkv_total = tn(tokens, own_grad)
    pair_total = tn(other_tokens, other_grad)
    qkv_total = cat([qkv_total[:, :width], qkv_total[:, width:] + pair_total], axis=1)
    qkv_grad = scattered(qkv_total, qkv_weight.shape)

    own_sum = jnp.sum(own_grad.astype(FULL), axis=0)
    other_sum = jnp.sum(other_grad.astype(FULL), axis=0)
    sums = [
        own_sum[:width],
        own_sum[2 * width :] + other_sum[width:],
        jnp.sum(grad_first, axis=0),
        jnp.sum(grad_hidden * first_normed, axis=0),
        jnp.sum(grad_hidden, axis=0),
        jnp.sum(grad_second, axis=0),
        jnp.sum(grad_out * second_normed, axis=0),
        jnp.sum(grad_out, axis=0),
        jnp.sum(grad_pre, axis=0),
    ]
    sums = lax.psum(cat(sums), ("dp", "row", "col"))
    index = lax.axis_index("row") * grid_cols + place
    devices = grid_rows * grid_cols
    split = sums[: 8 * width].reshape(8, width)
    vector_grad = lax.dynamic_slice_in_dim(split, index * (width // devices), width // devices, 1).T
    bias = sums[8 * width :]
    count = bias.shape[0] // devices
    bias_grad = lax.dynamic_slice_in_dim(bias, index * count, count, 0)
    return (
        result.reshape(batch, rows, width),
        grad_tokens,
        qkv_grad,
        out_grad,
        up_grad,
        down_grad,
        vector_grad,
        bias_grad,
    )


def solution(mesh):
    everywhere = ("dp", "row", "col")
    tokens = P(None, everywhere, None)
    matrix = P("row", "col")
    return jax.shard_map(
        local,
        mesh=mesh,
        in_specs=(
            tokens, matrix, matrix, matrix, matrix, P(), P(), P(None, ("dp", "row"), None), tokens,
        ),
        out_specs=(
            tokens, tokens, matrix, matrix, matrix, matrix, P(("row", "col"), None), P(("row", "col")),
        ),
        check_vma=False,
    )
```

```python
import functools
import math

import jax
import jax.numpy as jnp
from jax import lax
from jax.experimental import pallas as pl
from jax.experimental.pallas import tpu as pltpu
from jax.sharding import PartitionSpec as P

H = 12
CLEN = 128
LANES = 128
EPSILON = 1e-05
LOG2E = math.log2(math.e)
LOW = jnp.bfloat16
FULL = jnp.float32
cat = jnp.concatenate


def nt(left, right):
    return lax.dot_general(left, right, (((1,), (1,)), ((), ())), preferred_element_type=FULL)


def nn(left, right):
    return lax.dot_general(left, right, (((1,), (0,)), ((), ())), preferred_element_type=FULL)


def tn(left, right):
    return lax.dot_general(left, right, (((0,), (0,)), ((), ())), preferred_element_type=FULL)


def only(pick, value):
    return jnp.where(pick, value, jnp.zeros_like(value))


def spread(order):
    listed = []
    for stage in range(len(order)):
        for code in range(1 << stage):
            listed.append((stage, tuple(order[i] for i in range(stage) if code >> i & 1)))
    return listed


def flipped(position, axis, mask):
    bit = position[axis] // mask % 2
    return {**position, axis: position[axis] + mask * (1 - 2 * bit)}


def place_of(position, crossed):
    for axis, mask in crossed:
        position = flipped(position, axis, mask)
    return position


def here(axes):
    return {axis: lax.axis_index(axis) for axis in axes}


def bits_of(axis, size):
    return [(axis, 1 << bit) for bit in range(size.bit_length() - 1)]


def greet(partners):
    barrier = pltpu.get_barrier_semaphore()
    for axis, mask in partners:
        target = flipped(here((axis,)), axis, mask)
        pl.semaphore_signal(barrier, inc=1, device_id=target, device_id_type=pl.DeviceIdType.MESH)
    pl.semaphore_wait(barrier, len(partners))


class Gather:
    def __init__(self, own, whole, order, sends, arrivals, base):
        self.own, self.whole, self.order = own, whole, order
        self.sends, self.arrivals, self.base = sends, arrivals, base
        self.copies = spread(order)
        self.position = here(("row", "col"))

    def slot(self, position):
        depth, columns = self.own.shape
        first = pl.multiple_of(position["row"] * depth, 16)
        start = pl.multiple_of(position["col"] * columns, LANES)
        return self.whole.at[pl.ds(first, depth), pl.ds(start, columns)]

    def copy(self, index):
        stage, crossed = self.copies[index]
        axis, mask = self.order[stage]
        slot = self.slot(place_of(self.position, crossed))
        return pltpu.make_async_remote_copy(
            src_ref=slot if crossed else self.own,
            dst_ref=slot,
            send_sem=self.sends.at[self.base + index],
            recv_sem=self.arrivals.at[self.base + index],
            device_id=flipped(here((axis,)), axis, mask),
            device_id_type=pl.DeviceIdType.MESH,
        )

    def arrival(self, index):
        stage, crossed = self.copies[index]
        axis, mask = self.order[stage]
        slot = self.slot(place_of(self.position, crossed + (self.order[stage],)))
        return pltpu.make_async_remote_copy(
            src_ref=slot,
            dst_ref=slot,
            send_sem=self.sends.at[self.base + index],
            recv_sem=self.arrivals.at[self.base + index],
            device_id=flipped(here((axis,)), axis, mask),
            device_id_type=pl.DeviceIdType.MESH,
        )

    def placing(self, semaphore):
        return pltpu.make_async_copy(self.own, self.slot(self.position), semaphore)

    def source(self, index):
        crossed = self.copies[index][1]
        last = self.order.index(crossed[-1])
        return self.copies.index((last, crossed[:-1]))

    def first(self):
        return [i for i, (stage, crossed) in enumerate(self.copies) if not crossed]

    def later(self):
        return [i for i, (stage, crossed) in enumerate(self.copies) if crossed]


class Reduce:
    def __init__(self, total, low, acc, arrived, chain, sends, arrivals, loads, order, across):
        self.total, self.low, self.acc, self.arrived, self.chain = total, low, acc, arrived, chain
        self.sends, self.arrivals, self.loads = sends, arrivals, loads
        self.order, self.across = order, across
        self.position = here(("row", "col"))
        self.settled = set()

    def slot(self, crossed, size):
        position = place_of(self.position, crossed)
        depth, columns = self.acc.shape[1:]
        first = pl.multiple_of(position["row"] * size + self.low, 16)
        start = pl.multiple_of(position["col"] * columns, LANES)
        return self.total.at[pl.ds(first, depth), pl.ds(start, columns)]

    def crossed(self, code):
        return tuple(bit for i, bit in enumerate(self.order[1:]) if code >> i & 1)

    def number(self, stage, code):
        count = len(self.order)
        return sum(1 << (count - 1 - s) for s in range(stage)) + code

    def copy(self, stage, code, source):
        axis, mask = self.order[stage]
        number = self.number(stage, code)
        return pltpu.make_async_remote_copy(
            src_ref=source,
            dst_ref=self.arrived.at[number],
            send_sem=self.sends.at[number],
            recv_sem=self.arrivals.at[number],
            device_id=flipped(here((axis,)), axis, mask),
            device_id_type=pl.DeviceIdType.MESH,
        )

    def load(self, code, size):
        return pltpu.make_async_copy(
            self.slot(self.crossed(code), size), self.acc.at[code], self.loads.at[code]
        )

    def outgoing(self, stage, code, size):
        if stage == 0:
            return self.copy(0, code, self.slot((self.order[0],) + self.crossed(code), size))
        return self.copy(stage, code, self.acc.at[code << stage | 1 << (stage - 1)])

    def begin(self, size):
        self.size = size
        for code in range(1 << (len(self.order) - 1))[::-1]:
            self.outgoing(0, code, size).start()
        for code in range(1 << (len(self.order) - 1))[::-1]:
            self.load(code, size).start()

    def settle(self, stage, code):
        if (stage, code) in self.settled:
            return
        self.settled.add((stage, code))
        entry = code << stage
        if stage == 0:
            self.load(code, self.size).wait()
        else:
            self.settle(stage - 1, 2 * code)
        self.outgoing(stage, code, self.size).wait_recv()
        number = self.number(stage, code)
        value = self.acc[entry].astype(FULL) + self.arrived[number].astype(FULL)
        self.acc[entry] = value.astype(LOW)

    def codes(self, stage):
        return range(1 << (len(self.order) - 1 - stage))[::-1]

    def prepare(self, stage):
        count = len(self.order)
        if stage < count:
            for code in self.codes(stage):
                self.settle(stage - 1, 2 * code + 1)
        elif stage == count:
            self.settle(count - 1, 0)
        else:
            hop = stage - count - 1
            self.hop(hop).wait_recv()
            before = self.acc[0] if hop == 0 else self.chain[len(self.across) + hop - 1]
            value = before.astype(FULL) + self.chain[hop].astype(FULL)
            self.chain[len(self.across) + hop] = value.astype(LOW)

    def hop(self, hop):
        axis, mask = self.across[hop]
        number = (1 << len(self.order)) - 1 + hop
        target = self.target(axis, mask)
        source = self.acc.at[0] if hop == 0 else self.chain.at[len(self.across) + hop - 1]
        return pltpu.make_async_remote_copy(
            src_ref=source,
            dst_ref=self.chain.at[hop],
            send_sem=self.sends.at[number],
            recv_sem=self.arrivals.at[number],
            device_id=target,
            device_id_type=pl.DeviceIdType.MESH,
        )

    @staticmethod
    def target(axis, mask):
        return across_target(axis, mask)

    def launch(self, stage):
        if stage < len(self.order):
            for code in self.codes(stage):
                self.outgoing(stage, code, self.size).start()
        else:
            self.hop(stage - len(self.order)).start()

    def stages(self):
        return len(self.order) + len(self.across)

    def finish(self, out):
        hops = len(self.across)
        self.hop(hops - 1).wait_recv()
        before = self.acc[0] if hops == 1 else self.chain[2 * hops - 2]
        out[...] = before.astype(FULL) + self.chain[hops - 1].astype(FULL)
        for stage in range(len(self.order)):
            for code in self.codes(stage):
                self.outgoing(stage, code, self.size).wait_send()
        for hop in range(hops):
            self.hop(hop).wait_send()


def across_target(axis, mask):
    index = lax.axis_index(axis)
    return {axis: index // (mask + 1) * (mask + 1) + mask - index % (mask + 1)}


def across_bits(axis, size):
    return [(axis, (2 << bit) - 1) for bit in range(size.bit_length() - 1)]


def reduce_scratch(blocks, grid, hops):
    count = grid[0] * grid[1]
    shapes = []
    for depth, columns in blocks:
        shapes += [
            pltpu.VMEM((count // 2, depth, columns), LOW),
            pltpu.VMEM((count - 1, depth, columns), LOW),
            pltpu.VMEM((2 * hops, depth, columns), LOW),
            pltpu.SemaphoreType.DMA((count - 1 + hops,)),
            pltpu.SemaphoreType.DMA((count - 1 + hops,)),
            pltpu.SemaphoreType.DMA((count // 2,)),
        ]
    return shapes


def greet_all(row_bits, col_bits, across):
    barrier = pltpu.get_barrier_semaphore()
    targets = [flipped(here((axis,)), axis, mask) for axis, mask in row_bits + col_bits]
    targets += [across_target(axis, mask) for axis, mask in across]
    for target in targets:
        pl.semaphore_signal(barrier, inc=1, device_id=target, device_id_type=pl.DeviceIdType.MESH)
    pl.semaphore_wait(barrier, len(targets))


def end_kernel(total_ref, sums_ref, out_ref, all_ref, *scratch, grid, dp):
    rows, columns = grid
    row_bits, col_bits = bits_of("row", rows), bits_of("col", columns)
    across = across_bits("dp", dp)
    greet_all(row_bits, col_bits, across)
    depth = out_ref.shape[0]
    orders = [
        (tuple(row_bits + col_bits[::-1]), tuple(across)),
        (tuple(row_bits[:1] + col_bits[::-1] + row_bits[1:]), tuple(across[::-1])),
    ]
    parts = []
    for number, (order, hops) in enumerate(orders):
        buffers = scratch[6 * number : 6 * number + 6]
        acc, arrived, chain, sends, arrivals, loads = buffers
        part = Reduce(
            total_ref, number * depth // 2, acc, arrived, chain, sends, arrivals, loads, order, hops
        )
        parts.append(part)
    running, came, small_sends, small_arrivals = scratch[12:]
    targets = [flipped(here((axis,)), axis, mask) for axis, mask in row_bits + col_bits]
    targets += [across_target(axis, mask) for axis, mask in across]

    def small(stage):
        return pltpu.make_async_remote_copy(
            src_ref=running.at[stage],
            dst_ref=came.at[stage],
            send_sem=small_sends.at[stage],
            recv_sem=small_arrivals.at[stage],
            device_id=targets[stage],
            device_id_type=pl.DeviceIdType.MESH,
        )

    running[0] = sums_ref[...]
    for part in parts:
        part.begin(depth)
    small(0).start()
    stages = len(targets)
    for stage in range(1, stages):
        for part in parts:
            part.prepare(stage)
            part.launch(stage)
        small(stage - 1).wait_recv()
        running[stage] = running[stage - 1] + came[stage - 1]
        small(stage).start()
    for number, part in enumerate(parts):
        part.finish(out_ref.at[pl.ds(number * depth // 2, depth // 2)])
    small(stages - 1).wait_recv()
    all_ref[...] = running[stages - 1] + came[stages - 1]
    for stage in range(stages):
        small(stage).wait_send()


def end(total, sums, shape, grid, dp):
    hops = dp.bit_length() - 1
    stages = (grid[0] * grid[1] * dp).bit_length() - 1
    inside = pl.BlockSpec(memory_space=pltpu.VMEM)
    return pl.pallas_call(
        functools.partial(end_kernel, grid=grid, dp=dp),
        in_specs=[pl.BlockSpec(memory_space=pl.ANY), inside],
        out_specs=[inside, inside],
        out_shape=[jax.ShapeDtypeStruct(shape, FULL), jax.ShapeDtypeStruct(sums.shape, FULL)],
        scratch_shapes=reduce_scratch([(shape[0] // 2, shape[1])] * 2, grid, hops)
        + [
            pltpu.VMEM((stages,) + sums.shape, FULL),
            pltpu.VMEM((stages,) + sums.shape, FULL),
            pltpu.SemaphoreType.DMA((stages,)),
            pltpu.SemaphoreType.DMA((stages,)),
        ],
        compiler_params=pltpu.CompilerParams(collective_id=3, has_side_effects=True),
        name="end",
    )(total, sums)


def attend_step(q_ref, k_ref, v_ref, ok_ref, ov_ref, mask_ref, out_ref, lse_ref, *, head, exact):
    rows = q_ref.shape[1]
    half = rows // 2
    heads = LANES // head
    scale = jnp.asarray(head**-0.5, LOW)
    queries = q_ref[0]
    own_keys = k_ref[0] * scale
    own_values = v_ref[0]
    keys = cat([own_keys[:half], ok_ref[0] * scale], axis=0)
    near = own_keys[half:]
    values_t = cat([own_values[:half], ov_ref[0]], axis=0).T
    near_values_t = own_values[half:].T
    lane = lax.broadcasted_iota(jnp.int32, (1, LANES), 1) // head
    spans = [(start, start + CLEN) for start in range(0, half, CLEN)]
    picked = lax.broadcasted_iota(jnp.int32, (8, LANES), 0) == lane
    chooser = jnp.where(picked, 1.0, 0.0).astype(LOW)

    def with_ones(value):
        return cat([value, jnp.ones((16, value.shape[1]), LOW)], axis=0)

    def squares(value):
        return nt(chooser, value * value)

    flags = []
    if not exact:
        largest = jnp.maximum(
            jnp.max(squares(keys), axis=1, keepdims=True),
            jnp.max(squares(near), axis=1, keepdims=True),
        )
        bound = jnp.sqrt(squares(queries) * largest) * LOG2E
    for part in range(2):
        span = slice(part * half, (part + 1) * half)
        query = queries[span]
        outs = []
        for h in range(heads):
            pick = lane == h
            lines = slice(h * head, (h + 1) * head)
            scores = nt(only(pick, keys), query)
            if part:
                near_keys = only(pick, near)
                local = cat([nt(near_keys[a:b], query[a:b]) for a, b in spans], axis=1)
                local = local + mask_ref[0]
            if exact:
                top = jnp.max(scores, axis=0, keepdims=True)
                if part:
                    top = jnp.maximum(top, jnp.max(local, axis=0, keepdims=True))
                top = top * LOG2E
            else:
                top = bound[h : h + 1, span]
            weights = jnp.exp2(scores * LOG2E - top).astype(LOW)
            mixed = nn(with_ones(values_t[lines]), weights)
            if part:
                weights = jnp.exp2(local * LOG2E - top).astype(LOW)
                value = with_ones(near_values_t[lines])
                mixed = mixed + cat([nn(value[:, a:b], weights[:, a:b]) for a, b in spans], axis=1)
            total = mixed[head : head + 1]
            fine = jnp.logical_and(total > 1e-25, total < 1e30)
            flags.append(jnp.where(fine, 0.0, 1.0))
            outs.append(mixed[:head] / total)
            lse_ref[0, 0, h : h + 1, span] = top + jnp.log2(total)
        out_ref[0, span] = cat(outs, axis=0).T.astype(LOW)
    return sum(flags[1:], flags[0])


def attend_again_kernel(*refs, head):
    attend_step(*refs, head=head, exact=True)


def attend_kernel(
    q_ref, k_ref, v_ref, ok_ref, ov_ref, mask_ref, out_block, up_block, down_block,
    out_ref, lse_ref, flag_ref, out_whole, up_whole, down_whole,
    sends, arrivals, placed, *, head, grid,
):
    rows, columns = grid
    steps = pl.num_programs(1)
    step = pl.program_id(0) * steps + pl.program_id(1)
    final = 2 * steps - 1
    row_bits, col_bits = bits_of("row", rows), bits_of("col", columns)
    first_order = tuple(col_bits + row_bits[::-1])
    second_order = tuple(row_bits[:0:-1] + col_bits + row_bits[:1])
    per = len(spread(first_order))
    parts = [
        Gather(out_block, out_whole, first_order, sends, arrivals, 0),
        Gather(down_block, down_whole, first_order, sends, arrivals, per),
        Gather(up_block, up_whole, second_order, sends, arrivals, 2 * per),
    ]

    @pl.when(step == 0)
    def _():
        greet(row_bits + col_bits)
        for index in parts[0].first():
            for part in parts:
                part.copy(index).start()
        for number, part in enumerate(parts):
            part.placing(placed.at[number]).start()

    last = len(first_order) - 1
    events = {}
    for number, part in enumerate(parts):
        for index in part.later():
            stage, crossed = part.copies[index]
            if len(crossed) > 1 and number:
                when = final
            elif stage == last:
                when = (5, 8, 9)[number] + 2 * (len(crossed) > 1)
            else:
                when = (2, 6, 7)[number]
            events.setdefault(min(when, final), []).append((part, index))
    waited = set()
    for when in sorted(events):
        if when == final:
            continue

        @pl.when(step == when)
        def _(batch=events[when]):
            for part, index in batch:
                origin = part.source(index)
                if (part.base, origin) not in waited:
                    waited.add((part.base, origin))
                    part.arrival(origin).wait_recv()
                part.copy(index).start()

    flags = attend_step(
        q_ref, k_ref, v_ref, ok_ref, ov_ref, mask_ref, out_ref, lse_ref, head=head, exact=False
    )
    flag_ref[0, 0] = jnp.broadcast_to(flags, flag_ref.shape[2:])

    @pl.when(step == final)
    def _():
        for part, index in events.get(final, []):
            origin = part.source(index)
            if (part.base, origin) not in waited:
                waited.add((part.base, origin))
                part.arrival(origin).wait_recv()
            part.copy(index).start()
        for number, part in enumerate(parts):
            part.placing(placed.at[number]).wait()
            for index in range(per):
                if (part.base, index) not in waited:
                    part.arrival(index).wait_recv()
                part.copy(index).wait_send()


def attend_specs(own, other, mask):
    batch, rows, columns = own.shape
    steps = columns // (3 * LANES)

    def spec(count, offset):
        return pl.BlockSpec((1, count, LANES), lambda m, p: (m, 0, offset * steps + p))

    ins = [
        spec(rows, 0),
        spec(rows, 1),
        spec(rows, 2),
        spec(rows // 2, 0),
        spec(rows // 2, 1),
        pl.BlockSpec((1,) + mask.shape[1:], lambda m, p: (m, 0, 0)),
    ]
    return batch, rows, steps, spec, ins


def attend_again(own, other, mask, head):
    batch, rows, steps, spec, ins = attend_specs(own, other, mask)
    heads = LANES // head
    return pl.pallas_call(
        functools.partial(attend_again_kernel, head=head),
        grid=(batch, steps),
        in_specs=ins,
        out_specs=[spec(rows, 0), pl.BlockSpec((1, 1, heads, rows), lambda m, p: (m, p, 0, 0))],
        out_shape=[
            jax.ShapeDtypeStruct((batch, rows, steps * LANES), LOW),
            jax.ShapeDtypeStruct((batch, steps, heads, rows), FULL),
        ],
        name="attend_again",
    )(own, own, own, other, other, mask)


def attend(own, other, mask, blocks, grid, head):
    batch, rows, steps, spec, ins = attend_specs(own, other, mask)
    heads = LANES // head
    half = rows // 2
    anywhere = pl.BlockSpec(memory_space=pl.ANY)
    copies = 3 * (grid[0] * grid[1] - 1)
    work = batch * rows * (rows + CLEN) * steps * LANES
    wholes = [
        jax.ShapeDtypeStruct((block.shape[0] * grid[0], block.shape[1] * grid[1]), LOW)
        for block in blocks
    ]
    out, lse, flags, *wholes = pl.pallas_call(
        functools.partial(attend_kernel, head=head, grid=grid),
        grid=(batch, steps),
        in_specs=ins + [anywhere] * 3,
        out_specs=[
            spec(rows, 0),
            pl.BlockSpec((1, 1, heads, rows), lambda m, p: (m, p, 0, 0)),
            pl.BlockSpec((1, 1, 8, half), lambda m, p: (m, p, 0, 0)),
        ]
        + [anywhere] * 3,
        out_shape=[
            jax.ShapeDtypeStruct((batch, rows, steps * LANES), LOW),
            jax.ShapeDtypeStruct((batch, steps, heads, rows), FULL),
            jax.ShapeDtypeStruct((batch, steps, 8, half), FULL),
        ]
        + wholes,
        scratch_shapes=[
            pltpu.SemaphoreType.DMA((copies,)),
            pltpu.SemaphoreType.DMA((copies,)),
            pltpu.SemaphoreType.DMA((3,)),
        ],
        compiler_params=pltpu.CompilerParams(collective_id=1, has_side_effects=True),
        cost_estimate=pl.CostEstimate(
            flops=16 * work, bytes_accessed=own.size * 4, transcendentals=work // head
        ),
        name="attend",
    )(own, own, own, other, other, mask, *blocks)
    _, out, lse = lax.while_loop(
        lambda state: state[0] > 0.5,
        lambda state: (jnp.zeros((), FULL), *attend_again(own, other, mask, head)),
        (jnp.max(flags), out, lse),
    )
    return out, lse, wholes


def begin_kernel(tokens_ref, block_ref, other_ref, whole_ref, sends, arrivals, placed, *, grid):
    rows, columns = grid
    row_bits, col_bits = bits_of("row", rows), bits_of("col", columns)
    order = tuple(col_bits + row_bits[::-1])
    part = Gather(block_ref, whole_ref, order, sends, arrivals, 0)
    per = len(part.copies)
    half = other_ref.shape[1]
    partner = flipped(here(("col",)), "col", 1)
    exchanges = [
        pltpu.make_async_remote_copy(
            src_ref=tokens_ref.at[m, pl.ds(0, half)],
            dst_ref=other_ref.at[m],
            send_sem=sends.at[per + m],
            recv_sem=arrivals.at[per + m],
            device_id=partner,
            device_id_type=pl.DeviceIdType.MESH,
        )
        for m in range(other_ref.shape[0])
    ]
    greet(row_bits + col_bits)
    for index in part.first():
        part.copy(index).start()
    for exchange in exchanges:
        exchange.start()
    part.placing(placed.at[0]).start()
    waited = set()
    for index in part.later():
        origin = part.source(index)
        if origin not in waited:
            waited.add(origin)
            part.arrival(origin).wait_recv()
        part.copy(index).start()
    for index in range(per):
        if index not in waited:
            part.arrival(index).wait_recv()
        part.copy(index).wait_send()
    part.placing(placed.at[0]).wait()
    for exchange in exchanges:
        exchange.wait()


def begin(tokens, block, grid):
    batch, rows, width = tokens.shape
    copies = grid[0] * grid[1] - 1 + batch
    anywhere = pl.BlockSpec(memory_space=pl.ANY)
    return pl.pallas_call(
        functools.partial(begin_kernel, grid=grid),
        in_specs=[anywhere] * 2,
        out_specs=[anywhere] * 2,
        out_shape=[
            jax.ShapeDtypeStruct((batch, rows // 2, width), LOW),
            jax.ShapeDtypeStruct((block.shape[0] * grid[0], block.shape[1] * grid[1]), LOW),
        ],
        scratch_shapes=[
            pltpu.SemaphoreType.DMA((copies,)),
            pltpu.SemaphoreType.DMA((copies,)),
            pltpu.SemaphoreType.DMA((1,)),
        ],
        compiler_params=pltpu.CompilerParams(collective_id=0, has_side_effects=True),
        name="begin",
    )(tokens, block)


def attend_back_kernel(
    q_ref, k_ref, v_ref, ok_ref, ov_ref, mask_ref, out_ref, grad_ref, lse_ref,
    *rest, head, scale, grid, dp,
):
    if grid is not None:
        totals_in, rest = rest[:3], rest[3:]
    own_grad_ref, other_grad_ref, *rest = rest
    if grid is not None:
        blocks_out, rest = rest[:3], rest[3:]
    own_scratch, other_scratch, stored, *scratch = rest
    rows = q_ref.shape[1]
    half = rows // 2
    heads = LANES // head
    steps = pl.num_programs(1)
    group, tile = pl.program_id(0), pl.program_id(1)
    step = group * steps + tile
    slot = step % 2

    def stores(group, tile, slot):
        copies = []
        for part in range(3):
            lanes = pl.ds(pl.multiple_of((part * steps + tile) * LANES, LANES), LANES)
            copies.append(
                pltpu.make_async_copy(
                    own_scratch.at[slot, part], own_grad_ref.at[group, :, lanes], stored.at[slot, part]
                )
            )
        for part in range(2):
            lanes = pl.ds(pl.multiple_of((part * steps + tile) * LANES, LANES), LANES)
            copies.append(
                pltpu.make_async_copy(
                    other_scratch.at[slot, part],
                    other_grad_ref.at[group, :, lanes],
                    stored.at[slot, 3 + part],
                )
            )
        return copies

    @pl.when(step >= 2)
    def _():
        for copy in stores((step - 2) // steps, (step - 2) % steps, slot):
            copy.wait()

    launches = {}
    if grid is not None:
        final = pl.num_programs(0) * steps - 1
        row_bits, col_bits = bits_of("row", grid[0]), bits_of("col", grid[1])
        across = across_bits("dp", dp)
        by_row = tuple(row_bits + col_bits[::-1])
        by_col = tuple(row_bits[:1] + col_bits[::-1] + row_bits[1:])
        plans = [
            (by_row, tuple(across), (0, 1, 4, 8, 10)),
            (by_col, tuple(across[::-1]), (0, 1, 4, 8, 10)),
            (by_row, tuple(across), (0, 1, 6, 8, 10)),
        ]
        parts = []
        for number, (order, hops, _) in enumerate(plans):
            buffers = scratch[6 * number : 6 * number + 6]
            acc, arrived, chain, sends, arrivals, loads = buffers
            part = Reduce(
                totals_in[number], 0, acc, arrived, chain, sends, arrivals, loads, order, hops
            )
            part.size = blocks_out[number].shape[0]
            parts.append(part)

        @pl.when(step == 0)
        def _():
            greet_all(row_bits, col_bits, across)
            for part in parts:
                part.begin(part.size)

        for number, part in enumerate(parts):
            for stage in range(1, part.stages()):
                launches.setdefault(plans[number][2][stage], []).append((part, stage))
        for when in sorted(launches):

            @pl.when(step == when)
            def _(batch=launches[when]):
                for part, stage in batch:
                    part.prepare(stage)

    own_keys = k_ref[0] * jnp.asarray(scale, LOW)
    own_values = v_ref[0]
    keys = cat([own_keys[:half], ok_ref[0] * jnp.asarray(scale, LOW)], axis=0)
    near = own_keys[half:]
    values = cat([own_values[:half], ov_ref[0]], axis=0)
    near_values = own_values[half:]
    keys_t = keys.T
    near_t = near.T
    lane = lax.broadcasted_iota(jnp.int32, (1, LANES), 1) // head
    spans = [(start, start + CLEN) for start in range(0, half, CLEN)]
    totals = [None, None, None, None]

    def add(place, value):
        totals[place] = value if totals[place] is None else totals[place] + value

    for part in range(2):
        span = slice(part * half, (part + 1) * half)
        query = q_ref[0, span]
        grad = grad_ref[0, span]
        dots = (grad.astype(FULL) * out_ref[0, span].astype(FULL)).T
        query_grads = []
        for h in range(heads):
            pick = lane == h
            lines = slice(h * head, (h + 1) * head)
            lse = lse_ref[0, 0, h : h + 1, span]
            delta = jnp.sum(dots[lines], axis=0, keepdims=True)
            query_h = only(pick, query)
            grad_h = only(pick, grad)
            probs = jnp.exp2(nt(only(pick, keys), query) * LOG2E - lse)
            slopes = (probs * (nt(only(pick, values), grad) - delta)).astype(LOW)
            probs = probs.astype(LOW)
            query_grad = nn(keys_t[lines], slopes)
            add(0, nn(slopes, query_h))
            add(1, nn(probs, grad_h))
            if part:
                near_h = only(pick, near)
                near_values_h = only(pick, near_values)
                local = cat([nt(near_h[a:b], query[a:b]) for a, b in spans], axis=1)
                dlocal = cat([nt(near_values_h[a:b], grad[a:b]) for a, b in spans], axis=1)
                probs = jnp.exp2((local + mask_ref[0]) * LOG2E - lse)
                slopes = (probs * (dlocal - delta)).astype(LOW)
                probs = probs.astype(LOW)
                query_grad = query_grad + cat(
                    [nn(near_t[lines, a:b], slopes[:, a:b]) for a, b in spans], axis=1
                )
                add(2, cat([nn(slopes[:, a:b], query_h[a:b]) for a, b in spans], axis=0))
                add(3, cat([nn(probs[:, a:b], grad_h[a:b]) for a, b in spans], axis=0))
            query_grads.append(query_grad)
        own_scratch[slot, 0, span] = cat(query_grads, axis=0).T.astype(LOW)
    key_grad = (totals[0] * scale).astype(LOW)
    value_grad = totals[1].astype(LOW)
    own_scratch[slot, 1, :half] = key_grad[:half]
    own_scratch[slot, 2, :half] = value_grad[:half]
    own_scratch[slot, 1, half:] = (totals[2] * scale).astype(LOW)
    own_scratch[slot, 2, half:] = totals[3].astype(LOW)
    other_scratch[slot, 0] = key_grad[half:]
    other_scratch[slot, 1] = value_grad[half:]
    for copy in stores(group, tile, slot):
        copy.start()
    for when in sorted(launches):

        @pl.when(step == when)
        def _(batch=launches[when]):
            for part, stage in batch:
                part.launch(stage)

    if grid is not None:

        @pl.when(step == final)
        def _():
            for part, block in zip(parts, blocks_out):
                part.finish(block)

    @pl.when(step == pl.num_programs(0) * steps - 1)
    def _():
        for copy in stores((step - 1) // steps, (step - 1) % steps, 1 - slot):
            copy.wait()
        for copy in stores(group, tile, slot):
            copy.wait()


def attend_back(own, other, mask, out, grad, lse, head, sums=None, shapes=None, grid=None, dp=1):
    batch, rows, steps, spec, ins = attend_specs(own, other, mask)
    work = batch * rows * (rows + CLEN) * steps * LANES
    anywhere = pl.BlockSpec(memory_space=pl.ANY)
    more_in, more_out, more_shapes, more_scratch, operands = [], [], [], [], []
    params = None
    if grid is not None:
        more_in = [anywhere] * 3
        more_out = [pl.BlockSpec(shape, lambda m, p: (0, 0)) for shape in shapes]
        more_shapes = [jax.ShapeDtypeStruct(shape, FULL) for shape in shapes]
        more_scratch = reduce_scratch(shapes, grid, dp.bit_length() - 1)
        operands = list(sums)
        params = pltpu.CompilerParams(collective_id=2, has_side_effects=True)
    return pl.pallas_call(
        functools.partial(attend_back_kernel, head=head, scale=head**-0.5, grid=grid, dp=dp),
        grid=(batch, steps),
        in_specs=ins
        + [
            spec(rows, 0),
            spec(rows, 0),
            pl.BlockSpec((1, 1) + lse.shape[2:], lambda m, p: (m, p, 0, 0)),
        ]
        + more_in,
        out_specs=[anywhere] * 2 + more_out,
        out_shape=[
            jax.ShapeDtypeStruct(own.shape, LOW),
            jax.ShapeDtypeStruct(other.shape, LOW),
        ]
        + more_shapes,
        scratch_shapes=[
            pltpu.VMEM((2, 3, rows, LANES), LOW),
            pltpu.VMEM((2, 2, rows // 2, LANES), LOW),
            pltpu.SemaphoreType.DMA((2, 5)),
        ]
        + more_scratch,
        compiler_params=params,
        cost_estimate=pl.CostEstimate(
            flops=40 * work, bytes_accessed=own.size * 10, transcendentals=work // head
        ),
        name="attend_back",
    )(own, own, own, other, other, mask, out, grad, lse, *operands)


def swapped(value, axis, mask):
    pairs = [(source, source ^ mask) for source in range(lax.axis_size(axis))]
    return lax.ppermute(value, axis, pairs)


def masks_of(axis):
    return [1 << bit for bit in range(lax.axis_size(axis).bit_length() - 1)]


def bit_of(axis, mask):
    return jnp.where(lax.axis_index(axis) & mask == 0, 0, 1)


def joined(value, axis, mask, dim):
    other = swapped(value, axis, mask)
    first = bit_of(axis, mask) == 0
    return jnp.stack([jnp.where(first, value, other), jnp.where(first, other, value)], axis=dim)


def gathered(block):
    for mask in masks_of("col"):
        block = joined(block, "col", mask, 1).reshape(block.shape[0], -1)
    depth, columns = block.shape
    value = block[None]
    for mask in masks_of("row")[::-1]:
        value = joined(value, "row", mask, 1).reshape(-1, depth, columns)
    return value.reshape(-1, columns)


def parted(value, axis, mask, dim):
    bit = bit_of(axis, mask)
    keep = lax.dynamic_index_in_dim(value, bit, dim, keepdims=False)
    send = lax.dynamic_index_in_dim(value, 1 - bit, dim, keepdims=False)
    return keep + swapped(send.astype(LOW), axis, mask).astype(FULL)


def scattered(total, shape):
    value = total.reshape(-1, shape[0], total.shape[1])
    for mask in masks_of("row"):
        value = parted(value.reshape(-1, 2, *value.shape[1:]), "row", mask, 1)
    value = value.reshape(shape[0], -1)
    for mask in masks_of("col")[::-1]:
        value = parted(value.reshape(shape[0], 2, -1), "col", mask, 1)
    return over_dp(value)


def over_dp(value):
    for mask in masks_of("dp"):
        low = value.astype(LOW)
        value = low.astype(FULL) + swapped(low, "dp", 2 * mask - 1).astype(FULL)
    return value


def normalize(value):
    average = jnp.mean(value, axis=-1, keepdims=True)
    centred = value - average
    spread = jnp.mean(centred * centred, axis=-1, keepdims=True)
    inverse = lax.rsqrt(spread + EPSILON)
    return (centred * inverse, inverse)


def normalize_back(grad_normed, normed, inverse):
    first = jnp.mean(grad_normed, axis=-1, keepdims=True)
    second = jnp.mean(grad_normed * normed, axis=-1, keepdims=True)
    return inverse * (grad_normed - first - normed * second)


def near_mask(lengths, half):
    place = jnp.arange(CLEN, dtype=jnp.int32)[:, None]
    query = jnp.arange(half, dtype=jnp.int32)[None, :]
    limit = jnp.repeat(lengths, CLEN, axis=1)[:, None, :]
    seen = jnp.logical_and((place <= query % CLEN)[None], place[None] < limit)
    return jnp.where(seen, 0.0, -jnp.inf).astype(FULL)


def local(
    inputs,
    qkv_weight,
    out_weight,
    up_weight,
    down_weight,
    vectors,
    up_bias,
    cont_lengths,
    out_cotangent,
):
    grid_rows = lax.axis_size("row")
    grid_cols = lax.axis_size("col")
    place = lax.axis_index("col")
    side = place % 2
    batch, rows, width = inputs.shape
    half = rows // 2
    head = width // H
    half_conts = cont_lengths.shape[2] // 2
    group_lengths = lax.dynamic_index_in_dim(cont_lengths, place // 2, 1, keepdims=False)
    lengths = lax.dynamic_slice_in_dim(group_lengths, side * half_conts, half_conts, 1)
    mask = near_mask(lengths, half)

    grid = (grid_rows, grid_cols)
    direct = out_weight.shape[1] % LANES == 0 and qkv_weight.shape[1] % LANES == 0
    blocks = (out_weight, up_weight, down_weight)
    tokens = inputs.reshape(batch * rows, width)
    if direct:
        other_tokens, qkv_matrix = begin(inputs, qkv_weight, grid)
    else:
        other_tokens = swapped(inputs[:, :half], "col", 1)
        qkv_matrix = gathered(qkv_weight)
    other_tokens = other_tokens.reshape(batch * half, width)
    pair_matrix = qkv_matrix[:, width:]
    shift = cat([vectors[:, 0], jnp.zeros((width,), FULL), vectors[:, 1]])
    pair_shift = shift[width:]
    own = (nn(tokens, qkv_matrix) + shift).astype(LOW).reshape(batch, rows, 3 * width)
    other = (nn(other_tokens, pair_matrix) + pair_shift).astype(LOW)
    other = other.reshape(batch, half, 2 * width)
    if direct:
        attended, lse, (out_matrix, up_matrix, down_matrix) = attend(
            own, other, mask, blocks, grid, head
        )
    else:
        attended, lse = attend_again(own, other, mask, head)
        out_matrix, up_matrix, down_matrix = (gathered(block) for block in blocks)
    attended = attended.reshape(batch * rows, width)
    first_sum = tokens.astype(FULL) + nn(attended, out_matrix) + vectors[:, 2]
    first_normed, first_inverse = normalize(first_sum)
    hidden = first_normed * vectors[:, 3] + vectors[:, 4]
    hidden_low = hidden.astype(LOW)
    pre_act = nn(hidden_low, up_matrix) + up_bias
    phi = 0.5 + 0.5 * lax.erf(pre_act * (0.5**0.5))
    slope = phi + pre_act * (jnp.exp(-0.5 * pre_act * pre_act) * ((2 * math.pi) ** -0.5))
    act_low = (pre_act * phi).astype(LOW)
    slope_low = slope.astype(LOW)
    second_sum = hidden + nn(act_low, down_matrix) + vectors[:, 5]
    second_normed, second_inverse = normalize(second_sum)
    result = (second_normed * vectors[:, 6] + vectors[:, 7]).astype(LOW)

    grad_out = out_cotangent.reshape(batch * rows, width).astype(FULL)
    grad_second = normalize_back(grad_out * vectors[:, 6], second_normed, second_inverse)
    grad_second_low = grad_second.astype(LOW)
    grad_pre = nt(grad_second_low, down_matrix) * slope_low.astype(FULL)
    grad_pre_low = grad_pre.astype(LOW)
    grad_hidden = grad_second + nt(grad_pre_low, up_matrix)
    grad_first = normalize_back(grad_hidden * vectors[:, 3], first_normed, first_inverse)
    grad_first_low = grad_first.astype(LOW)
    grad_attended = nt(grad_first_low, out_matrix).astype(LOW)
    shapes = (down_weight.shape, up_weight.shape, out_weight.shape)
    totals = (
        tn(act_low, grad_second_low), tn(hidden_low, grad_pre_low), tn(attended, grad_first_low),
    )
    operands = (
        own,
        other,
        mask,
        attended.reshape(batch, rows, width),
        grad_attended.reshape(batch, rows, width),
        lse,
        head,
    )
    if direct:
        totals = [total.astype(LOW) for total in totals]
        own_grad, other_grad, down_grad, up_grad, out_grad = attend_back(
            *operands, totals, shapes, grid, lax.axis_size("dp")
        )
    else:
        own_grad, other_grad = attend_back(*operands)
        down_grad, up_grad, out_grad = (
            scattered(total, shape) for total, shape in zip(totals, shapes)
        )
    own_grad = own_grad.reshape(batch * rows, 3 * width)
    other_grad = other_grad.reshape(batch * half, 2 * width)
    sent = nt(other_grad, pair_matrix).astype(LOW).reshape(batch, half, width)
    received = swapped(sent, "col", 1).astype(FULL)
    grad_tokens = (grad_first + nt(own_grad, qkv_matrix)).reshape(batch, rows, width)
    grad_tokens = cat([grad_tokens[:, :half] + received, grad_tokens[:, half:]], axis=1)
    grad_tokens = grad_tokens.astype(LOW)
    qkv_total = tn(tokens, own_grad)
    pair_total = tn(other_tokens, other_grad)
    qkv_total = cat([qkv_total[:, :width], qkv_total[:, width:] + pair_total], axis=1)

    own_sum = jnp.sum(own_grad.astype(FULL), axis=0)
    other_sum = jnp.sum(other_grad.astype(FULL), axis=0)
    sums = [
        own_sum[:width],
        own_sum[2 * width :] + other_sum[width:],
        jnp.sum(grad_first, axis=0),
        jnp.sum(grad_hidden * first_normed, axis=0),
        jnp.sum(grad_hidden, axis=0),
        jnp.sum(grad_second, axis=0),
        jnp.sum(grad_out * second_normed, axis=0),
        jnp.sum(grad_out, axis=0),
        jnp.sum(grad_pre, axis=0),
    ]
    sums = cat(sums)
    if direct:
        lines = sums.reshape(-1, width)
        lines = jnp.pad(lines, ((0, -lines.shape[0] % 8), (0, 0)))
        qkv_grad, lines = end(
            qkv_total.astype(LOW), lines, qkv_weight.shape, grid, lax.axis_size("dp")
        )
        sums = lines.reshape(-1)[: sums.shape[0]]
    else:
        qkv_grad = scattered(qkv_total, qkv_weight.shape)
        sums = lax.psum(sums, ("dp", "row", "col"))
    index = lax.axis_index("row") * grid_cols + place
    devices = grid_rows * grid_cols
    split = sums[: 8 * width].reshape(8, width)
    vector_grad = lax.dynamic_slice_in_dim(split, index * (width // devices), width // devices, 1).T
    bias = sums[8 * width :]
    count = bias.shape[0] // devices
    bias_grad = lax.dynamic_slice_in_dim(bias, index * count, count, 0)
    return (
        result.reshape(batch, rows, width),
        grad_tokens,
        qkv_grad,
        out_grad,
        up_grad,
        down_grad,
        vector_grad,
        bias_grad,
    )


def solution(mesh):
    everywhere = ("dp", "row", "col")
    tokens = P(None, everywhere, None)
    matrix = P("row", "col")
    return jax.shard_map(
        local,
        mesh=mesh,
        in_specs=(
            tokens, matrix, matrix, matrix, matrix, P(), P(), P(None, ("dp", "row"), None), tokens,
        ),
        out_specs=(
            tokens, tokens, matrix, matrix, matrix, matrix, P(("row", "col"), None), P(("row", "col")),
        ),
        check_vma=False,
    )
```

```python
import functools
import math

import jax
import jax.numpy as jnp
from jax import lax
from jax.experimental import pallas as pl
from jax.experimental.pallas import tpu as pltpu
from jax.sharding import PartitionSpec as P

H = 12
CLEN = 128
LANES = 128
EPSILON = 1e-05
LOG2E = math.log2(math.e)
LOW = jnp.bfloat16
FULL = jnp.float32
cat = jnp.concatenate


def nt(left, right):
    return lax.dot_general(left, right, (((1,), (1,)), ((), ())), preferred_element_type=FULL)


def nn(left, right):
    return lax.dot_general(left, right, (((1,), (0,)), ((), ())), preferred_element_type=FULL)


def tn(left, right):
    return lax.dot_general(left, right, (((0,), (0,)), ((), ())), preferred_element_type=FULL)


def folded(value):
    return jnp.sum(value.reshape(-1, 8, value.shape[1]), axis=0)


def only(pick, value):
    return jnp.where(pick, value, jnp.zeros_like(value))


def spread(order):
    listed = []
    for stage in range(len(order)):
        for code in range(1 << stage):
            listed.append((stage, tuple(order[i] for i in range(stage) if code >> i & 1)))
    return listed


def flipped(position, axis, mask):
    bit = position[axis] // mask % 2
    return {**position, axis: position[axis] + mask * (1 - 2 * bit)}


def place_of(position, crossed):
    for axis, mask in crossed:
        position = flipped(position, axis, mask)
    return position


def here(axes):
    return {axis: lax.axis_index(axis) for axis in axes}


def bits_of(axis, size):
    return [(axis, 1 << bit) for bit in range(size.bit_length() - 1)]


def greet(partners):
    barrier = pltpu.get_barrier_semaphore()
    for axis, mask in partners:
        target = flipped(here((axis,)), axis, mask)
        pl.semaphore_signal(barrier, inc=1, device_id=target, device_id_type=pl.DeviceIdType.MESH)
    pl.semaphore_wait(barrier, len(partners))


class Gather:
    def __init__(self, own, whole, order, sends, arrivals, base):
        self.own, self.whole, self.order = own, whole, order
        self.sends, self.arrivals, self.base = sends, arrivals, base
        self.copies = spread(order)
        self.position = here(("row", "col"))

    def slot(self, position):
        depth, columns = self.own.shape
        first = pl.multiple_of(position["row"] * depth, 16)
        start = pl.multiple_of(position["col"] * columns, LANES)
        return self.whole.at[pl.ds(first, depth), pl.ds(start, columns)]

    def copy(self, index):
        stage, crossed = self.copies[index]
        axis, mask = self.order[stage]
        slot = self.slot(place_of(self.position, crossed))
        return pltpu.make_async_remote_copy(
            src_ref=slot if crossed else self.own,
            dst_ref=slot,
            send_sem=self.sends.at[self.base + index],
            recv_sem=self.arrivals.at[self.base + index],
            device_id=flipped(here((axis,)), axis, mask),
            device_id_type=pl.DeviceIdType.MESH,
        )

    def arrival(self, index):
        stage, crossed = self.copies[index]
        axis, mask = self.order[stage]
        slot = self.slot(place_of(self.position, crossed + (self.order[stage],)))
        return pltpu.make_async_remote_copy(
            src_ref=slot,
            dst_ref=slot,
            send_sem=self.sends.at[self.base + index],
            recv_sem=self.arrivals.at[self.base + index],
            device_id=flipped(here((axis,)), axis, mask),
            device_id_type=pl.DeviceIdType.MESH,
        )

    def loading(self, held, semaphores):
        return pltpu.make_async_copy(self.own, held, semaphores.at[0])

    def placing(self, held, semaphores):
        return pltpu.make_async_copy(held, self.slot(self.position), semaphores.at[1])

    def source(self, index):
        crossed = self.copies[index][1]
        last = self.order.index(crossed[-1])
        return self.copies.index((last, crossed[:-1]))

    def first(self):
        return [i for i, (stage, crossed) in enumerate(self.copies) if not crossed]

    def later(self):
        return [i for i, (stage, crossed) in enumerate(self.copies) if crossed]


class Reduce:
    def __init__(self, total, low, acc, arrived, chain, sends, arrivals, loads, order, across):
        self.total, self.low, self.acc, self.arrived, self.chain = total, low, acc, arrived, chain
        self.sends, self.arrivals, self.loads = sends, arrivals, loads
        self.order, self.across = order, across
        self.position = here(("row", "col"))
        self.settled = set()

    def slot(self, crossed, size):
        position = place_of(self.position, crossed)
        depth, columns = self.acc.shape[1:]
        first = pl.multiple_of(position["row"] * size + self.low, 16)
        start = pl.multiple_of(position["col"] * columns, LANES)
        return self.total.at[pl.ds(first, depth), pl.ds(start, columns)]

    def crossed(self, code):
        return tuple(bit for i, bit in enumerate(self.order[1:]) if code >> i & 1)

    def number(self, stage, code):
        count = len(self.order)
        return sum(1 << (count - 1 - s) for s in range(stage)) + code

    def copy(self, stage, code, source):
        axis, mask = self.order[stage]
        number = self.number(stage, code)
        return pltpu.make_async_remote_copy(
            src_ref=source,
            dst_ref=self.arrived.at[number],
            send_sem=self.sends.at[number],
            recv_sem=self.arrivals.at[number],
            device_id=flipped(here((axis,)), axis, mask),
            device_id_type=pl.DeviceIdType.MESH,
        )

    def load(self, code, size):
        return pltpu.make_async_copy(
            self.slot(self.crossed(code), size), self.acc.at[code], self.loads.at[code]
        )

    def outgoing(self, stage, code, size):
        if stage == 0:
            return self.copy(0, code, self.slot((self.order[0],) + self.crossed(code), size))
        return self.copy(stage, code, self.acc.at[code << stage | 1 << (stage - 1)])

    def begin(self, size):
        self.size = size
        for code in range(1 << (len(self.order) - 1))[::-1]:
            self.outgoing(0, code, size).start()
        for code in range(1 << (len(self.order) - 1))[::-1]:
            self.load(code, size).start()

    def settle(self, stage, code):
        if (stage, code) in self.settled:
            return
        self.settled.add((stage, code))
        entry = code << stage
        if stage == 0:
            self.load(code, self.size).wait()
        else:
            self.settle(stage - 1, 2 * code)
        self.outgoing(stage, code, self.size).wait_recv()
        number = self.number(stage, code)
        value = self.acc[entry].astype(FULL) + self.arrived[number].astype(FULL)
        self.acc[entry] = value.astype(LOW)

    def codes(self, stage):
        return range(1 << (len(self.order) - 1 - stage))[::-1]

    def prepare(self, stage):
        count = len(self.order)
        if stage < count:
            for code in self.codes(stage):
                self.settle(stage - 1, 2 * code + 1)
        elif stage == count:
            self.settle(count - 1, 0)
        else:
            hop = stage - count - 1
            self.hop(hop).wait_recv()
            before = self.acc[0] if hop == 0 else self.chain[len(self.across) + hop - 1]
            value = before.astype(FULL) + self.chain[hop].astype(FULL)
            self.chain[len(self.across) + hop] = value.astype(LOW)

    def hop(self, hop):
        axis, mask = self.across[hop]
        number = (1 << len(self.order)) - 1 + hop
        target = self.target(axis, mask)
        source = self.acc.at[0] if hop == 0 else self.chain.at[len(self.across) + hop - 1]
        return pltpu.make_async_remote_copy(
            src_ref=source,
            dst_ref=self.chain.at[hop],
            send_sem=self.sends.at[number],
            recv_sem=self.arrivals.at[number],
            device_id=target,
            device_id_type=pl.DeviceIdType.MESH,
        )

    @staticmethod
    def target(axis, mask):
        return across_target(axis, mask)

    def launch(self, stage):
        if stage < len(self.order):
            for code in self.codes(stage):
                self.outgoing(stage, code, self.size).start()
        else:
            self.hop(stage - len(self.order)).start()

    def stages(self):
        return len(self.order) + len(self.across)

    def close(self, out):
        self.settle(len(self.order) - 1, 0)
        out[...] = self.acc[0]
        self.sent()

    def sent(self):
        for stage in range(len(self.order)):
            for code in self.codes(stage):
                self.outgoing(stage, code, self.size).wait_send()

    def finish(self, out):
        hops = len(self.across)
        self.hop(hops - 1).wait_recv()
        before = self.acc[0] if hops == 1 else self.chain[2 * hops - 2]
        out[...] = before.astype(FULL) + self.chain[hops - 1].astype(FULL)
        self.sent()
        for hop in range(hops):
            self.hop(hop).wait_send()


def across_target(axis, mask):
    index = lax.axis_index(axis)
    return {axis: index // (mask + 1) * (mask + 1) + mask - index % (mask + 1)}


def across_bits(axis, size):
    return [(axis, (2 << bit) - 1) for bit in range(size.bit_length() - 1)]


class Chain:
    def __init__(self, start, buffers, sends, arrivals, across):
        self.start, self.buffers, self.across = start, buffers, across
        self.sends, self.arrivals = sends, arrivals

    def before(self, hop):
        return self.start if hop == 0 else self.buffers.at[len(self.across) + hop - 1]

    def hop(self, hop):
        axis, mask = self.across[hop]
        return pltpu.make_async_remote_copy(
            src_ref=self.before(hop),
            dst_ref=self.buffers.at[hop],
            send_sem=self.sends.at[hop],
            recv_sem=self.arrivals.at[hop],
            device_id=across_target(axis, mask),
            device_id_type=pl.DeviceIdType.MESH,
        )

    def total(self, hop):
        self.hop(hop).wait_recv()
        return self.before(hop)[...].astype(FULL) + self.buffers[hop].astype(FULL)

    def prepare(self, hop):
        self.buffers[len(self.across) + hop - 1] = self.total(hop - 1).astype(LOW)

    def launch(self, hop):
        self.hop(hop).start()

    def finish(self, out):
        out[...] = self.total(len(self.across) - 1)
        for hop in range(len(self.across)):
            self.hop(hop).wait_send()


def chain_scratch(blocks, hops):
    shapes = []
    for depth, columns in blocks:
        shapes += [
            pltpu.VMEM((2 * hops, depth, columns), LOW),
            pltpu.SemaphoreType.DMA((hops,)),
            pltpu.SemaphoreType.DMA((hops,)),
        ]
    return shapes


def halve_scratch(shape, grid):
    count = grid[0] * grid[1]
    depth, columns = shape
    return [
        pltpu.VMEM((count // 2, depth // 2, columns), LOW),
        pltpu.VMEM((count - 1, depth // 2, columns), LOW),
        pltpu.SemaphoreType.DMA((count - 1,)),
        pltpu.SemaphoreType.DMA((count - 1,)),
        pltpu.SemaphoreType.DMA((count // 2,)),
    ] * 2


class Halving:
    def __init__(self, total, out, scratch, grid, whens):
        self.row_bits, self.col_bits = bits_of("row", grid[0]), bits_of("col", grid[1])
        self.out, self.whens = out, whens
        self.depth = out.shape[0]
        first, later = tuple(self.row_bits[:1]), tuple(self.row_bits[1:])
        orders = [first + later + tuple(self.col_bits[::-1]), first + tuple(self.col_bits[::-1]) + later]
        self.parts = []
        for number, order in enumerate(orders):
            acc, arrived, sends, arrivals, loads = scratch[5 * number : 5 * number + 5]
            low = number * self.depth // 2
            self.parts.append(
                Reduce(total, low, acc, arrived, None, sends, arrivals, loads, order, ())
            )

    def before(self, step):
        @pl.when(step == 0)
        def _():
            greet(self.row_bits + self.col_bits)
            for part in self.parts:
                part.begin(self.depth)

        for part in self.parts:
            part.size = self.depth
        for stage in range(1, self.parts[0].stages()):

            @pl.when(step == self.whens[stage])
            def _(stage=stage):
                for part in self.parts:
                    part.prepare(stage)
                    part.launch(stage)

    def after(self, step, final):
        @pl.when(step == final)
        def _():
            half = self.depth // 2
            for number, part in enumerate(self.parts):
                part.close(self.out.at[pl.ds(number * half, half)])


def widen_kernel(
    second_ref, hidden_ref, down_ref, slope_ref, total_ref,
    grad_ref, up_ref, sums_ref, block_ref, turned, *scratch, grid, whens, chunk,
):
    step = pl.program_id(0)
    carried = Halving(total_ref, block_ref, scratch, grid, whens)
    carried.before(step)

    @pl.when(step == 0)
    def _():
        turned[...] = hidden_ref[...].T

    rows = grad_ref.shape[0]

    def part(index, total):
        span = pl.ds(pl.multiple_of(index * chunk, chunk), chunk)
        grad = nt(second_ref[span], down_ref[...]) * slope_ref[span].astype(FULL)
        grad_ref[span] = grad.astype(LOW)
        return total + jnp.sum(grad.reshape(chunk // 8, 8, grad.shape[1]), axis=0)

    sums_ref[...] = lax.fori_loop(0, rows // chunk, part, jnp.zeros(sums_ref.shape, FULL))
    up_ref[...] = nn(turned[...], grad_ref[...]).astype(LOW)
    carried.after(step, pl.num_programs(0) - 1)


def widen(second, hidden, down_matrix, slope, down_total, shape, grid):
    rows, width = second.shape
    hidden_units = down_matrix.shape[0]
    tile = 512
    steps = hidden_units // tile
    once = pl.Buffered(buffer_count=1)
    return pl.pallas_call(
        functools.partial(widen_kernel, grid=grid, whens=(0, 1, 4), chunk=min(rows, 1024)),
        grid=(steps,),
        in_specs=[
            pl.BlockSpec((rows, width), lambda i: (0, 0), pipeline_mode=once),
            pl.BlockSpec((rows, width), lambda i: (0, 0), pipeline_mode=once),
            pl.BlockSpec((tile, width), lambda i: (i, 0)),
            pl.BlockSpec((rows, tile), lambda i: (0, i)),
            pl.BlockSpec(memory_space=pl.ANY),
        ],
        out_specs=[
            pl.BlockSpec((rows, tile), lambda i: (0, i)),
            pl.BlockSpec((width, tile), lambda i: (0, i)),
            pl.BlockSpec((8, tile), lambda i: (0, i)),
            pl.BlockSpec(shape, lambda i: (0, 0)),
        ],
        out_shape=[
            jax.ShapeDtypeStruct((rows, hidden_units), LOW),
            jax.ShapeDtypeStruct((width, hidden_units), LOW),
            jax.ShapeDtypeStruct((8, hidden_units), FULL),
            jax.ShapeDtypeStruct(shape, LOW),
        ],
        scratch_shapes=[pltpu.VMEM((width, rows), LOW)] + halve_scratch(shape, grid),
        compiler_params=pltpu.CompilerParams(
            collective_id=4, has_side_effects=True, vmem_limit_bytes=56 * 2**20
        ),
        cost_estimate=pl.CostEstimate(
            flops=4 * rows * width * hidden_units, bytes_accessed=6 * rows * hidden_units, transcendentals=0
        ),
        name="widen",
    )(second, hidden, down_matrix, slope, down_total)


def narrow_kernel(
    grad_ref, second_ref, normed_ref, inverse_ref, attended_ref, up_ref, out_ref, gain_ref, total_ref,
    first_ref, back_ref, out_total_ref, sums_ref, block_ref, held, *scratch, grid, whens,
):
    step = pl.program_id(0)
    final = pl.num_programs(0) - 1
    carried = Halving(total_ref, block_ref, scratch, grid, whens)
    carried.before(step)

    @pl.when(step == 0)
    def _():
        held[...] = jnp.zeros(held.shape, FULL)
        sums_ref[...] = jnp.zeros(sums_ref.shape, FULL)

    grad_hidden = nt(grad_ref[...], up_ref[...]) + second_ref[...].astype(FULL)
    normed = normed_ref[...].astype(FULL)
    grad_first = normalize_back(grad_hidden * gain_ref[...], normed, inverse_ref[...])
    low = grad_first.astype(LOW)
    first_ref[...] = low
    back_ref[...] = nt(low, out_ref[...]).astype(LOW)
    held[...] += tn(attended_ref[...], low)

    sums_ref[0:8] += folded(grad_first)
    sums_ref[8:16] += folded(grad_hidden * normed)
    sums_ref[16:24] += folded(grad_hidden)
    carried.after(step, final)

    @pl.when(step == final)
    def _():
        out_total_ref[...] = held[...].astype(LOW)


def narrow(grad, second, normed, inverse, attended, up_matrix, out_matrix, gain, up_total, shape, grid):
    rows, width = second.shape
    hidden_units = grad.shape[1]
    tile = 256
    once = pl.Buffered(buffer_count=1)

    def block(columns):
        return pl.BlockSpec((tile, columns), lambda i: (i, 0))

    def whole(shape, **more):
        return pl.BlockSpec(shape, lambda i: (0, 0), **more)

    return pl.pallas_call(
        functools.partial(narrow_kernel, grid=grid, whens=(0, 1, 5)),
        grid=(rows // tile,),
        in_specs=[
            block(hidden_units),
            block(width),
            block(width),
            block(1),
            block(width),
            whole(up_matrix.shape, pipeline_mode=once),
            whole(out_matrix.shape, pipeline_mode=once),
            whole(gain.shape),
            pl.BlockSpec(memory_space=pl.ANY),
        ],
        out_specs=[
            block(width), block(width), whole(out_matrix.shape), whole((24, width)), whole(shape),
        ],
        out_shape=[
            jax.ShapeDtypeStruct((rows, width), LOW),
            jax.ShapeDtypeStruct((rows, width), LOW),
            jax.ShapeDtypeStruct(out_matrix.shape, LOW),
            jax.ShapeDtypeStruct((24, width), FULL),
            jax.ShapeDtypeStruct(shape, LOW),
        ],
        scratch_shapes=[pltpu.VMEM(out_matrix.shape, FULL)] + halve_scratch(shape, grid),
        compiler_params=pltpu.CompilerParams(
            collective_id=5, has_side_effects=True, vmem_limit_bytes=56 * 2**20
        ),
        cost_estimate=pl.CostEstimate(
            flops=2 * rows * width * (hidden_units + 2 * width),
            bytes_accessed=2 * rows * hidden_units,
            transcendentals=0,
        ),
        name="narrow",
    )(grad, second, normed, inverse, attended, up_matrix, out_matrix, gain, up_total)


def reduce_scratch(blocks, grid, hops):
    count = grid[0] * grid[1]
    shapes = []
    for depth, columns in blocks:
        shapes += [
            pltpu.VMEM((count // 2, depth, columns), LOW),
            pltpu.VMEM((count - 1, depth, columns), LOW),
            pltpu.VMEM((2 * hops, depth, columns), LOW),
            pltpu.SemaphoreType.DMA((count - 1 + hops,)),
            pltpu.SemaphoreType.DMA((count - 1 + hops,)),
            pltpu.SemaphoreType.DMA((count // 2,)),
        ]
    return shapes


def greet_all(row_bits, col_bits, across):
    barrier = pltpu.get_barrier_semaphore()
    targets = [flipped(here((axis,)), axis, mask) for axis, mask in row_bits + col_bits]
    targets += [across_target(axis, mask) for axis, mask in across]
    for target in targets:
        pl.semaphore_signal(barrier, inc=1, device_id=target, device_id_type=pl.DeviceIdType.MESH)
    pl.semaphore_wait(barrier, len(targets))


def end_kernel(
    own_ref, matrix_ref, first_ref, total_ref, pair_ref, norm_ref, bias_ref, last_ref,
    tokens_ref, out_ref, all_ref, *scratch, grid, dp,
):
    step = pl.program_id(0)
    final = pl.num_programs(0) - 1
    rows, columns = grid
    row_bits, col_bits = bits_of("row", rows), bits_of("col", columns)
    across = across_bits("dp", dp)
    first, later = tuple(row_bits[:1]), tuple(row_bits[1:])
    orders = [first + later + tuple(col_bits[::-1]), first + tuple(col_bits[::-1]) + later]
    depth = out_ref.shape[0]
    part_depth = depth // 4
    parts = []
    for number in range(4):
        acc, arrived, chain, sends, arrivals, loads = scratch[6 * number : 6 * number + 6]
        part = Reduce(
            total_ref, number * part_depth, acc, arrived, chain, sends, arrivals, loads,
            orders[number % 2], tuple(across),
        )
        part.size = depth
        parts.append(part)
    running, came, small_sends, small_arrivals = scratch[24:]
    targets = [flipped(here((axis,)), axis, mask) for axis, mask in row_bits + col_bits]
    targets += [across_target(axis, mask) for axis, mask in across]

    def small(stage):
        return pltpu.make_async_remote_copy(
            src_ref=running.at[stage],
            dst_ref=came.at[stage],
            send_sem=small_sends.at[stage],
            recv_sem=small_arrivals.at[stage],
            device_id=targets[stage],
            device_id_type=pl.DeviceIdType.MESH,
        )

    stages = len(targets)
    events = []
    for number, part in enumerate(parts):
        for stage in range(1, stages):
            late = 0 if number < 2 else (1.1 if stage == 1 else 2.1)
            events.append((stage + late, number, stage))
    whens = {1: 2, 2: 5, 3: 5}
    batches = {}
    for key, number, stage in sorted(events):
        batches.setdefault(min(whens.get(int(key), final), final), []).append((number, stage))

    def advance(batch):
        for number, stage in batch:
            parts[number].prepare(stage)
            parts[number].launch(stage)
            if number == 1:
                small(stage - 1).wait_recv()
                running[stage] = running[stage - 1] + came[stage - 1]
                small(stage).start()

    @pl.when(step == 0)
    def _():
        greet_all(row_bits, col_bits, across)
        for part in parts:
            part.begin(depth)
        running[0] = jnp.zeros(running.shape[1:], FULL)

        def column_sums(value):
            return jnp.sum(value, axis=0, keepdims=True)

        width = running.shape[2]
        tiles = pair_ref.shape[1]
        for kind in range(2):
            lines = slice(8 * kind, 8 * kind + 8)
            for tile in range(tiles):
                value = sum(pair_ref[m, tile, lines] for m in range(pair_ref.shape[0]))
                running[0, kind : kind + 1, tile * LANES : (tile + 1) * LANES] = column_sums(value)
        for number in range(3):
            running[0, 2 + number : 3 + number] = column_sums(norm_ref[8 * number : 8 * number + 8])
            running[0, 5 + number : 6 + number] = last_ref[number : number + 1]
        for number in range(bias_ref.shape[1] // width):
            value = bias_ref[:, number * width : (number + 1) * width]
            running[0, 8 + number : 9 + number] = column_sums(value)
        small(0).start()

    for when in sorted(batches):
        if when < final:
            pl.when(step == when)(functools.partial(advance, batches[when]))

    grad = nt(own_ref[...], matrix_ref[...]) + first_ref[...].astype(FULL)
    tokens_ref[...] = grad.astype(LOW)

    @pl.when(step == final)
    def _():
        advance(batches.get(final, []))
        for number, part in enumerate(parts):
            part.finish(out_ref.at[pl.ds(number * part_depth, part_depth)])
        small(stages - 1).wait_recv()
        all_ref[...] = running[stages - 1] + came[stages - 1]
        for stage in range(stages):
            small(stage).wait_send()


def end(own, matrix, first, total, sums, shape, grid, dp):
    lines = 8 + sums[2].shape[1] // first.shape[1]
    lines = (lines + -lines % 8, first.shape[1])
    hops = dp.bit_length() - 1
    stages = (grid[0] * grid[1] * dp).bit_length() - 1
    rows, width = first.shape
    tile = 256

    def block(columns):
        return pl.BlockSpec((tile, columns), lambda i: (i, 0))

    def whole(shape, **more):
        return pl.BlockSpec(shape, lambda i: (0, 0), **more)

    return pl.pallas_call(
        functools.partial(end_kernel, grid=grid, dp=dp),
        grid=(rows // tile,),
        in_specs=[
            block(own.shape[1]),
            whole(matrix.shape, pipeline_mode=pl.Buffered(buffer_count=1)),
            block(width),
            pl.BlockSpec(memory_space=pl.ANY),
            pl.BlockSpec(sums[0].shape, lambda i: (0, 0, 0, 0)),
            *(whole(value.shape) for value in sums[1:]),
        ],
        out_specs=[block(width), whole(shape), whole(lines)],
        out_shape=[
            jax.ShapeDtypeStruct((rows, width), LOW),
            jax.ShapeDtypeStruct(shape, FULL),
            jax.ShapeDtypeStruct(lines, FULL),
        ],
        scratch_shapes=reduce_scratch([(shape[0] // 4, shape[1])] * 4, grid, hops)
        + [
            pltpu.VMEM((stages,) + lines, FULL),
            pltpu.VMEM((stages,) + lines, FULL),
            pltpu.SemaphoreType.DMA((stages,)),
            pltpu.SemaphoreType.DMA((stages,)),
        ],
        compiler_params=pltpu.CompilerParams(
            collective_id=3, has_side_effects=True, vmem_limit_bytes=56 * 2**20
        ),
        cost_estimate=pl.CostEstimate(
            flops=2 * rows * width * own.shape[1], bytes_accessed=8 * own.size, transcendentals=0
        ),
        name="end",
    )(own, matrix, first, total, *sums)


def attend_step(q_ref, k_ref, v_ref, ok_ref, ov_ref, mask_ref, out_ref, lse_ref, *, head, exact):
    rows = q_ref.shape[1]
    half = rows // 2
    heads = LANES // head
    scale = jnp.asarray(head**-0.5, LOW)
    queries = q_ref[0]
    own_keys = k_ref[0] * scale
    own_values = v_ref[0]
    keys = cat([own_keys[:half], ok_ref[0] * scale], axis=0)
    near = own_keys[half:]
    values_t = cat([own_values[:half], ov_ref[0]], axis=0).T
    near_values_t = own_values[half:].T
    lane = lax.broadcasted_iota(jnp.int32, (1, LANES), 1) // head
    spans = [(start, start + CLEN) for start in range(0, half, CLEN)]
    picked = lax.broadcasted_iota(jnp.int32, (8, LANES), 0) == lane
    chooser = jnp.where(picked, 1.0, 0.0).astype(LOW)

    def with_ones(value):
        return cat([value, jnp.ones((16, value.shape[1]), LOW)], axis=0)

    def squares(value):
        return nt(chooser, value * value)

    flags = []
    if not exact:
        largest = jnp.maximum(
            jnp.max(squares(keys), axis=1, keepdims=True),
            jnp.max(squares(near), axis=1, keepdims=True),
        )
        bound = jnp.sqrt(squares(queries) * largest) * LOG2E
    for part in range(2):
        span = slice(part * half, (part + 1) * half)
        query = queries[span]
        outs = []
        for h in range(heads):
            pick = lane == h
            lines = slice(h * head, (h + 1) * head)
            scores = nt(only(pick, keys), query)
            if part:
                near_keys = only(pick, near)
                local = cat([nt(near_keys[a:b], query[a:b]) for a, b in spans], axis=1)
                local = local + mask_ref[0]
            if exact:
                top = jnp.max(scores, axis=0, keepdims=True)
                if part:
                    top = jnp.maximum(top, jnp.max(local, axis=0, keepdims=True))
                top = top * LOG2E
            else:
                top = bound[h : h + 1, span]
            weights = jnp.exp2(scores * LOG2E - top).astype(LOW)
            mixed = nn(with_ones(values_t[lines]), weights)
            if part:
                weights = jnp.exp2(local * LOG2E - top).astype(LOW)
                value = with_ones(near_values_t[lines])
                mixed = mixed + cat([nn(value[:, a:b], weights[:, a:b]) for a, b in spans], axis=1)
            total = mixed[head : head + 1]
            fine = jnp.logical_and(total > 1e-25, total < 1e30)
            flags.append(jnp.where(fine, 0.0, 1.0))
            outs.append(mixed[:head] / total)
            lse_ref[0, 0, h : h + 1, span] = top + jnp.log2(total)
        out_ref[0, span] = cat(outs, axis=0).T.astype(LOW)
    return sum(flags[1:], flags[0])


def attend_again_kernel(*refs, head):
    attend_step(*refs, head=head, exact=True)


def attend_kernel(
    q_ref, k_ref, v_ref, ok_ref, ov_ref, mask_ref, out_block, up_block, down_block,
    out_ref, lse_ref, flag_ref, out_whole, up_whole, down_whole,
    sends, arrivals, placed, *held, head, grid,
):
    rows, columns = grid
    steps = pl.num_programs(1)
    step = pl.program_id(0) * steps + pl.program_id(1)
    final = 2 * steps - 1
    row_bits, col_bits = bits_of("row", rows), bits_of("col", columns)
    first_order = tuple(col_bits + row_bits[::-1])
    second_order = tuple(row_bits[:0:-1] + col_bits + row_bits[:1])
    per = len(spread(first_order))
    parts = [
        Gather(out_block, out_whole, first_order, sends, arrivals, 0),
        Gather(down_block, down_whole, first_order, sends, arrivals, per),
        Gather(up_block, up_whole, second_order, sends, arrivals, 2 * per),
    ]

    @pl.when(step == 0)
    def _():
        greet(row_bits + col_bits)
        for index in parts[0].first():
            for part in parts:
                part.copy(index).start()
        for number, part in enumerate(parts):
            part.loading(held[number], placed.at[number]).start()

    @pl.when(step == 1)
    def _():
        for number, part in enumerate(parts):
            part.loading(held[number], placed.at[number]).wait()
            part.placing(held[number], placed.at[number]).start()

    last = len(first_order) - 1
    events = {}
    for number, part in enumerate(parts):
        for index in part.later():
            stage, crossed = part.copies[index]
            if len(crossed) > 1 and number:
                when = final
            elif stage == last:
                when = (5, 10, 10)[number] + 2 * (len(crossed) > 1)
            else:
                when = (2, 6, 7)[number]
            events.setdefault(min(when, final), []).append((part, index))
    waited = set()
    for when in sorted(events):
        if when == final:
            continue

        @pl.when(step == when)
        def _(batch=events[when]):
            for part, index in batch:
                origin = part.source(index)
                if (part.base, origin) not in waited:
                    waited.add((part.base, origin))
                    part.arrival(origin).wait_recv()
                part.copy(index).start()

    flags = attend_step(
        q_ref, k_ref, v_ref, ok_ref, ov_ref, mask_ref, out_ref, lse_ref, head=head, exact=False
    )
    flag_ref[0, 0] = jnp.broadcast_to(flags, flag_ref.shape[2:])

    @pl.when(step == final)
    def _():
        for part, index in events.get(final, []):
            origin = part.source(index)
            if (part.base, origin) not in waited:
                waited.add((part.base, origin))
                part.arrival(origin).wait_recv()
            part.copy(index).start()
        for number, part in enumerate(parts):
            part.placing(held[number], placed.at[number]).wait()
            for index in range(per):
                if (part.base, index) not in waited:
                    part.arrival(index).wait_recv()
                part.copy(index).wait_send()


def attend_specs(own, other, mask):
    batch, rows, columns = own.shape
    steps = columns // (3 * LANES)

    def spec(count, offset):
        return pl.BlockSpec((1, count, LANES), lambda m, p: (m, 0, offset * steps + p))

    ins = [
        spec(rows, 0),
        spec(rows, 1),
        spec(rows, 2),
        spec(rows // 2, 0),
        spec(rows // 2, 1),
        pl.BlockSpec((1,) + mask.shape[1:], lambda m, p: (m, 0, 0)),
    ]
    return batch, rows, steps, spec, ins


def attend_again(own, other, mask, head):
    batch, rows, steps, spec, ins = attend_specs(own, other, mask)
    heads = LANES // head
    return pl.pallas_call(
        functools.partial(attend_again_kernel, head=head),
        grid=(batch, steps),
        in_specs=ins,
        out_specs=[spec(rows, 0), pl.BlockSpec((1, 1, heads, rows), lambda m, p: (m, p, 0, 0))],
        out_shape=[
            jax.ShapeDtypeStruct((batch, rows, steps * LANES), LOW),
            jax.ShapeDtypeStruct((batch, steps, heads, rows), FULL),
        ],
        name="attend_again",
    )(own, own, own, other, other, mask)


def attend(own, other, mask, blocks, grid, head):
    batch, rows, steps, spec, ins = attend_specs(own, other, mask)
    heads = LANES // head
    half = rows // 2
    anywhere = pl.BlockSpec(memory_space=pl.ANY)
    copies = 3 * (grid[0] * grid[1] - 1)
    work = batch * rows * (rows + CLEN) * steps * LANES
    wholes = [
        jax.ShapeDtypeStruct((block.shape[0] * grid[0], block.shape[1] * grid[1]), LOW)
        for block in blocks
    ]
    out, lse, flags, *wholes = pl.pallas_call(
        functools.partial(attend_kernel, head=head, grid=grid),
        grid=(batch, steps),
        in_specs=ins + [anywhere] * 3,
        out_specs=[
            spec(rows, 0),
            pl.BlockSpec((1, 1, heads, rows), lambda m, p: (m, p, 0, 0)),
            pl.BlockSpec((1, 1, 8, half), lambda m, p: (m, p, 0, 0)),
        ]
        + [anywhere] * 3,
        out_shape=[
            jax.ShapeDtypeStruct((batch, rows, steps * LANES), LOW),
            jax.ShapeDtypeStruct((batch, steps, heads, rows), FULL),
            jax.ShapeDtypeStruct((batch, steps, 8, half), FULL),
        ]
        + wholes,
        scratch_shapes=[
            pltpu.SemaphoreType.DMA((copies,)),
            pltpu.SemaphoreType.DMA((copies,)),
            pltpu.SemaphoreType.DMA((3, 2)),
        ]
        + [pltpu.VMEM(blocks[i].shape, LOW) for i in (0, 2, 1)],
        compiler_params=pltpu.CompilerParams(collective_id=1, has_side_effects=True),
        cost_estimate=pl.CostEstimate(
            flops=16 * work, bytes_accessed=own.size * 4, transcendentals=work // head
        ),
        name="attend",
    )(own, own, own, other, other, mask, *blocks)
    _, out, lse = lax.while_loop(
        lambda state: state[0] > 0.5,
        lambda state: (jnp.zeros((), FULL), *attend_again(own, other, mask, head)),
        (jnp.max(flags), out, lse),
    )
    return out, lse, wholes


def begin_kernel(tokens_ref, block_ref, other_ref, whole_ref, sends, arrivals, placed, held, *, grid):
    rows, columns = grid
    row_bits, col_bits = bits_of("row", rows), bits_of("col", columns)
    order = tuple(col_bits + row_bits[::-1])
    part = Gather(block_ref, whole_ref, order, sends, arrivals, 0)
    per = len(part.copies)
    exchange = pltpu.make_async_remote_copy(
        src_ref=tokens_ref.at[0, pl.ds(0, other_ref.shape[0])],
        dst_ref=other_ref,
        send_sem=sends.at[per],
        recv_sem=arrivals.at[per],
        device_id=flipped(here(("col",)), "col", 1),
        device_id_type=pl.DeviceIdType.MESH,
    )
    greet(row_bits + col_bits)
    for index in part.first():
        part.copy(index).start()
    exchange.start()
    part.loading(held, placed).start()
    part.loading(held, placed).wait()
    part.placing(held, placed).start()
    waited = set()
    for index in part.later():
        origin = part.source(index)
        if origin not in waited:
            waited.add(origin)
            part.arrival(origin).wait_recv()
        part.copy(index).start()
    for index in range(per):
        if index not in waited:
            part.arrival(index).wait_recv()
        part.copy(index).wait_send()
    part.placing(held, placed).wait()
    exchange.wait()


def begin(tokens, block, grid):
    batch, rows, width = tokens.shape
    copies = grid[0] * grid[1]
    anywhere = pl.BlockSpec(memory_space=pl.ANY)
    return pl.pallas_call(
        functools.partial(begin_kernel, grid=grid),
        in_specs=[anywhere] * 2,
        out_specs=[anywhere] * 2,
        out_shape=[
            jax.ShapeDtypeStruct((rows // 2, width), LOW),
            jax.ShapeDtypeStruct((block.shape[0] * grid[0], block.shape[1] * grid[1]), LOW),
        ],
        scratch_shapes=[
            pltpu.SemaphoreType.DMA((copies,)),
            pltpu.SemaphoreType.DMA((copies,)),
            pltpu.SemaphoreType.DMA((2,)),
            pltpu.VMEM(block.shape, LOW),
        ],
        compiler_params=pltpu.CompilerParams(collective_id=0, has_side_effects=True),
        cost_estimate=pl.CostEstimate(
            flops=0, bytes_accessed=block.size * copies * 16, transcendentals=0
        ),
        name="begin",
    )(tokens, block)


def attend_back_kernel(
    q_ref, k_ref, v_ref, ok_ref, ov_ref, mask_ref, out_ref, grad_ref, lse_ref,
    *rest, head, scale, grid, dp,
):
    if grid is not None:
        totals_in, matrices_in, rest = rest[:3], rest[3:5], rest[5:]
    own_grad_ref, other_grad_ref, sums_ref, *rest = rest
    if grid is not None:
        blocks_out, early_ref, rest = rest[:3], rest[3], rest[4:]
    own_scratch, other_scratch, stored, *scratch = rest
    rows = q_ref.shape[1]
    half = rows // 2
    heads = LANES // head
    steps = pl.num_programs(1)
    group, tile = pl.program_id(0), pl.program_id(1)
    step = group * steps + tile
    slot = step % 2

    def stores(group, tile, slot):
        copies = []
        for part in range(3):
            lanes = pl.ds(pl.multiple_of((part * steps + tile) * LANES, LANES), LANES)
            copies.append(
                pltpu.make_async_copy(
                    own_scratch.at[slot, part], own_grad_ref.at[group, :, lanes], stored.at[slot, part]
                )
            )
        for part in range(2):
            lanes = pl.ds(pl.multiple_of((part * steps + tile) * LANES, LANES), LANES)
            copies.append(
                pltpu.make_async_copy(
                    other_scratch.at[slot, part],
                    other_grad_ref.at[group, :, lanes],
                    stored.at[slot, 3 + part],
                )
            )
        return copies

    @pl.when(step >= 2)
    def _():
        for copy in stores((step - 2) // steps, (step - 2) % steps, slot):
            copy.wait()

    launches = {}
    if grid is not None:
        final = pl.num_programs(0) * steps - 1
        row_bits, col_bits = bits_of("row", grid[0]), bits_of("col", grid[1])
        across = across_bits("dp", dp)
        by_row = tuple(row_bits + col_bits[::-1])
        parts = []
        for number, hops in enumerate((tuple(across), tuple(across))):
            buffers, sends, arrivals = scratch[3 * number : 3 * number + 3]
            parts.append(Chain(totals_in[number], buffers, sends, arrivals, hops))
        acc, arrived, chain, sends, arrivals, loads = scratch[6:12]
        last = Reduce(
            totals_in[2], 0, acc, arrived, chain, sends, arrivals, loads, by_row, tuple(across)
        )
        last.size = blocks_out[2].shape[0]
        parts.append(last)

        @pl.when(step == 0)
        def _():
            greet_all(row_bits, col_bits, across)
            for part in parts[:2]:
                part.launch(0)
            last.begin(last.size)

        kept, sent, sent_sem, early_sem = scratch[12:]
        exchange = pltpu.make_async_remote_copy(
            src_ref=sent,
            dst_ref=early_ref,
            send_sem=sent_sem,
            recv_sem=early_sem,
            device_id=flipped(here(("col",)), "col", 1),
            device_id_type=pl.DeviceIdType.MESH,
        )

        @pl.when(step == steps)
        def _():
            width = kept.shape[1] // 2
            value = nt(kept[:, :width], matrices_in[0][...]) + nt(kept[:, width:], matrices_in[1][...])
            sent[...] = value.astype(LOW)
            exchange.start()

        for hop in range(1, len(across)):
            launches.setdefault(min(2 * hop, final), []).append((parts[0], hop))
            launches.setdefault(min(2 * hop + 2, final), []).append((parts[1], hop))
        for stage in range(1, last.stages()):
            when = min((0, 1, 3, 5, 9)[stage] if stage < 5 else final, final)
            launches.setdefault(when, []).append((last, stage))
        for when in sorted(launches):

            @pl.when(step == when)
            def _(batch=launches[when]):
                for part, stage in batch:
                    part.prepare(stage)

    own_keys = k_ref[0] * jnp.asarray(scale, LOW)
    own_values = v_ref[0]
    keys = cat([own_keys[:half], ok_ref[0] * jnp.asarray(scale, LOW)], axis=0)
    near = own_keys[half:]
    values = cat([own_values[:half], ov_ref[0]], axis=0)
    near_values = own_values[half:]
    keys_t = keys.T
    near_t = near.T
    lane = lax.broadcasted_iota(jnp.int32, (1, LANES), 1) // head
    spans = [(start, start + CLEN) for start in range(0, half, CLEN)]
    totals = [None, None, None, None]
    query_sums = []

    def add(place, value):
        totals[place] = value if totals[place] is None else totals[place] + value

    for part in range(2):
        span = slice(part * half, (part + 1) * half)
        query = q_ref[0, span]
        grad = grad_ref[0, span]
        dots = (grad.astype(FULL) * out_ref[0, span].astype(FULL)).T
        query_grads = []
        for h in range(heads):
            pick = lane == h
            lines = slice(h * head, (h + 1) * head)
            lse = lse_ref[0, 0, h : h + 1, span]
            delta = jnp.sum(dots[lines], axis=0, keepdims=True)
            query_h = only(pick, query)
            grad_h = only(pick, grad)
            probs = jnp.exp2(nt(only(pick, keys), query) * LOG2E - lse)
            slopes = (probs * (nt(only(pick, values), grad) - delta)).astype(LOW)
            probs = probs.astype(LOW)
            query_grad = nn(keys_t[lines], slopes)
            add(0, nn(slopes, query_h))
            add(1, nn(probs, grad_h))
            if part:
                near_h = only(pick, near)
                near_values_h = only(pick, near_values)
                local = cat([nt(near_h[a:b], query[a:b]) for a, b in spans], axis=1)
                dlocal = cat([nt(near_values_h[a:b], grad[a:b]) for a, b in spans], axis=1)
                probs = jnp.exp2((local + mask_ref[0]) * LOG2E - lse)
                slopes = (probs * (dlocal - delta)).astype(LOW)
                probs = probs.astype(LOW)
                query_grad = query_grad + cat(
                    [nn(near_t[lines, a:b], slopes[:, a:b]) for a, b in spans], axis=1
                )
                add(2, cat([nn(slopes[:, a:b], query_h[a:b]) for a, b in spans], axis=0))
                add(3, cat([nn(probs[:, a:b], grad_h[a:b]) for a, b in spans], axis=0))
            query_grads.append(query_grad)
        query_grad = cat(query_grads, axis=0).T
        query_sums.append(folded(query_grad))
        own_scratch[slot, 0, span] = query_grad.astype(LOW)
    key_grad = (totals[0] * scale).astype(LOW)
    value_grad = totals[1].astype(LOW)
    own_scratch[slot, 1, :half] = key_grad[:half]
    own_scratch[slot, 2, :half] = value_grad[:half]
    own_scratch[slot, 1, half:] = (totals[2] * scale).astype(LOW)
    own_scratch[slot, 2, half:] = totals[3].astype(LOW)
    other_scratch[slot, 0] = key_grad[half:]
    other_scratch[slot, 1] = value_grad[half:]
    if grid is not None:
        for part in range(2):
            lanes = pl.ds(pl.multiple_of((part * steps + tile) * LANES, LANES), LANES)
            kept[:, lanes] = other_scratch[slot, part]
    sums_ref[0, 0, 0:8] = query_sums[0] + query_sums[1]
    sums_ref[0, 0, 8:16] = folded(totals[1]) + folded(totals[3])
    for copy in stores(group, tile, slot):
        copy.start()
    for when in sorted(launches):

        @pl.when(step == when)
        def _(batch=launches[when]):
            for part, stage in batch:
                part.launch(stage)

    if grid is not None:

        @pl.when(step == final)
        def _():
            for part, block in zip(parts, blocks_out):
                part.finish(block)
            exchange.wait()

    @pl.when(step == pl.num_programs(0) * steps - 1)
    def _():
        for copy in stores((step - 1) // steps, (step - 1) % steps, 1 - slot):
            copy.wait()
        for copy in stores(group, tile, slot):
            copy.wait()


def attend_back(
    own, other, mask, out, grad, lse, head, sums=None, matrix=None, shapes=None, grid=None, dp=1
):
    batch, rows, steps, spec, ins = attend_specs(own, other, mask)
    work = batch * rows * (rows + CLEN) * steps * LANES
    anywhere = pl.BlockSpec(memory_space=pl.ANY)
    more_in, more_out, more_shapes, more_scratch, operands = [], [], [], [], []
    params = None
    if grid is not None:
        width = steps * LANES
        once = pl.Buffered(buffer_count=1)
        more_in = [pl.BlockSpec(shape, lambda m, p: (0, 0)) for shape in shapes[:2]] + [anywhere]
        more_in += [
            pl.BlockSpec((width, width), lambda m, p: (0, 1), pipeline_mode=once),
            pl.BlockSpec((width, width), lambda m, p: (0, 2), pipeline_mode=once),
        ]
        more_out = [pl.BlockSpec(shape, lambda m, p: (0, 0)) for shape in shapes] + [anywhere]
        more_shapes = [jax.ShapeDtypeStruct(shape, FULL) for shape in shapes]
        more_shapes += [jax.ShapeDtypeStruct((rows // 2, width), LOW)]
        hops = dp.bit_length() - 1
        more_scratch = chain_scratch(shapes[:2], hops) + reduce_scratch(shapes[2:], grid, hops)
        more_scratch += [
            pltpu.VMEM((rows // 2, 2 * width), LOW),
            pltpu.VMEM((rows // 2, width), LOW),
            pltpu.SemaphoreType.DMA,
            pltpu.SemaphoreType.DMA,
        ]
        operands = list(sums) + [matrix, matrix]
        params = pltpu.CompilerParams(
            collective_id=2, has_side_effects=True, vmem_limit_bytes=60 * 2**20
        )
    return pl.pallas_call(
        functools.partial(attend_back_kernel, head=head, scale=head**-0.5, grid=grid, dp=dp),
        grid=(batch, steps),
        in_specs=ins
        + [
            spec(rows, 0),
            spec(rows, 0),
            pl.BlockSpec((1, 1) + lse.shape[2:], lambda m, p: (m, p, 0, 0)),
        ]
        + more_in,
        out_specs=[anywhere] * 2
        + [pl.BlockSpec((1, 1, 16, LANES), lambda m, p: (m, p, 0, 0))]
        + more_out,
        out_shape=[
            jax.ShapeDtypeStruct(own.shape, LOW),
            jax.ShapeDtypeStruct(other.shape, LOW),
            jax.ShapeDtypeStruct((batch, steps, 16, LANES), FULL),
        ]
        + more_shapes,
        scratch_shapes=[
            pltpu.VMEM((2, 3, rows, LANES), LOW),
            pltpu.VMEM((2, 2, rows // 2, LANES), LOW),
            pltpu.SemaphoreType.DMA((2, 5)),
        ]
        + more_scratch,
        compiler_params=params,
        cost_estimate=pl.CostEstimate(
            flops=40 * work, bytes_accessed=own.size * 10, transcendentals=work // head
        ),
        name="attend_back",
    )(own, own, own, other, other, mask, out, grad, lse, *operands)


def swapped(value, axis, mask):
    pairs = [(source, source ^ mask) for source in range(lax.axis_size(axis))]
    return lax.ppermute(value, axis, pairs)


def masks_of(axis):
    return [1 << bit for bit in range(lax.axis_size(axis).bit_length() - 1)]


def bit_of(axis, mask):
    return jnp.where(lax.axis_index(axis) & mask == 0, 0, 1)


def joined(value, axis, mask, dim):
    other = swapped(value, axis, mask)
    first = bit_of(axis, mask) == 0
    return jnp.stack([jnp.where(first, value, other), jnp.where(first, other, value)], axis=dim)


def gathered(block):
    for mask in masks_of("col"):
        block = joined(block, "col", mask, 1).reshape(block.shape[0], -1)
    depth, columns = block.shape
    value = block[None]
    for mask in masks_of("row")[::-1]:
        value = joined(value, "row", mask, 1).reshape(-1, depth, columns)
    return value.reshape(-1, columns)


def parted(value, axis, mask, dim):
    bit = bit_of(axis, mask)
    keep = lax.dynamic_index_in_dim(value, bit, dim, keepdims=False)
    send = lax.dynamic_index_in_dim(value, 1 - bit, dim, keepdims=False)
    return keep + swapped(send.astype(LOW), axis, mask).astype(FULL)


def scattered(total, shape):
    value = total.reshape(-1, shape[0], total.shape[1])
    for mask in masks_of("row"):
        value = parted(value.reshape(-1, 2, *value.shape[1:]), "row", mask, 1)
    value = value.reshape(shape[0], -1)
    for mask in masks_of("col")[::-1]:
        value = parted(value.reshape(shape[0], 2, -1), "col", mask, 1)
    return over_dp(value)


def over_dp(value):
    for mask in masks_of("dp"):
        low = value.astype(LOW)
        value = low.astype(FULL) + swapped(low, "dp", 2 * mask - 1).astype(FULL)
    return value


def normalize(value):
    average = jnp.mean(value, axis=-1, keepdims=True)
    centred = value - average
    spread = jnp.mean(centred * centred, axis=-1, keepdims=True)
    inverse = lax.rsqrt(spread + EPSILON)
    return (centred * inverse, inverse)


def normalize_back(grad_normed, normed, inverse):
    first = jnp.mean(grad_normed, axis=-1, keepdims=True)
    second = jnp.mean(grad_normed * normed, axis=-1, keepdims=True)
    return inverse * (grad_normed - first - normed * second)


def near_mask(lengths, half):
    place = jnp.arange(CLEN, dtype=jnp.int32)[:, None]
    query = jnp.arange(half, dtype=jnp.int32)[None, :]
    limit = jnp.repeat(lengths, CLEN, axis=1)[:, None, :]
    seen = jnp.logical_and((place <= query % CLEN)[None], place[None] < limit)
    return jnp.where(seen, 0.0, -jnp.inf).astype(FULL)


def local(
    inputs,
    qkv_weight,
    out_weight,
    up_weight,
    down_weight,
    vectors,
    up_bias,
    cont_lengths,
    out_cotangent,
):
    grid_rows = lax.axis_size("row")
    grid_cols = lax.axis_size("col")
    place = lax.axis_index("col")
    side = place % 2
    batch, rows, width = inputs.shape
    half = rows // 2
    head = width // H
    half_conts = cont_lengths.shape[2] // 2
    group_lengths = lax.dynamic_index_in_dim(cont_lengths, place // 2, 1, keepdims=False)
    lengths = lax.dynamic_slice_in_dim(group_lengths, side * half_conts, half_conts, 1)
    mask = near_mask(lengths, half)

    grid = (grid_rows, grid_cols)
    direct = out_weight.shape[1] % LANES == 0 and qkv_weight.shape[1] % LANES == 0
    blocks = (out_weight, up_weight, down_weight)
    tokens = inputs.reshape(batch * rows, width)
    if direct:
        early, qkv_matrix = begin(inputs, qkv_weight, grid)
        late, qkv_matrix = lax.optimization_barrier((inputs[1:, :half], qkv_matrix))
        other_tokens = cat([early[None], swapped(late, "col", 1)], axis=0)
    else:
        other_tokens = swapped(inputs[:, :half], "col", 1)
        qkv_matrix = gathered(qkv_weight)
    other_tokens = other_tokens.reshape(batch * half, width)
    pair_matrix = qkv_matrix[:, width:]
    shift = cat([vectors[:, 0], jnp.zeros((width,), FULL), vectors[:, 1]])
    pair_shift = shift[width:]
    own = (nn(tokens, qkv_matrix) + shift).astype(LOW).reshape(batch, rows, 3 * width)
    other = (nn(other_tokens, pair_matrix) + pair_shift).astype(LOW)
    other = other.reshape(batch, half, 2 * width)
    if direct:
        attended, lse, (out_matrix, up_matrix, down_matrix) = attend(
            own, other, mask, blocks, grid, head
        )
    else:
        attended, lse = attend_again(own, other, mask, head)
        out_matrix, up_matrix, down_matrix = (gathered(block) for block in blocks)
    attended = attended.reshape(batch * rows, width)
    first_sum = tokens.astype(FULL) + nn(attended, out_matrix) + vectors[:, 2]
    first_normed, first_inverse = normalize(first_sum)
    hidden = first_normed * vectors[:, 3] + vectors[:, 4]
    hidden_low = hidden.astype(LOW)
    pre_act = nn(hidden_low, up_matrix) + up_bias
    phi = 0.5 + 0.5 * lax.erf(pre_act * (0.5**0.5))
    slope = phi + pre_act * (jnp.exp(-0.5 * pre_act * pre_act) * ((2 * math.pi) ** -0.5))
    act_low = (pre_act * phi).astype(LOW)
    slope_low = slope.astype(LOW)
    second_sum = hidden + nn(act_low, down_matrix) + vectors[:, 5]
    second_normed, second_inverse = normalize(second_sum)
    result = (second_normed * vectors[:, 6] + vectors[:, 7]).astype(LOW)

    grad_out = out_cotangent.reshape(batch * rows, width).astype(FULL)
    grad_second = normalize_back(grad_out * vectors[:, 6], second_normed, second_inverse)
    grad_second_low = grad_second.astype(LOW)
    shapes = (down_weight.shape, up_weight.shape, out_weight.shape)
    down_total = tn(act_low, grad_second_low)
    if direct:
        grad_pre_low, up_total, bias_sums, down_block = widen(
            grad_second_low, hidden_low, down_matrix, slope_low, down_total.astype(LOW), shapes[0], grid
        )
        grad_first, grad_attended, out_total, norm_sums, up_block = narrow(
            grad_pre_low, grad_second_low, first_normed.astype(LOW), first_inverse, attended,
            up_matrix, out_matrix, vectors[:, 3][None], up_total, shapes[1], grid,
        )
        totals = [down_block, up_block, out_total]
    else:
        grad_pre = nt(grad_second_low, down_matrix) * slope_low.astype(FULL)
        grad_pre_low = grad_pre.astype(LOW)
        grad_hidden = grad_second + nt(grad_pre_low, up_matrix)
        grad_first = normalize_back(grad_hidden * vectors[:, 3], first_normed, first_inverse)
        grad_first_low = grad_first.astype(LOW)
        grad_attended = nt(grad_first_low, out_matrix).astype(LOW)
        totals = (down_total, tn(hidden_low, grad_pre_low), tn(attended, grad_first_low))
        first_sums = [
            jnp.sum(grad_first, axis=0),
            jnp.sum(grad_hidden * first_normed, axis=0),
            jnp.sum(grad_hidden, axis=0),
        ]
        bias_sum = jnp.sum(grad_pre, axis=0)
    operands = (
        own,
        other,
        mask,
        attended.reshape(batch, rows, width),
        grad_attended.reshape(batch, rows, width),
        lse,
        head,
    )
    if direct:
        own_grad, other_grad, pair_sums, down_grad, up_grad, out_grad, received = attend_back(
            *operands, totals, qkv_matrix, shapes, grid, lax.axis_size("dp")
        )
        sent = nt(other_grad[1:].reshape(-1, 2 * width), pair_matrix).astype(LOW)
        sent, own_grad = lax.optimization_barrier((sent, own_grad))
        late = swapped(sent.reshape(batch - 1, half, width), "col", 1)
        received = cat([received[None], late], axis=0)
        own_grad = own_grad.reshape(batch * rows, 3 * width)
        other_grad = other_grad.reshape(batch * half, 2 * width)
    else:
        own_grad, other_grad, pair_sums = attend_back(*operands)
        down_grad, up_grad, out_grad = (
            scattered(total, shape) for total, shape in zip(totals, shapes)
        )
        own_grad = own_grad.reshape(batch * rows, 3 * width)
        other_grad = other_grad.reshape(batch * half, 2 * width)
        sent = nt(other_grad, pair_matrix).astype(LOW).reshape(batch, half, width)
        received = swapped(sent, "col", 1).astype(FULL)
        grad_tokens = (grad_first + nt(own_grad, qkv_matrix)).reshape(batch, rows, width)
        grad_tokens = cat([grad_tokens[:, :half] + received, grad_tokens[:, half:]], axis=1)
        grad_tokens = grad_tokens.astype(LOW)
    qkv_total = tn(tokens, own_grad)
    pair_total = tn(other_tokens, other_grad)
    qkv_total = cat([qkv_total[:, :width], qkv_total[:, width:] + pair_total], axis=1)
    last_sums = [
        jnp.sum(grad_second, axis=0),
        jnp.sum(grad_out * second_normed, axis=0),
        jnp.sum(grad_out, axis=0),
    ]
    if direct:
        grad_tokens, qkv_grad, sums = end(
            own_grad, qkv_matrix, grad_first, qkv_total.astype(LOW),
            (pair_sums, norm_sums, bias_sums, jnp.stack(last_sums)),
            qkv_weight.shape, grid, lax.axis_size("dp"),
        )
        received = jnp.pad(received, ((0, 0), (0, rows - half), (0, 0))).astype(FULL)
        grad_tokens = (grad_tokens.reshape(batch, rows, width).astype(FULL) + received).astype(LOW)
        sums = sums.reshape(-1)[: 8 * width + up_bias.shape[0]]
    else:
        qkv_grad = scattered(qkv_total, qkv_weight.shape)
        pair_sums = jnp.sum(pair_sums, axis=0)
        pair_sums = [jnp.sum(pair_sums[:, i : i + 8], axis=1).reshape(width) for i in (0, 8)]
        sums = lax.psum(cat([*pair_sums, *first_sums, *last_sums, bias_sum]), ("dp", "row", "col"))
    index = lax.axis_index("row") * grid_cols + place
    devices = grid_rows * grid_cols
    split = sums[: 8 * width].reshape(8, width)
    vector_grad = lax.dynamic_slice_in_dim(split, index * (width // devices), width // devices, 1).T
    bias = sums[8 * width :]
    count = bias.shape[0] // devices
    bias_grad = lax.dynamic_slice_in_dim(bias, index * count, count, 0)
    return (
        result.reshape(batch, rows, width),
        grad_tokens,
        qkv_grad,
        out_grad,
        up_grad,
        down_grad,
        vector_grad,
        bias_grad,
    )


def solution(mesh):
    everywhere = ("dp", "row", "col")
    tokens = P(None, everywhere, None)
    matrix = P("row", "col")
    return jax.shard_map(
        local,
        mesh=mesh,
        in_specs=(
            tokens, matrix, matrix, matrix, matrix, P(), P(), P(None, ("dp", "row"), None), tokens,
        ),
        out_specs=(
            tokens, tokens, matrix, matrix, matrix, matrix, P(("row", "col"), None), P(("row", "col")),
        ),
        check_vma=False,
    )
```

```python
import functools
import math

import jax
import jax.numpy as jnp
from jax import lax
from jax.experimental import pallas as pl
from jax.experimental.pallas import tpu as pltpu
from jax.sharding import PartitionSpec as P

H = 12
CLEN = 128
LANES = 128
EPSILON = 1e-05
LOG2E = math.log2(math.e)
LOW = jnp.bfloat16
FULL = jnp.float32
cat = jnp.concatenate


def nt(left, right):
    return lax.dot_general(left, right, (((1,), (1,)), ((), ())), preferred_element_type=FULL)


def nn(left, right):
    return lax.dot_general(left, right, (((1,), (0,)), ((), ())), preferred_element_type=FULL)


def tn(left, right):
    return lax.dot_general(left, right, (((0,), (0,)), ((), ())), preferred_element_type=FULL)


def folded(value):
    return jnp.sum(value.reshape(-1, 8, value.shape[1]), axis=0)


def only(pick, value):
    return jnp.where(pick, value, jnp.zeros_like(value))


def spread(order):
    listed = []
    for stage in range(len(order)):
        for code in range(1 << stage):
            listed.append((stage, tuple(order[i] for i in range(stage) if code >> i & 1)))
    return listed


def flipped(position, axis, mask):
    bit = position[axis] // mask % 2
    return {**position, axis: position[axis] + mask * (1 - 2 * bit)}


def place_of(position, crossed):
    for axis, mask in crossed:
        position = flipped(position, axis, mask)
    return position


def here(axes):
    return {axis: lax.axis_index(axis) for axis in axes}


def bits_of(axis, size):
    return [(axis, 1 << bit) for bit in range(size.bit_length() - 1)]


def greet(partners):
    barrier = pltpu.get_barrier_semaphore()
    for axis, mask in partners:
        target = flipped(here((axis,)), axis, mask)
        pl.semaphore_signal(barrier, inc=1, device_id=target, device_id_type=pl.DeviceIdType.MESH)
    pl.semaphore_wait(barrier, len(partners))


class Gather:
    def __init__(self, own, whole, order, sends, arrivals, base, rows=None, moved=None):
        self.own, self.whole, self.order = own, whole, order
        self.sends, self.arrivals, self.base = sends, arrivals, base
        self.low, self.count = rows if rows else (0, own.shape[0])
        self.copies = spread(order)
        self.position = here(("row", "col"))
        self.bit, self.moved = moved if moved else (None, None)

    def slot(self, position):
        depth, columns = self.own.shape
        first = pl.multiple_of(position["row"] * depth + self.low, 16)
        start = pl.multiple_of(position["col"] * columns, LANES)
        return self.whole.at[pl.ds(first, self.count), pl.ds(start, columns)]

    def origin(self, crossed):
        if not crossed:
            return self.own.at[pl.ds(self.low, self.count)]
        return self.moved if crossed == (self.bit,) else self.slot(place_of(self.position, crossed))

    def remote(self, index, source, slot):
        axis, mask = self.order[self.copies[index][0]]
        return pltpu.make_async_remote_copy(
            src_ref=source,
            dst_ref=slot,
            send_sem=self.sends.at[self.base + index],
            recv_sem=self.arrivals.at[self.base + index],
            device_id=flipped(here((axis,)), axis, mask),
            device_id_type=pl.DeviceIdType.MESH,
        )

    def copy(self, index):
        crossed = self.copies[index][1]
        return self.remote(index, self.origin(crossed), self.slot(place_of(self.position, crossed)))

    def arrival(self, index):
        stage, crossed = self.copies[index]
        slot = self.slot(place_of(self.position, crossed + (self.order[stage],)))
        return self.remote(index, slot, slot)

    def placed(self):
        pairs = [(self.origin(()), self.slot(self.position))]
        if self.bit:
            pairs.append((self.moved, self.slot(place_of(self.position, (self.bit,)))))
        return pairs

    def source(self, index):
        crossed = self.copies[index][1]
        last = self.order.index(crossed[-1])
        found = self.copies.index((last, crossed[:-1]))
        return found if self.sent(found) else None

    def sent(self, index):
        stage, crossed = self.copies[index]
        return bool(crossed) or self.order[stage] != self.bit

    def first(self):
        return [i for i, (stage, crossed) in enumerate(self.copies) if not crossed and self.sent(i)]

    def later(self):
        return [i for i, (stage, crossed) in enumerate(self.copies) if crossed]

    def used(self):
        return [i for i in range(len(self.copies)) if self.sent(i)]


class Reduce:
    def __init__(self, total, low, acc, arrived, chain, sends, arrivals, loads, order, across):
        self.total, self.low, self.acc, self.arrived, self.chain = total, low, acc, arrived, chain
        self.sends, self.arrivals, self.loads = sends, arrivals, loads
        self.order, self.across = order, across
        self.position = here(("row", "col"))
        self.settled = set()

    def slot(self, crossed, size):
        position = place_of(self.position, crossed)
        depth, columns = self.acc.shape[1:]
        first = pl.multiple_of(position["row"] * size + self.low, 16)
        start = pl.multiple_of(position["col"] * columns, LANES)
        return self.total.at[pl.ds(first, depth), pl.ds(start, columns)]

    def crossed(self, code):
        return tuple(bit for i, bit in enumerate(self.order[1:]) if code >> i & 1)

    def number(self, stage, code):
        count = len(self.order)
        return sum(1 << (count - 1 - s) for s in range(stage)) + code

    def copy(self, stage, code, source):
        axis, mask = self.order[stage]
        number = self.number(stage, code)
        return pltpu.make_async_remote_copy(
            src_ref=source,
            dst_ref=self.arrived.at[number],
            send_sem=self.sends.at[number],
            recv_sem=self.arrivals.at[number],
            device_id=flipped(here((axis,)), axis, mask),
            device_id_type=pl.DeviceIdType.MESH,
        )

    def load(self, code, size):
        return pltpu.make_async_copy(
            self.slot(self.crossed(code), size), self.acc.at[code], self.loads.at[code]
        )

    def outgoing(self, stage, code, size):
        if stage == 0:
            return self.copy(0, code, self.slot((self.order[0],) + self.crossed(code), size))
        return self.copy(stage, code, self.acc.at[code << stage | 1 << (stage - 1)])

    def begin(self, size):
        self.size = size
        for code in range(1 << (len(self.order) - 1))[::-1]:
            self.outgoing(0, code, size).start()
        for code in range(1 << (len(self.order) - 1))[::-1]:
            self.load(code, size).start()

    def settle(self, stage, code):
        if (stage, code) in self.settled:
            return
        self.settled.add((stage, code))
        entry = code << stage
        if stage == 0:
            self.load(code, self.size).wait()
        else:
            self.settle(stage - 1, 2 * code)
        self.outgoing(stage, code, self.size).wait_recv()
        number = self.number(stage, code)
        value = self.acc[entry].astype(FULL) + self.arrived[number].astype(FULL)
        self.acc[entry] = value.astype(LOW)

    def codes(self, stage):
        return range(1 << (len(self.order) - 1 - stage))[::-1]

    def prepare(self, stage):
        count = len(self.order)
        if stage < count:
            for code in self.codes(stage):
                self.settle(stage - 1, 2 * code + 1)
        elif stage == count:
            self.settle(count - 1, 0)
        else:
            hop = stage - count - 1
            self.hop(hop).wait_recv()
            before = self.acc[0] if hop == 0 else self.chain[len(self.across) + hop - 1]
            value = before.astype(FULL) + self.chain[hop].astype(FULL)
            self.chain[len(self.across) + hop] = value.astype(LOW)

    def hop(self, hop):
        axis, mask = self.across[hop]
        number = (1 << len(self.order)) - 1 + hop
        target = self.target(axis, mask)
        source = self.acc.at[0] if hop == 0 else self.chain.at[len(self.across) + hop - 1]
        return pltpu.make_async_remote_copy(
            src_ref=source,
            dst_ref=self.chain.at[hop],
            send_sem=self.sends.at[number],
            recv_sem=self.arrivals.at[number],
            device_id=target,
            device_id_type=pl.DeviceIdType.MESH,
        )

    @staticmethod
    def target(axis, mask):
        return across_target(axis, mask)

    def launch(self, stage):
        if stage < len(self.order):
            for code in self.codes(stage):
                self.outgoing(stage, code, self.size).start()
        else:
            self.hop(stage - len(self.order)).start()

    def stages(self):
        return len(self.order) + len(self.across)

    def close(self, out):
        self.settle(len(self.order) - 1, 0)
        out[...] = self.acc[0]
        self.sent()

    def sent(self):
        for stage in range(len(self.order)):
            for code in self.codes(stage):
                self.outgoing(stage, code, self.size).wait_send()

    def finish(self, out):
        hops = len(self.across)
        self.hop(hops - 1).wait_recv()
        before = self.acc[0] if hops == 1 else self.chain[2 * hops - 2]
        out[...] = before.astype(FULL) + self.chain[hops - 1].astype(FULL)
        self.sent()
        for hop in range(hops):
            self.hop(hop).wait_send()


def across_target(axis, mask):
    index = lax.axis_index(axis)
    return {axis: index // (mask + 1) * (mask + 1) + mask - index % (mask + 1)}


def across_bits(axis, size):
    return [(axis, (2 << bit) - 1) for bit in range(size.bit_length() - 1)]


class Chain:
    def __init__(self, start, buffers, sends, arrivals, across):
        self.start, self.buffers, self.across = start, buffers, across
        self.sends, self.arrivals = sends, arrivals

    def before(self, hop):
        return self.start if hop == 0 else self.buffers.at[len(self.across) + hop - 1]

    def hop(self, hop):
        axis, mask = self.across[hop]
        return pltpu.make_async_remote_copy(
            src_ref=self.before(hop),
            dst_ref=self.buffers.at[hop],
            send_sem=self.sends.at[hop],
            recv_sem=self.arrivals.at[hop],
            device_id=across_target(axis, mask),
            device_id_type=pl.DeviceIdType.MESH,
        )

    def total(self, hop):
        self.hop(hop).wait_recv()
        return self.before(hop)[...].astype(FULL) + self.buffers[hop].astype(FULL)

    def prepare(self, hop):
        self.buffers[len(self.across) + hop - 1] = self.total(hop - 1).astype(LOW)

    def launch(self, hop):
        self.hop(hop).start()

    def finish(self, out):
        out[...] = self.total(len(self.across) - 1)
        for hop in range(len(self.across)):
            self.hop(hop).wait_send()


def chain_scratch(blocks, hops):
    shapes = []
    for depth, columns in blocks:
        shapes += [
            pltpu.VMEM((2 * hops, depth, columns), LOW),
            pltpu.SemaphoreType.DMA((hops,)),
            pltpu.SemaphoreType.DMA((hops,)),
        ]
    return shapes


def halve_scratch(shape, grid):
    count = grid[0] * grid[1]
    depth, columns = shape
    return [
        pltpu.VMEM((count // 2, depth // 2, columns), LOW),
        pltpu.VMEM((count - 1, depth // 2, columns), LOW),
        pltpu.SemaphoreType.DMA((count - 1,)),
        pltpu.SemaphoreType.DMA((count - 1,)),
        pltpu.SemaphoreType.DMA((count // 2,)),
    ] * 2


class Halving:
    def __init__(self, total, out, scratch, grid, whens):
        self.row_bits, self.col_bits = bits_of("row", grid[0]), bits_of("col", grid[1])
        self.out, self.whens = out, whens
        self.depth = out.shape[0]
        first, later = tuple(self.row_bits[:1]), tuple(self.row_bits[1:])
        orders = [first + later + tuple(self.col_bits[::-1]), first + tuple(self.col_bits[::-1]) + later]
        self.parts = []
        for number, order in enumerate(orders):
            acc, arrived, sends, arrivals, loads = scratch[5 * number : 5 * number + 5]
            low = number * self.depth // 2
            self.parts.append(
                Reduce(total, low, acc, arrived, None, sends, arrivals, loads, order, ())
            )

    def before(self, step):
        @pl.when(step == 0)
        def _():
            greet(self.row_bits + self.col_bits)
            for part in self.parts:
                part.begin(self.depth)

        for part in self.parts:
            part.size = self.depth
        for stage in range(1, self.parts[0].stages()):

            @pl.when(step == self.whens[stage])
            def _(stage=stage):
                for part in self.parts:
                    part.prepare(stage)
                    part.launch(stage)

    def after(self, step, final):
        @pl.when(step == final)
        def _():
            half = self.depth // 2
            for number, part in enumerate(self.parts):
                part.close(self.out.at[pl.ds(number * half, half)])


def widen_kernel(
    second_ref, hidden_ref, down_ref, slope_ref, total_ref,
    grad_ref, up_ref, sums_ref, block_ref, turned, *scratch, grid, whens, chunk,
):
    step = pl.program_id(0)
    carried = Halving(total_ref, block_ref, scratch, grid, whens)
    carried.before(step)

    @pl.when(step == 0)
    def _():
        turned[...] = hidden_ref[...].T

    rows = grad_ref.shape[0]

    def part(index, total):
        span = pl.ds(pl.multiple_of(index * chunk, chunk), chunk)
        grad = nt(second_ref[span], down_ref[...]) * slope_ref[span].astype(FULL)
        grad_ref[span] = grad.astype(LOW)
        return total + jnp.sum(grad.reshape(chunk // 8, 8, grad.shape[1]), axis=0)

    sums_ref[...] = lax.fori_loop(0, rows // chunk, part, jnp.zeros(sums_ref.shape, FULL))
    up_ref[...] = nn(turned[...], grad_ref[...]).astype(LOW)
    carried.after(step, pl.num_programs(0) - 1)


def widen(second, hidden, down_matrix, slope, down_total, shape, grid):
    rows, width = second.shape
    hidden_units = down_matrix.shape[0]
    tile = 512
    steps = hidden_units // tile
    once = pl.Buffered(buffer_count=1)
    return pl.pallas_call(
        functools.partial(widen_kernel, grid=grid, whens=(0, 1, 4), chunk=min(rows, 1024)),
        grid=(steps,),
        in_specs=[
            pl.BlockSpec((rows, width), lambda i: (0, 0), pipeline_mode=once),
            pl.BlockSpec((rows, width), lambda i: (0, 0), pipeline_mode=once),
            pl.BlockSpec((tile, width), lambda i: (i, 0)),
            pl.BlockSpec((rows, tile), lambda i: (0, i)),
            pl.BlockSpec(memory_space=pl.ANY),
        ],
        out_specs=[
            pl.BlockSpec((rows, tile), lambda i: (0, i)),
            pl.BlockSpec((width, tile), lambda i: (0, i)),
            pl.BlockSpec((8, tile), lambda i: (0, i)),
            pl.BlockSpec(shape, lambda i: (0, 0)),
        ],
        out_shape=[
            jax.ShapeDtypeStruct((rows, hidden_units), LOW),
            jax.ShapeDtypeStruct((width, hidden_units), LOW),
            jax.ShapeDtypeStruct((8, hidden_units), FULL),
            jax.ShapeDtypeStruct(shape, LOW),
        ],
        scratch_shapes=[pltpu.VMEM((width, rows), LOW)] + halve_scratch(shape, grid),
        compiler_params=pltpu.CompilerParams(
            collective_id=4, has_side_effects=True, vmem_limit_bytes=56 * 2**20
        ),
        cost_estimate=pl.CostEstimate(
            flops=4 * rows * width * hidden_units, bytes_accessed=6 * rows * hidden_units, transcendentals=0
        ),
        name="widen",
    )(second, hidden, down_matrix, slope, down_total)


def narrow_kernel(
    grad_ref, second_ref, normed_ref, inverse_ref, attended_ref, up_ref, out_ref, gain_ref, total_ref,
    first_ref, back_ref, out_total_ref, sums_ref, block_ref, held, *scratch, grid, whens,
):
    step = pl.program_id(0)
    final = pl.num_programs(0) - 1
    carried = Halving(total_ref, block_ref, scratch, grid, whens)
    carried.before(step)

    @pl.when(step == 0)
    def _():
        held[...] = jnp.zeros(held.shape, FULL)
        sums_ref[...] = jnp.zeros(sums_ref.shape, FULL)

    grad_hidden = nt(grad_ref[...], up_ref[...]) + second_ref[...].astype(FULL)
    normed = normed_ref[...].astype(FULL)
    grad_first = normalize_back(grad_hidden * gain_ref[...], normed, inverse_ref[...])
    low = grad_first.astype(LOW)
    first_ref[...] = low
    back_ref[...] = nt(low, out_ref[...]).astype(LOW)
    held[...] += tn(attended_ref[...], low)

    sums_ref[0:8] += folded(grad_first)
    sums_ref[8:16] += folded(grad_hidden * normed)
    sums_ref[16:24] += folded(grad_hidden)
    carried.after(step, final)

    @pl.when(step == final)
    def _():
        out_total_ref[...] = held[...].astype(LOW)


def narrow(grad, second, normed, inverse, attended, up_matrix, out_matrix, gain, up_total, shape, grid):
    rows, width = second.shape
    hidden_units = grad.shape[1]
    tile = 256
    once = pl.Buffered(buffer_count=1)

    def block(columns):
        return pl.BlockSpec((tile, columns), lambda i: (i, 0))

    def whole(shape, **more):
        return pl.BlockSpec(shape, lambda i: (0, 0), **more)

    return pl.pallas_call(
        functools.partial(narrow_kernel, grid=grid, whens=(0, 1, 5)),
        grid=(rows // tile,),
        in_specs=[
            block(hidden_units),
            block(width),
            block(width),
            block(1),
            block(width),
            whole(up_matrix.shape, pipeline_mode=once),
            whole(out_matrix.shape, pipeline_mode=once),
            whole(gain.shape),
            pl.BlockSpec(memory_space=pl.ANY),
        ],
        out_specs=[
            block(width), block(width), whole(out_matrix.shape), whole((24, width)), whole(shape),
        ],
        out_shape=[
            jax.ShapeDtypeStruct((rows, width), LOW),
            jax.ShapeDtypeStruct((rows, width), LOW),
            jax.ShapeDtypeStruct(out_matrix.shape, LOW),
            jax.ShapeDtypeStruct((24, width), FULL),
            jax.ShapeDtypeStruct(shape, LOW),
        ],
        scratch_shapes=[pltpu.VMEM(out_matrix.shape, FULL)] + halve_scratch(shape, grid),
        compiler_params=pltpu.CompilerParams(
            collective_id=5, has_side_effects=True, vmem_limit_bytes=56 * 2**20
        ),
        cost_estimate=pl.CostEstimate(
            flops=2 * rows * width * (hidden_units + 2 * width),
            bytes_accessed=2 * rows * hidden_units,
            transcendentals=0,
        ),
        name="narrow",
    )(grad, second, normed, inverse, attended, up_matrix, out_matrix, gain, up_total)


def reduce_scratch(blocks, grid, hops):
    count = grid[0] * grid[1]
    shapes = []
    for depth, columns in blocks:
        shapes += [
            pltpu.VMEM((count // 2, depth, columns), LOW),
            pltpu.VMEM((count - 1, depth, columns), LOW),
            pltpu.VMEM((2 * hops, depth, columns), LOW),
            pltpu.SemaphoreType.DMA((count - 1 + hops,)),
            pltpu.SemaphoreType.DMA((count - 1 + hops,)),
            pltpu.SemaphoreType.DMA((count // 2,)),
        ]
    return shapes


def greet_all(row_bits, col_bits, across):
    barrier = pltpu.get_barrier_semaphore()
    targets = [flipped(here((axis,)), axis, mask) for axis, mask in row_bits + col_bits]
    targets += [across_target(axis, mask) for axis, mask in across]
    for target in targets:
        pl.semaphore_signal(barrier, inc=1, device_id=target, device_id_type=pl.DeviceIdType.MESH)
    pl.semaphore_wait(barrier, len(targets))


def end_kernel(
    own_ref, matrix_ref, first_ref, total_ref, sent_ref, pair_ref, norm_ref, bias_ref, last_ref,
    tokens_ref, out_ref, all_ref, came_ref, *scratch, grid, dp,
):
    step = pl.program_id(0)
    final = pl.num_programs(0) - 1
    rows, columns = grid
    row_bits, col_bits = bits_of("row", rows), bits_of("col", columns)
    across = across_bits("dp", dp)
    first, later = tuple(row_bits[:1]), tuple(row_bits[1:])
    orders = [first + later + tuple(col_bits[::-1]), first + tuple(col_bits[::-1]) + later]
    depth = out_ref.shape[0]
    part_depth = depth // 4
    parts = []
    for number in range(4):
        acc, arrived, chain, sends, arrivals, loads = scratch[6 * number : 6 * number + 6]
        part = Reduce(
            total_ref, number * part_depth, acc, arrived, chain, sends, arrivals, loads,
            orders[number % 2], tuple(across),
        )
        part.size = depth
        parts.append(part)
    running, came, small_sends, small_arrivals, sent_sem, came_sem = scratch[24:]
    exchange = pltpu.make_async_remote_copy(
        src_ref=sent_ref,
        dst_ref=came_ref,
        send_sem=sent_sem,
        recv_sem=came_sem,
        device_id=flipped(here(("col",)), "col", 1),
        device_id_type=pl.DeviceIdType.MESH,
    )
    targets = [flipped(here((axis,)), axis, mask) for axis, mask in row_bits + col_bits]
    targets += [across_target(axis, mask) for axis, mask in across]

    def small(stage):
        return pltpu.make_async_remote_copy(
            src_ref=running.at[stage],
            dst_ref=came.at[stage],
            send_sem=small_sends.at[stage],
            recv_sem=small_arrivals.at[stage],
            device_id=targets[stage],
            device_id_type=pl.DeviceIdType.MESH,
        )

    stages = len(targets)
    events = []
    for number, part in enumerate(parts):
        for stage in range(1, stages):
            late = 0 if number < 2 else (1.1 if stage == 1 else 2.1)
            events.append((stage + late, number, stage))
    whens = {1: 2, 2: 5, 3: 5}
    batches = {}
    for key, number, stage in sorted(events):
        batches.setdefault(min(whens.get(int(key), final), final), []).append((number, stage))

    def advance(batch):
        for number, stage in batch:
            parts[number].prepare(stage)
            parts[number].launch(stage)
            if number == 3 and stage == len(orders[0]) - 1:
                exchange.start()
            if number == 1:
                small(stage - 1).wait_recv()
                running[stage] = running[stage - 1] + came[stage - 1]
                small(stage).start()

    @pl.when(step == 0)
    def _():
        greet_all(row_bits, col_bits, across)
        for part in parts:
            part.begin(depth)
        running[0] = jnp.zeros(running.shape[1:], FULL)

        def column_sums(value):
            return jnp.sum(value, axis=0, keepdims=True)

        width = running.shape[2]
        tiles = pair_ref.shape[1]
        for kind in range(2):
            lines = slice(8 * kind, 8 * kind + 8)
            for tile in range(tiles):
                value = sum(pair_ref[m, tile, lines] for m in range(pair_ref.shape[0]))
                running[0, kind : kind + 1, tile * LANES : (tile + 1) * LANES] = column_sums(value)
        for number in range(3):
            running[0, 2 + number : 3 + number] = column_sums(norm_ref[8 * number : 8 * number + 8])
            running[0, 5 + number : 6 + number] = last_ref[number : number + 1]
        for number in range(bias_ref.shape[1] // width):
            value = bias_ref[:, number * width : (number + 1) * width]
            running[0, 8 + number : 9 + number] = column_sums(value)
        small(0).start()

    for when in sorted(batches):
        if when < final:
            pl.when(step == when)(functools.partial(advance, batches[when]))

    grad = nt(own_ref[...], matrix_ref[...]) + first_ref[...].astype(FULL)
    tokens_ref[...] = grad.astype(LOW)

    @pl.when(step == final)
    def _():
        advance(batches.get(final, []))
        for number, part in enumerate(parts):
            part.finish(out_ref.at[pl.ds(number * part_depth, part_depth)])
        small(stages - 1).wait_recv()
        all_ref[...] = running[stages - 1] + came[stages - 1]
        for stage in range(stages):
            small(stage).wait_send()
        exchange.wait()


def end(own, matrix, first, total, sent, sums, shape, grid, dp):
    lines = 8 + sums[2].shape[1] // first.shape[1]
    lines = (lines + -lines % 8, first.shape[1])
    hops = dp.bit_length() - 1
    stages = (grid[0] * grid[1] * dp).bit_length() - 1
    rows, width = first.shape
    tile = 256

    def block(columns):
        return pl.BlockSpec((tile, columns), lambda i: (i, 0))

    def whole(shape, **more):
        return pl.BlockSpec(shape, lambda i: (0, 0), **more)

    return pl.pallas_call(
        functools.partial(end_kernel, grid=grid, dp=dp),
        grid=(rows // tile,),
        in_specs=[
            block(own.shape[1]),
            whole(matrix.shape, pipeline_mode=pl.Buffered(buffer_count=1)),
            block(width),
            pl.BlockSpec(memory_space=pl.ANY),
            pl.BlockSpec(memory_space=pl.ANY),
            pl.BlockSpec(sums[0].shape, lambda i: (0, 0, 0, 0)),
            *(whole(value.shape) for value in sums[1:]),
        ],
        out_specs=[block(width), whole(shape), whole(lines), pl.BlockSpec(memory_space=pl.ANY)],
        out_shape=[
            jax.ShapeDtypeStruct((rows, width), LOW),
            jax.ShapeDtypeStruct(shape, FULL),
            jax.ShapeDtypeStruct(lines, FULL),
            jax.ShapeDtypeStruct(sent.shape, LOW),
        ],
        scratch_shapes=reduce_scratch([(shape[0] // 4, shape[1])] * 4, grid, hops)
        + [
            pltpu.VMEM((stages,) + lines, FULL),
            pltpu.VMEM((stages,) + lines, FULL),
            pltpu.SemaphoreType.DMA((stages,)),
            pltpu.SemaphoreType.DMA((stages,)),
            pltpu.SemaphoreType.DMA,
            pltpu.SemaphoreType.DMA,
        ],
        compiler_params=pltpu.CompilerParams(
            collective_id=3, has_side_effects=True, vmem_limit_bytes=56 * 2**20
        ),
        cost_estimate=pl.CostEstimate(
            flops=2 * rows * width * own.shape[1], bytes_accessed=8 * own.size, transcendentals=0
        ),
        name="end",
    )(own, matrix, first, total, sent, *sums)


def attend_step(q_ref, k_ref, v_ref, ok_ref, ov_ref, mask_ref, out_ref, lse_ref, *, head, exact):
    rows = q_ref.shape[1]
    half = rows // 2
    heads = LANES // head
    scale = jnp.asarray(head**-0.5, LOW)
    queries = q_ref[0]
    own_keys = k_ref[0] * scale
    own_values = v_ref[0]
    keys = cat([own_keys[:half], ok_ref[0] * scale], axis=0)
    near = own_keys[half:]
    values_t = cat([own_values[:half], ov_ref[0]], axis=0).T
    near_values_t = own_values[half:].T
    lane = lax.broadcasted_iota(jnp.int32, (1, LANES), 1) // head
    spans = [(start, start + CLEN) for start in range(0, half, CLEN)]
    picked = lax.broadcasted_iota(jnp.int32, (8, LANES), 0) == lane
    chooser = jnp.where(picked, 1.0, 0.0).astype(LOW)

    def with_ones(value):
        return cat([value, jnp.ones((16, value.shape[1]), LOW)], axis=0)

    def squares(value):
        return nt(chooser, value * value)

    flags = []
    if not exact:
        largest = jnp.maximum(
            jnp.max(squares(keys), axis=1, keepdims=True),
            jnp.max(squares(near), axis=1, keepdims=True),
        )
        bound = jnp.sqrt(squares(queries) * largest) * LOG2E
    for part in range(2):
        span = slice(part * half, (part + 1) * half)
        query = queries[span]
        outs = []
        for h in range(heads):
            pick = lane == h
            lines = slice(h * head, (h + 1) * head)
            scores = nt(only(pick, keys), query)
            if part:
                near_keys = only(pick, near)
                local = cat([nt(near_keys[a:b], query[a:b]) for a, b in spans], axis=1)
                local = local + mask_ref[0]
            if exact:
                top = jnp.max(scores, axis=0, keepdims=True)
                if part:
                    top = jnp.maximum(top, jnp.max(local, axis=0, keepdims=True))
                top = top * LOG2E
            else:
                top = bound[h : h + 1, span]
            weights = jnp.exp2(scores * LOG2E - top).astype(LOW)
            mixed = nn(with_ones(values_t[lines]), weights)
            if part:
                weights = jnp.exp2(local * LOG2E - top).astype(LOW)
                value = with_ones(near_values_t[lines])
                mixed = mixed + cat([nn(value[:, a:b], weights[:, a:b]) for a, b in spans], axis=1)
            total = mixed[head : head + 1]
            fine = jnp.logical_and(total > 1e-25, total < 1e30)
            flags.append(jnp.where(fine, 0.0, 1.0))
            outs.append(mixed[:head] / total)
            lse_ref[0, 0, h : h + 1, span] = top + jnp.log2(total)
        out_ref[0, span] = cat(outs, axis=0).T.astype(LOW)
    return sum(flags[1:], flags[0])


def attend_again_kernel(*refs, head):
    attend_step(*refs, head=head, exact=True)


def attend_kernel(
    q_ref, k_ref, v_ref, ok_ref, ov_ref, mask_ref, out_block, up_block, down_block, moved_block,
    out_ref, lse_ref, flag_ref, out_whole, up_whole, down_whole,
    sends, arrivals, placed, *held, head, grid,
):
    rows, columns = grid
    steps = pl.num_programs(1)
    step = pl.program_id(0) * steps + pl.program_id(1)
    final = 2 * steps - 1
    row_bits, col_bits = bits_of("row", rows), bits_of("col", columns)
    first_order = tuple(col_bits + row_bits[::-1])
    second_order = tuple(row_bits[:0:-1] + col_bits + row_bits[:1])
    per = len(spread(first_order))
    half = up_block.shape[0] // 2
    down_moved = (row_bits[-1], moved_block)
    parts = [
        Gather(out_block, out_whole, first_order, sends, arrivals, 0),
        Gather(down_block, down_whole, first_order, sends, arrivals, per, moved=down_moved),
        Gather(up_block, up_whole, second_order, sends, arrivals, 2 * per, (0, half)),
        Gather(up_block, up_whole, first_order, sends, arrivals, 3 * per, (half, half)),
    ]
    locals_ = [pair for part in parts for pair in part.placed()]

    def load(number):
        return pltpu.make_async_copy(locals_[number][0], held[number], placed.at[number, 0])

    def store(number):
        return pltpu.make_async_copy(held[number], locals_[number][1], placed.at[number, 1])

    @pl.when(step == 0)
    def _():
        greet(row_bits + col_bits)
        for index in range(per):
            for part in parts:
                if index in part.first():
                    part.copy(index).start()
        for number in range(len(held)):
            load(number).start()

    @pl.when(step == 1)
    def _():
        for number in range(len(held)):
            load(number).wait()
            store(number).start()

    reached = (
        {("col",): 2, ("row",): 4, ("col", "row"): 7},
        {("col",): 6, ("row",): 1},
        {("row",): 3, ("col",): 10},
        {("col",): 8, ("row",): 6},
    )
    events = {}
    for number, part in enumerate(parts):
        for index in part.later():
            crossed = tuple(axis for axis, mask in part.copies[index][1])
            when = min(reached[number].get(crossed, final), final)
            events.setdefault(when, []).append((part, index))
    waited = set()

    def forward(batch):
        for part, index in batch:
            origin = part.source(index)
            if origin is not None and (part.base, origin) not in waited:
                waited.add((part.base, origin))
                part.arrival(origin).wait_recv()
            part.copy(index).start()

    for when in sorted(events):
        if when < final:
            pl.when(step == when)(functools.partial(forward, events[when]))

    flags = attend_step(
        q_ref, k_ref, v_ref, ok_ref, ov_ref, mask_ref, out_ref, lse_ref, head=head, exact=False
    )
    flag_ref[0, 0] = jnp.broadcast_to(flags, flag_ref.shape[2:])

    @pl.when(step == final)
    def _():
        forward(events.get(final, []))
        for number in range(len(held)):
            store(number).wait()
        for part in parts:
            for index in part.used():
                if (part.base, index) not in waited:
                    part.arrival(index).wait_recv()
                part.copy(index).wait_send()


def attend_specs(own, other, mask):
    batch, rows, columns = own.shape
    steps = columns // (3 * LANES)

    def spec(count, offset):
        return pl.BlockSpec((1, count, LANES), lambda m, p: (m, 0, offset * steps + p))

    ins = [
        spec(rows, 0),
        spec(rows, 1),
        spec(rows, 2),
        spec(rows // 2, 0),
        spec(rows // 2, 1),
        pl.BlockSpec((1,) + mask.shape[1:], lambda m, p: (m, 0, 0)),
    ]
    return batch, rows, steps, spec, ins


def attend_again(own, other, mask, head):
    batch, rows, steps, spec, ins = attend_specs(own, other, mask)
    heads = LANES // head
    return pl.pallas_call(
        functools.partial(attend_again_kernel, head=head),
        grid=(batch, steps),
        in_specs=ins,
        out_specs=[spec(rows, 0), pl.BlockSpec((1, 1, heads, rows), lambda m, p: (m, p, 0, 0))],
        out_shape=[
            jax.ShapeDtypeStruct((batch, rows, steps * LANES), LOW),
            jax.ShapeDtypeStruct((batch, steps, heads, rows), FULL),
        ],
        name="attend_again",
    )(own, own, own, other, other, mask)


def attend(own, other, mask, blocks, moved, grid, head):
    batch, rows, steps, spec, ins = attend_specs(own, other, mask)
    heads = LANES // head
    half = rows // 2
    anywhere = pl.BlockSpec(memory_space=pl.ANY)
    copies = 4 * (grid[0] * grid[1] - 1)
    out_shape, up_shape, down_shape = (block.shape for block in blocks)
    half_shape = (up_shape[0] // 2, up_shape[1])
    held = [out_shape, down_shape, down_shape, half_shape, half_shape]
    work = batch * rows * (rows + CLEN) * steps * LANES
    wholes = [
        jax.ShapeDtypeStruct((block.shape[0] * grid[0], block.shape[1] * grid[1]), LOW)
        for block in blocks
    ]
    out, lse, flags, *wholes = pl.pallas_call(
        functools.partial(attend_kernel, head=head, grid=grid),
        grid=(batch, steps),
        in_specs=ins + [anywhere] * 4,
        out_specs=[
            spec(rows, 0),
            pl.BlockSpec((1, 1, heads, rows), lambda m, p: (m, p, 0, 0)),
            pl.BlockSpec((1, 1, 8, half), lambda m, p: (m, p, 0, 0)),
        ]
        + [anywhere] * 3,
        out_shape=[
            jax.ShapeDtypeStruct((batch, rows, steps * LANES), LOW),
            jax.ShapeDtypeStruct((batch, steps, heads, rows), FULL),
            jax.ShapeDtypeStruct((batch, steps, 8, half), FULL),
        ]
        + wholes,
        scratch_shapes=[
            pltpu.SemaphoreType.DMA((copies,)),
            pltpu.SemaphoreType.DMA((copies,)),
            pltpu.SemaphoreType.DMA((len(held), 2)),
        ]
        + [pltpu.VMEM(shape, LOW) for shape in held],
        compiler_params=pltpu.CompilerParams(collective_id=1, has_side_effects=True),
        cost_estimate=pl.CostEstimate(
            flops=16 * work, bytes_accessed=own.size * 4, transcendentals=work // head
        ),
        name="attend",
    )(own, own, own, other, other, mask, *blocks, moved)
    _, out, lse = lax.while_loop(
        lambda state: state[0] > 0.5,
        lambda state: (jnp.zeros((), FULL), *attend_again(own, other, mask, head)),
        (jnp.max(flags), out, lse),
    )
    return out, lse, wholes


def begin_kernel(tokens_ref, block_ref, other_ref, whole_ref, sends, arrivals, placed, held, *, grid):
    rows, columns = grid
    row_bits, col_bits = bits_of("row", rows), bits_of("col", columns)
    order = tuple(col_bits + row_bits[::-1])
    part = Gather(block_ref, whole_ref, order, sends, arrivals, 0)
    per = len(part.copies)
    exchange = pltpu.make_async_remote_copy(
        src_ref=tokens_ref.at[0, pl.ds(0, other_ref.shape[0])],
        dst_ref=other_ref,
        send_sem=sends.at[per],
        recv_sem=arrivals.at[per],
        device_id=flipped(here(("col",)), "col", 1),
        device_id_type=pl.DeviceIdType.MESH,
    )
    greet(row_bits + col_bits)
    for index in part.first():
        part.copy(index).start()
    exchange.start()
    source, slot = part.placed()[0]
    load = pltpu.make_async_copy(source, held, placed.at[0])
    store = pltpu.make_async_copy(held, slot, placed.at[1])
    load.start()
    load.wait()
    store.start()
    waited = set()
    for index in part.later():
        origin = part.source(index)
        if origin not in waited:
            waited.add(origin)
            part.arrival(origin).wait_recv()
        part.copy(index).start()
    for index in range(per):
        if index not in waited:
            part.arrival(index).wait_recv()
        part.copy(index).wait_send()
    store.wait()
    exchange.wait()


def begin(tokens, block, grid):
    batch, rows, width = tokens.shape
    copies = grid[0] * grid[1]
    anywhere = pl.BlockSpec(memory_space=pl.ANY)
    return pl.pallas_call(
        functools.partial(begin_kernel, grid=grid),
        in_specs=[anywhere] * 2,
        out_specs=[anywhere] * 2,
        out_shape=[
            jax.ShapeDtypeStruct((rows // 2, width), LOW),
            jax.ShapeDtypeStruct((block.shape[0] * grid[0], block.shape[1] * grid[1]), LOW),
        ],
        scratch_shapes=[
            pltpu.SemaphoreType.DMA((copies,)),
            pltpu.SemaphoreType.DMA((copies,)),
            pltpu.SemaphoreType.DMA((2,)),
            pltpu.VMEM(block.shape, LOW),
        ],
        compiler_params=pltpu.CompilerParams(collective_id=0, has_side_effects=True),
        cost_estimate=pl.CostEstimate(
            flops=0, bytes_accessed=block.size * copies * 16, transcendentals=0
        ),
        name="begin",
    )(tokens, block)


def attend_back_kernel(
    q_ref, k_ref, v_ref, ok_ref, ov_ref, mask_ref, out_ref, grad_ref, lse_ref,
    *rest, head, scale, grid, dp,
):
    if grid is not None:
        totals_in, matrices_in, rest = rest[:3], rest[3:5], rest[5:]
    own_grad_ref, other_grad_ref, sums_ref, *rest = rest
    if grid is not None:
        blocks_out, early_ref, rest = rest[:3], rest[3], rest[4:]
    own_scratch, other_scratch, stored, *scratch = rest
    rows = q_ref.shape[1]
    half = rows // 2
    heads = LANES // head
    steps = pl.num_programs(1)
    group, tile = pl.program_id(0), pl.program_id(1)
    step = group * steps + tile
    slot = step % 2

    def stores(group, tile, slot):
        copies = []
        for part in range(3):
            lanes = pl.ds(pl.multiple_of((part * steps + tile) * LANES, LANES), LANES)
            copies.append(
                pltpu.make_async_copy(
                    own_scratch.at[slot, part], own_grad_ref.at[group, :, lanes], stored.at[slot, part]
                )
            )
        for part in range(2):
            lanes = pl.ds(pl.multiple_of((part * steps + tile) * LANES, LANES), LANES)
            copies.append(
                pltpu.make_async_copy(
                    other_scratch.at[slot, part],
                    other_grad_ref.at[group, :, lanes],
                    stored.at[slot, 3 + part],
                )
            )
        return copies

    @pl.when(step >= 2)
    def _():
        for copy in stores((step - 2) // steps, (step - 2) % steps, slot):
            copy.wait()

    launches = {}
    if grid is not None:
        final = pl.num_programs(0) * steps - 1
        row_bits, col_bits = bits_of("row", grid[0]), bits_of("col", grid[1])
        across = across_bits("dp", dp)
        by_row = tuple(row_bits + col_bits[::-1])
        parts = []
        for number, hops in enumerate((tuple(across), tuple(across))):
            buffers, sends, arrivals = scratch[3 * number : 3 * number + 3]
            parts.append(Chain(totals_in[number], buffers, sends, arrivals, hops))
        acc, arrived, chain, sends, arrivals, loads = scratch[6:12]
        last = Reduce(
            totals_in[2], 0, acc, arrived, chain, sends, arrivals, loads, by_row, tuple(across)
        )
        last.size = blocks_out[2].shape[0]
        parts.append(last)

        @pl.when(step == 0)
        def _():
            greet_all(row_bits, col_bits, across)
            for part in parts[:2]:
                part.launch(0)
            last.begin(last.size)

        kept, sent, sent_sem, early_sem = scratch[12:]
        exchange = pltpu.make_async_remote_copy(
            src_ref=sent,
            dst_ref=early_ref,
            send_sem=sent_sem,
            recv_sem=early_sem,
            device_id=flipped(here(("col",)), "col", 1),
            device_id_type=pl.DeviceIdType.MESH,
        )

        @pl.when(step == steps)
        def _():
            width = kept.shape[1] // 2
            value = nt(kept[:, :width], matrices_in[0][...]) + nt(kept[:, width:], matrices_in[1][...])
            sent[...] = value.astype(LOW)
            exchange.start()

        for hop in range(1, len(across)):
            launches.setdefault(min(2 * hop, final), []).append((parts[0], hop))
            launches.setdefault(min(2 * hop + 2, final), []).append((parts[1], hop))
        for stage in range(1, last.stages()):
            when = min((0, 1, 3, 5, 9)[stage] if stage < 5 else final, final)
            launches.setdefault(when, []).append((last, stage))
        for when in sorted(launches):

            @pl.when(step == when)
            def _(batch=launches[when]):
                for part, stage in batch:
                    part.prepare(stage)

    own_keys = k_ref[0] * jnp.asarray(scale, LOW)
    own_values = v_ref[0]
    keys = cat([own_keys[:half], ok_ref[0] * jnp.asarray(scale, LOW)], axis=0)
    near = own_keys[half:]
    values = cat([own_values[:half], ov_ref[0]], axis=0)
    near_values = own_values[half:]
    keys_t = keys.T
    near_t = near.T
    lane = lax.broadcasted_iota(jnp.int32, (1, LANES), 1) // head
    spans = [(start, start + CLEN) for start in range(0, half, CLEN)]
    totals = [None, None, None, None]
    query_sums = []

    def add(place, value):
        totals[place] = value if totals[place] is None else totals[place] + value

    for part in range(2):
        span = slice(part * half, (part + 1) * half)
        query = q_ref[0, span]
        grad = grad_ref[0, span]
        dots = (grad.astype(FULL) * out_ref[0, span].astype(FULL)).T
        query_grads = []
        for h in range(heads):
            pick = lane == h
            lines = slice(h * head, (h + 1) * head)
            lse = lse_ref[0, 0, h : h + 1, span]
            delta = jnp.sum(dots[lines], axis=0, keepdims=True)
            query_h = only(pick, query)
            grad_h = only(pick, grad)
            probs = jnp.exp2(nt(only(pick, keys), query) * LOG2E - lse)
            slopes = (probs * (nt(only(pick, values), grad) - delta)).astype(LOW)
            probs = probs.astype(LOW)
            query_grad = nn(keys_t[lines], slopes)
            add(0, nn(slopes, query_h))
            add(1, nn(probs, grad_h))
            if part:
                near_h = only(pick, near)
                near_values_h = only(pick, near_values)
                local = cat([nt(near_h[a:b], query[a:b]) for a, b in spans], axis=1)
                dlocal = cat([nt(near_values_h[a:b], grad[a:b]) for a, b in spans], axis=1)
                probs = jnp.exp2((local + mask_ref[0]) * LOG2E - lse)
                slopes = (probs * (dlocal - delta)).astype(LOW)
                probs = probs.astype(LOW)
                query_grad = query_grad + cat(
                    [nn(near_t[lines, a:b], slopes[:, a:b]) for a, b in spans], axis=1
                )
                add(2, cat([nn(slopes[:, a:b], query_h[a:b]) for a, b in spans], axis=0))
                add(3, cat([nn(probs[:, a:b], grad_h[a:b]) for a, b in spans], axis=0))
            query_grads.append(query_grad)
        query_grad = cat(query_grads, axis=0).T
        query_sums.append(folded(query_grad))
        own_scratch[slot, 0, span] = query_grad.astype(LOW)
    key_grad = (totals[0] * scale).astype(LOW)
    value_grad = totals[1].astype(LOW)
    own_scratch[slot, 1, :half] = key_grad[:half]
    own_scratch[slot, 2, :half] = value_grad[:half]
    own_scratch[slot, 1, half:] = (totals[2] * scale).astype(LOW)
    own_scratch[slot, 2, half:] = totals[3].astype(LOW)
    other_scratch[slot, 0] = key_grad[half:]
    other_scratch[slot, 1] = value_grad[half:]
    if grid is not None:
        for part in range(2):
            lanes = pl.ds(pl.multiple_of((part * steps + tile) * LANES, LANES), LANES)
            kept[:, lanes] = other_scratch[slot, part]
    sums_ref[0, 0, 0:8] = query_sums[0] + query_sums[1]
    sums_ref[0, 0, 8:16] = folded(totals[1]) + folded(totals[3])
    for copy in stores(group, tile, slot):
        copy.start()
    for when in sorted(launches):

        @pl.when(step == when)
        def _(batch=launches[when]):
            for part, stage in batch:
                part.launch(stage)

    if grid is not None:

        @pl.when(step == final)
        def _():
            for part, block in zip(parts, blocks_out):
                part.finish(block)
            exchange.wait()

    @pl.when(step == pl.num_programs(0) * steps - 1)
    def _():
        for copy in stores((step - 1) // steps, (step - 1) % steps, 1 - slot):
            copy.wait()
        for copy in stores(group, tile, slot):
            copy.wait()


def attend_back(
    own, other, mask, out, grad, lse, head, sums=None, matrix=None, shapes=None, grid=None, dp=1
):
    batch, rows, steps, spec, ins = attend_specs(own, other, mask)
    work = batch * rows * (rows + CLEN) * steps * LANES
    anywhere = pl.BlockSpec(memory_space=pl.ANY)
    more_in, more_out, more_shapes, more_scratch, operands = [], [], [], [], []
    params = None
    if grid is not None:
        width = steps * LANES
        once = pl.Buffered(buffer_count=1)
        more_in = [pl.BlockSpec(shape, lambda m, p: (0, 0)) for shape in shapes[:2]] + [anywhere]
        more_in += [
            pl.BlockSpec((width, width), lambda m, p: (0, 1), pipeline_mode=once),
            pl.BlockSpec((width, width), lambda m, p: (0, 2), pipeline_mode=once),
        ]
        more_out = [pl.BlockSpec(shape, lambda m, p: (0, 0)) for shape in shapes] + [anywhere]
        more_shapes = [jax.ShapeDtypeStruct(shape, FULL) for shape in shapes]
        more_shapes += [jax.ShapeDtypeStruct((rows // 2, width), LOW)]
        hops = dp.bit_length() - 1
        more_scratch = chain_scratch(shapes[:2], hops) + reduce_scratch(shapes[2:], grid, hops)
        more_scratch += [
            pltpu.VMEM((rows // 2, 2 * width), LOW),
            pltpu.VMEM((rows // 2, width), LOW),
            pltpu.SemaphoreType.DMA,
            pltpu.SemaphoreType.DMA,
        ]
        operands = list(sums) + [matrix, matrix]
        params = pltpu.CompilerParams(
            collective_id=2, has_side_effects=True, vmem_limit_bytes=60 * 2**20
        )
    return pl.pallas_call(
        functools.partial(attend_back_kernel, head=head, scale=head**-0.5, grid=grid, dp=dp),
        grid=(batch, steps),
        in_specs=ins
        + [
            spec(rows, 0),
            spec(rows, 0),
            pl.BlockSpec((1, 1) + lse.shape[2:], lambda m, p: (m, p, 0, 0)),
        ]
        + more_in,
        out_specs=[anywhere] * 2
        + [pl.BlockSpec((1, 1, 16, LANES), lambda m, p: (m, p, 0, 0))]
        + more_out,
        out_shape=[
            jax.ShapeDtypeStruct(own.shape, LOW),
            jax.ShapeDtypeStruct(other.shape, LOW),
            jax.ShapeDtypeStruct((batch, steps, 16, LANES), FULL),
        ]
        + more_shapes,
        scratch_shapes=[
            pltpu.VMEM((2, 3, rows, LANES), LOW),
            pltpu.VMEM((2, 2, rows // 2, LANES), LOW),
            pltpu.SemaphoreType.DMA((2, 5)),
        ]
        + more_scratch,
        compiler_params=params,
        cost_estimate=pl.CostEstimate(
            flops=40 * work, bytes_accessed=own.size * 10, transcendentals=work // head
        ),
        name="attend_back",
    )(own, own, own, other, other, mask, out, grad, lse, *operands)


def swapped(value, axis, mask):
    pairs = [(source, source ^ mask) for source in range(lax.axis_size(axis))]
    return lax.ppermute(value, axis, pairs)


def masks_of(axis):
    return [1 << bit for bit in range(lax.axis_size(axis).bit_length() - 1)]


def bit_of(axis, mask):
    return jnp.where(lax.axis_index(axis) & mask == 0, 0, 1)


def joined(value, axis, mask, dim):
    other = swapped(value, axis, mask)
    first = bit_of(axis, mask) == 0
    return jnp.stack([jnp.where(first, value, other), jnp.where(first, other, value)], axis=dim)


def gathered(block):
    for mask in masks_of("col"):
        block = joined(block, "col", mask, 1).reshape(block.shape[0], -1)
    depth, columns = block.shape
    value = block[None]
    for mask in masks_of("row")[::-1]:
        value = joined(value, "row", mask, 1).reshape(-1, depth, columns)
    return value.reshape(-1, columns)


def parted(value, axis, mask, dim):
    bit = bit_of(axis, mask)
    keep = lax.dynamic_index_in_dim(value, bit, dim, keepdims=False)
    send = lax.dynamic_index_in_dim(value, 1 - bit, dim, keepdims=False)
    return keep + swapped(send.astype(LOW), axis, mask).astype(FULL)


def scattered(total, shape):
    value = total.reshape(-1, shape[0], total.shape[1])
    for mask in masks_of("row"):
        value = parted(value.reshape(-1, 2, *value.shape[1:]), "row", mask, 1)
    value = value.reshape(shape[0], -1)
    for mask in masks_of("col")[::-1]:
        value = parted(value.reshape(shape[0], 2, -1), "col", mask, 1)
    return over_dp(value)


def over_dp(value):
    for mask in masks_of("dp"):
        low = value.astype(LOW)
        value = low.astype(FULL) + swapped(low, "dp", 2 * mask - 1).astype(FULL)
    return value


def normalize(value):
    average = jnp.mean(value, axis=-1, keepdims=True)
    centred = value - average
    spread = jnp.mean(centred * centred, axis=-1, keepdims=True)
    inverse = lax.rsqrt(spread + EPSILON)
    return (centred * inverse, inverse)


def normalize_back(grad_normed, normed, inverse):
    first = jnp.mean(grad_normed, axis=-1, keepdims=True)
    second = jnp.mean(grad_normed * normed, axis=-1, keepdims=True)
    return inverse * (grad_normed - first - normed * second)


def near_mask(lengths, half):
    place = jnp.arange(CLEN, dtype=jnp.int32)[:, None]
    query = jnp.arange(half, dtype=jnp.int32)[None, :]
    limit = jnp.repeat(lengths, CLEN, axis=1)[:, None, :]
    seen = jnp.logical_and((place <= query % CLEN)[None], place[None] < limit)
    return jnp.where(seen, 0.0, -jnp.inf).astype(FULL)


def local(
    inputs,
    qkv_weight,
    out_weight,
    up_weight,
    down_weight,
    vectors,
    up_bias,
    cont_lengths,
    out_cotangent,
):
    grid_rows = lax.axis_size("row")
    grid_cols = lax.axis_size("col")
    place = lax.axis_index("col")
    side = place % 2
    batch, rows, width = inputs.shape
    half = rows // 2
    head = width // H
    half_conts = cont_lengths.shape[2] // 2
    group_lengths = lax.dynamic_index_in_dim(cont_lengths, place // 2, 1, keepdims=False)
    lengths = lax.dynamic_slice_in_dim(group_lengths, side * half_conts, half_conts, 1)
    mask = near_mask(lengths, half)

    grid = (grid_rows, grid_cols)
    direct = out_weight.shape[1] % LANES == 0 and qkv_weight.shape[1] % LANES == 0
    blocks = (out_weight, up_weight, down_weight)
    tokens = inputs.reshape(batch * rows, width)
    if direct:
        early, qkv_matrix = begin(inputs, qkv_weight, grid)
        late, moved, qkv_matrix = lax.optimization_barrier(
            (inputs[1:, :half], down_weight, qkv_matrix)
        )
        moved = swapped(moved, "row", masks_of("row")[-1])
        other_tokens = cat([early[None], swapped(late, "col", 1)], axis=0)
    else:
        other_tokens = swapped(inputs[:, :half], "col", 1)
        qkv_matrix = gathered(qkv_weight)
    other_tokens = other_tokens.reshape(batch * half, width)
    pair_matrix = qkv_matrix[:, width:]
    shift = cat([vectors[:, 0], jnp.zeros((width,), FULL), vectors[:, 1]])
    pair_shift = shift[width:]
    own = (nn(tokens, qkv_matrix) + shift).astype(LOW).reshape(batch, rows, 3 * width)
    other = (nn(other_tokens, pair_matrix) + pair_shift).astype(LOW)
    other = other.reshape(batch, half, 2 * width)
    if direct:
        attended, lse, (out_matrix, up_matrix, down_matrix) = attend(
            own, other, mask, blocks, moved, grid, head
        )
    else:
        attended, lse = attend_again(own, other, mask, head)
        out_matrix, up_matrix, down_matrix = (gathered(block) for block in blocks)
    attended = attended.reshape(batch * rows, width)
    first_sum = tokens.astype(FULL) + nn(attended, out_matrix) + vectors[:, 2]
    first_normed, first_inverse = normalize(first_sum)
    hidden = first_normed * vectors[:, 3] + vectors[:, 4]
    hidden_low = hidden.astype(LOW)
    pre_act = nn(hidden_low, up_matrix) + up_bias
    phi = 0.5 + 0.5 * lax.erf(pre_act * (0.5**0.5))
    slope = phi + pre_act * (jnp.exp(-0.5 * pre_act * pre_act) * ((2 * math.pi) ** -0.5))
    act_low = (pre_act * phi).astype(LOW)
    slope_low = slope.astype(LOW)
    second_sum = hidden + nn(act_low, down_matrix) + vectors[:, 5]
    second_normed, second_inverse = normalize(second_sum)
    result = (second_normed * vectors[:, 6] + vectors[:, 7]).astype(LOW)

    grad_out = out_cotangent.reshape(batch * rows, width).astype(FULL)
    grad_second = normalize_back(grad_out * vectors[:, 6], second_normed, second_inverse)
    grad_second_low = grad_second.astype(LOW)
    shapes = (down_weight.shape, up_weight.shape, out_weight.shape)
    down_total = tn(act_low, grad_second_low)
    if direct:
        grad_pre_low, up_total, bias_sums, down_block = widen(
            grad_second_low, hidden_low, down_matrix, slope_low, down_total.astype(LOW), shapes[0], grid
        )
        grad_first, grad_attended, out_total, norm_sums, up_block = narrow(
            grad_pre_low, grad_second_low, first_normed.astype(LOW), first_inverse, attended,
            up_matrix, out_matrix, vectors[:, 3][None], up_total, shapes[1], grid,
        )
        totals = [down_block, up_block, out_total]
    else:
        grad_pre = nt(grad_second_low, down_matrix) * slope_low.astype(FULL)
        grad_pre_low = grad_pre.astype(LOW)
        grad_hidden = grad_second + nt(grad_pre_low, up_matrix)
        grad_first = normalize_back(grad_hidden * vectors[:, 3], first_normed, first_inverse)
        grad_first_low = grad_first.astype(LOW)
        grad_attended = nt(grad_first_low, out_matrix).astype(LOW)
        totals = (down_total, tn(hidden_low, grad_pre_low), tn(attended, grad_first_low))
        first_sums = [
            jnp.sum(grad_first, axis=0),
            jnp.sum(grad_hidden * first_normed, axis=0),
            jnp.sum(grad_hidden, axis=0),
        ]
        bias_sum = jnp.sum(grad_pre, axis=0)
    operands = (
        own,
        other,
        mask,
        attended.reshape(batch, rows, width),
        grad_attended.reshape(batch, rows, width),
        lse,
        head,
    )
    if direct:
        own_grad, other_grad, pair_sums, down_grad, up_grad, out_grad, received = attend_back(
            *operands, totals, qkv_matrix, shapes, grid, lax.axis_size("dp")
        )
        sent = nt(other_grad[1:].reshape(-1, 2 * width), pair_matrix).astype(LOW)
        own_grad = own_grad.reshape(batch * rows, 3 * width)
        other_grad = other_grad.reshape(batch * half, 2 * width)
    else:
        own_grad, other_grad, pair_sums = attend_back(*operands)
        down_grad, up_grad, out_grad = (
            scattered(total, shape) for total, shape in zip(totals, shapes)
        )
        own_grad = own_grad.reshape(batch * rows, 3 * width)
        other_grad = other_grad.reshape(batch * half, 2 * width)
        sent = nt(other_grad, pair_matrix).astype(LOW).reshape(batch, half, width)
        received = swapped(sent, "col", 1).astype(FULL)
        grad_tokens = (grad_first + nt(own_grad, qkv_matrix)).reshape(batch, rows, width)
        grad_tokens = cat([grad_tokens[:, :half] + received, grad_tokens[:, half:]], axis=1)
        grad_tokens = grad_tokens.astype(LOW)
    qkv_total = tn(tokens, own_grad)
    pair_total = tn(other_tokens, other_grad)
    qkv_total = cat([qkv_total[:, :width], qkv_total[:, width:] + pair_total], axis=1)
    last_sums = [
        jnp.sum(grad_second, axis=0),
        jnp.sum(grad_out * second_normed, axis=0),
        jnp.sum(grad_out, axis=0),
    ]
    if direct:
        grad_tokens, qkv_grad, sums, late = end(
            own_grad, qkv_matrix, grad_first, qkv_total.astype(LOW), sent,
            (pair_sums, norm_sums, bias_sums, jnp.stack(last_sums)),
            qkv_weight.shape, grid, lax.axis_size("dp"),
        )
        received = cat([received[None], late.reshape(batch - 1, half, width)], axis=0)
        received = jnp.pad(received, ((0, 0), (0, rows - half), (0, 0))).astype(FULL)
        grad_tokens = (grad_tokens.reshape(batch, rows, width).astype(FULL) + received).astype(LOW)
        sums = sums.reshape(-1)[: 8 * width + up_bias.shape[0]]
    else:
        qkv_grad = scattered(qkv_total, qkv_weight.shape)
        pair_sums = jnp.sum(pair_sums, axis=0)
        pair_sums = [jnp.sum(pair_sums[:, i : i + 8], axis=1).reshape(width) for i in (0, 8)]
        sums = lax.psum(cat([*pair_sums, *first_sums, *last_sums, bias_sum]), ("dp", "row", "col"))
    index = lax.axis_index("row") * grid_cols + place
    devices = grid_rows * grid_cols
    split = sums[: 8 * width].reshape(8, width)
    vector_grad = lax.dynamic_slice_in_dim(split, index * (width // devices), width // devices, 1).T
    bias = sums[8 * width :]
    count = bias.shape[0] // devices
    bias_grad = lax.dynamic_slice_in_dim(bias, index * count, count, 0)
    return (
        result.reshape(batch, rows, width),
        grad_tokens,
        qkv_grad,
        out_grad,
        up_grad,
        down_grad,
        vector_grad,
        bias_grad,
    )


def solution(mesh):
    everywhere = ("dp", "row", "col")
    tokens = P(None, everywhere, None)
    matrix = P("row", "col")
    return jax.shard_map(
        local,
        mesh=mesh,
        in_specs=(
            tokens, matrix, matrix, matrix, matrix, P(), P(), P(None, ("dp", "row"), None), tokens,
        ),
        out_specs=(
            tokens, tokens, matrix, matrix, matrix, matrix, P(("row", "col"), None), P(("row", "col")),
        ),
        check_vma=False,
    )
```

```python
import functools
import math

import jax
import jax.numpy as jnp
from jax import lax
from jax.experimental import pallas as pl
from jax.experimental.pallas import tpu as pltpu
from jax.sharding import PartitionSpec as P

H = 12
CLEN = 128
LANES = 128
EPSILON = 1e-05
LOG2E = math.log2(math.e)
LOW = jnp.bfloat16
FULL = jnp.float32
cat = jnp.concatenate


def nt(left, right):
    return lax.dot_general(left, right, (((1,), (1,)), ((), ())), preferred_element_type=FULL)


def nn(left, right):
    return lax.dot_general(left, right, (((1,), (0,)), ((), ())), preferred_element_type=FULL)


def tn(left, right):
    return lax.dot_general(left, right, (((0,), (0,)), ((), ())), preferred_element_type=FULL)


def folded(value):
    return jnp.sum(value.reshape(-1, 8, value.shape[1]), axis=0)


def only(pick, value):
    return jnp.where(pick, value, jnp.zeros_like(value))


def spread(order):
    listed = []
    for stage in range(len(order)):
        for code in range(1 << stage):
            listed.append((stage, tuple(order[i] for i in range(stage) if code >> i & 1)))
    return listed


def flipped(position, axis, mask):
    bit = position[axis] // mask % 2
    return {**position, axis: position[axis] + mask * (1 - 2 * bit)}


def place_of(position, crossed):
    for axis, mask in crossed:
        position = flipped(position, axis, mask)
    return position


def here(axes):
    return {axis: lax.axis_index(axis) for axis in axes}


def bits_of(axis, size):
    return [(axis, 1 << bit) for bit in range(size.bit_length() - 1)]


def greet(partners):
    barrier = pltpu.get_barrier_semaphore()
    for axis, mask in partners:
        target = flipped(here((axis,)), axis, mask)
        pl.semaphore_signal(barrier, inc=1, device_id=target, device_id_type=pl.DeviceIdType.MESH)
    pl.semaphore_wait(barrier, len(partners))


class Gather:
    def __init__(self, own, whole, order, sends, arrivals, base, rows=None, moved=None):
        self.own, self.whole, self.order = own, whole, order
        self.sends, self.arrivals, self.base = sends, arrivals, base
        self.low, self.count = rows if rows else (0, own.shape[0])
        self.copies = spread(order)
        self.position = here(("row", "col"))
        self.bit, self.moved = moved if moved else (None, None)

    def slot(self, position):
        depth, columns = self.own.shape
        first = pl.multiple_of(position["row"] * depth + self.low, 16)
        start = pl.multiple_of(position["col"] * columns, LANES)
        return self.whole.at[pl.ds(first, self.count), pl.ds(start, columns)]

    def origin(self, crossed):
        if not crossed:
            return self.own.at[pl.ds(self.low, self.count)]
        return self.moved if crossed == (self.bit,) else self.slot(place_of(self.position, crossed))

    def remote(self, index, source, slot):
        axis, mask = self.order[self.copies[index][0]]
        return pltpu.make_async_remote_copy(
            src_ref=source,
            dst_ref=slot,
            send_sem=self.sends.at[self.base + index],
            recv_sem=self.arrivals.at[self.base + index],
            device_id=flipped(here((axis,)), axis, mask),
            device_id_type=pl.DeviceIdType.MESH,
        )

    def copy(self, index):
        crossed = self.copies[index][1]
        return self.remote(index, self.origin(crossed), self.slot(place_of(self.position, crossed)))

    def arrival(self, index):
        stage, crossed = self.copies[index]
        slot = self.slot(place_of(self.position, crossed + (self.order[stage],)))
        return self.remote(index, slot, slot)

    def placed(self):
        pairs = [(self.origin(()), self.slot(self.position))]
        if self.bit:
            pairs.append((self.moved, self.slot(place_of(self.position, (self.bit,)))))
        return pairs

    def source(self, index):
        crossed = self.copies[index][1]
        last = self.order.index(crossed[-1])
        found = self.copies.index((last, crossed[:-1]))
        return found if self.sent(found) else None

    def sent(self, index):
        stage, crossed = self.copies[index]
        return bool(crossed) or self.order[stage] != self.bit

    def first(self):
        return [i for i, (stage, crossed) in enumerate(self.copies) if not crossed and self.sent(i)]

    def later(self):
        return [i for i, (stage, crossed) in enumerate(self.copies) if crossed]

    def used(self):
        return [i for i in range(len(self.copies)) if self.sent(i)]


class Reduce:
    def __init__(self, total, low, acc, arrived, chain, sends, arrivals, loads, order, across):
        self.total, self.low, self.acc, self.arrived, self.chain = total, low, acc, arrived, chain
        self.sends, self.arrivals, self.loads = sends, arrivals, loads
        self.order, self.across = order, across
        self.position = here(("row", "col"))
        self.settled = set()

    def slot(self, crossed, size):
        position = place_of(self.position, crossed)
        depth, columns = self.acc.shape[1:]
        first = pl.multiple_of(position["row"] * size + self.low, 16)
        start = pl.multiple_of(position["col"] * columns, LANES)
        return self.total.at[pl.ds(first, depth), pl.ds(start, columns)]

    def crossed(self, code):
        return tuple(bit for i, bit in enumerate(self.order[1:]) if code >> i & 1)

    def number(self, stage, code):
        count = len(self.order)
        return sum(1 << (count - 1 - s) for s in range(stage)) + code

    def copy(self, stage, code, source):
        axis, mask = self.order[stage]
        number = self.number(stage, code)
        return pltpu.make_async_remote_copy(
            src_ref=source,
            dst_ref=self.arrived.at[number],
            send_sem=self.sends.at[number],
            recv_sem=self.arrivals.at[number],
            device_id=flipped(here((axis,)), axis, mask),
            device_id_type=pl.DeviceIdType.MESH,
        )

    def load(self, code, size):
        return pltpu.make_async_copy(
            self.slot(self.crossed(code), size), self.acc.at[code], self.loads.at[code]
        )

    def outgoing(self, stage, code, size):
        if stage == 0:
            return self.copy(0, code, self.slot((self.order[0],) + self.crossed(code), size))
        return self.copy(stage, code, self.acc.at[code << stage | 1 << (stage - 1)])

    def begin(self, size):
        self.size = size
        for code in range(1 << (len(self.order) - 1))[::-1]:
            self.outgoing(0, code, size).start()
        for code in range(1 << (len(self.order) - 1))[::-1]:
            self.load(code, size).start()

    def settle(self, stage, code):
        if (stage, code) in self.settled:
            return
        self.settled.add((stage, code))
        entry = code << stage
        if stage == 0:
            self.load(code, self.size).wait()
        else:
            self.settle(stage - 1, 2 * code)
        self.outgoing(stage, code, self.size).wait_recv()
        number = self.number(stage, code)
        value = self.acc[entry].astype(FULL) + self.arrived[number].astype(FULL)
        self.acc[entry] = value.astype(LOW)

    def codes(self, stage):
        return range(1 << (len(self.order) - 1 - stage))[::-1]

    def prepare(self, stage):
        count = len(self.order)
        if stage < count:
            for code in self.codes(stage):
                self.settle(stage - 1, 2 * code + 1)
        elif stage == count:
            self.settle(count - 1, 0)
        else:
            hop = stage - count - 1
            self.hop(hop).wait_recv()
            before = self.acc[0] if hop == 0 else self.chain[len(self.across) + hop - 1]
            value = before.astype(FULL) + self.chain[hop].astype(FULL)
            self.chain[len(self.across) + hop] = value.astype(LOW)

    def hop(self, hop):
        axis, mask = self.across[hop]
        number = (1 << len(self.order)) - 1 + hop
        target = self.target(axis, mask)
        source = self.acc.at[0] if hop == 0 else self.chain.at[len(self.across) + hop - 1]
        return pltpu.make_async_remote_copy(
            src_ref=source,
            dst_ref=self.chain.at[hop],
            send_sem=self.sends.at[number],
            recv_sem=self.arrivals.at[number],
            device_id=target,
            device_id_type=pl.DeviceIdType.MESH,
        )

    @staticmethod
    def target(axis, mask):
        return across_target(axis, mask)

    def launch(self, stage):
        if stage < len(self.order):
            for code in self.codes(stage):
                self.outgoing(stage, code, self.size).start()
        else:
            self.hop(stage - len(self.order)).start()

    def stages(self):
        return len(self.order) + len(self.across)

    def close(self, out):
        self.settle(len(self.order) - 1, 0)
        out[...] = self.acc[0]
        self.sent()

    def sent(self):
        for stage in range(len(self.order)):
            for code in self.codes(stage):
                self.outgoing(stage, code, self.size).wait_send()

    def finish(self, out):
        hops = len(self.across)
        self.hop(hops - 1).wait_recv()
        before = self.acc[0] if hops == 1 else self.chain[2 * hops - 2]
        out[...] = before.astype(FULL) + self.chain[hops - 1].astype(FULL)
        self.sent()
        for hop in range(hops):
            self.hop(hop).wait_send()


def across_target(axis, mask):
    index = lax.axis_index(axis)
    return {axis: index // (mask + 1) * (mask + 1) + mask - index % (mask + 1)}


def across_bits(axis, size):
    return [(axis, (2 << bit) - 1) for bit in range(size.bit_length() - 1)]


class Chain:
    def __init__(self, start, buffers, sends, arrivals, across):
        self.start, self.buffers, self.across = start, buffers, across
        self.sends, self.arrivals = sends, arrivals

    def before(self, hop):
        return self.start if hop == 0 else self.buffers.at[len(self.across) + hop - 1]

    def hop(self, hop):
        axis, mask = self.across[hop]
        return pltpu.make_async_remote_copy(
            src_ref=self.before(hop),
            dst_ref=self.buffers.at[hop],
            send_sem=self.sends.at[hop],
            recv_sem=self.arrivals.at[hop],
            device_id=across_target(axis, mask),
            device_id_type=pl.DeviceIdType.MESH,
        )

    def total(self, hop):
        self.hop(hop).wait_recv()
        return self.before(hop)[...].astype(FULL) + self.buffers[hop].astype(FULL)

    def prepare(self, hop):
        self.buffers[len(self.across) + hop - 1] = self.total(hop - 1).astype(LOW)

    def launch(self, hop):
        self.hop(hop).start()

    def finish(self, out):
        out[...] = self.total(len(self.across) - 1)
        for hop in range(len(self.across)):
            self.hop(hop).wait_send()


def chain_scratch(blocks, hops):
    shapes = []
    for depth, columns in blocks:
        shapes += [
            pltpu.VMEM((2 * hops, depth, columns), LOW),
            pltpu.SemaphoreType.DMA((hops,)),
            pltpu.SemaphoreType.DMA((hops,)),
        ]
    return shapes


def halve_scratch(shape, grid):
    count = grid[0] * grid[1]
    depth, columns = shape
    return [
        pltpu.VMEM((count // 2, depth // 2, columns), LOW),
        pltpu.VMEM((count - 1, depth // 2, columns), LOW),
        pltpu.SemaphoreType.DMA((count - 1,)),
        pltpu.SemaphoreType.DMA((count - 1,)),
        pltpu.SemaphoreType.DMA((count // 2,)),
    ] * 2


class Halving:
    def __init__(self, total, out, scratch, grid, whens):
        self.row_bits, self.col_bits = bits_of("row", grid[0]), bits_of("col", grid[1])
        self.out, self.whens = out, whens
        self.depth = out.shape[0]
        first, later = tuple(self.row_bits[:1]), tuple(self.row_bits[1:])
        orders = [first + later + tuple(self.col_bits[::-1]), first + tuple(self.col_bits[::-1]) + later]
        self.parts = []
        for number, order in enumerate(orders):
            acc, arrived, sends, arrivals, loads = scratch[5 * number : 5 * number + 5]
            low = number * self.depth // 2
            self.parts.append(
                Reduce(total, low, acc, arrived, None, sends, arrivals, loads, order, ())
            )

    def before(self, step):
        @pl.when(step == 0)
        def _():
            greet(self.row_bits + self.col_bits)
            for part in self.parts:
                part.begin(self.depth)

        for part in self.parts:
            part.size = self.depth
        for stage in range(1, self.parts[0].stages()):

            @pl.when(step == self.whens[stage])
            def _(stage=stage):
                for part in self.parts:
                    part.prepare(stage)
                    part.launch(stage)

    def after(self, step, final):
        @pl.when(step == final)
        def _():
            half = self.depth // 2
            for number, part in enumerate(self.parts):
                part.close(self.out.at[pl.ds(number * half, half)])


def widen_kernel(
    second_ref, hidden_ref, down_ref, slope_ref, total_ref,
    grad_ref, up_ref, sums_ref, block_ref, turned, *scratch, grid, whens, chunk,
):
    step = pl.program_id(0)
    carried = Halving(total_ref, block_ref, scratch, grid, whens)
    carried.before(step)

    @pl.when(step == 0)
    def _():
        turned[...] = hidden_ref[...].T

    rows = grad_ref.shape[0]

    def part(index, total):
        span = pl.ds(pl.multiple_of(index * chunk, chunk), chunk)
        grad = nt(second_ref[span], down_ref[...]) * slope_ref[span].astype(FULL)
        grad_ref[span] = grad.astype(LOW)
        return total + jnp.sum(grad.reshape(chunk // 8, 8, grad.shape[1]), axis=0)

    sums_ref[...] = lax.fori_loop(0, rows // chunk, part, jnp.zeros(sums_ref.shape, FULL))
    up_ref[...] = nn(turned[...], grad_ref[...]).astype(LOW)
    carried.after(step, pl.num_programs(0) - 1)


def widen(second, hidden, down_matrix, slope, down_total, shape, grid):
    rows, width = second.shape
    hidden_units = down_matrix.shape[0]
    tile = 512
    steps = hidden_units // tile
    once = pl.Buffered(buffer_count=1)
    return pl.pallas_call(
        functools.partial(widen_kernel, grid=grid, whens=(0, 1, 4), chunk=min(rows, 1024)),
        grid=(steps,),
        in_specs=[
            pl.BlockSpec((rows, width), lambda i: (0, 0), pipeline_mode=once),
            pl.BlockSpec((rows, width), lambda i: (0, 0), pipeline_mode=once),
            pl.BlockSpec((tile, width), lambda i: (i, 0)),
            pl.BlockSpec((rows, tile), lambda i: (0, i)),
            pl.BlockSpec(memory_space=pl.ANY),
        ],
        out_specs=[
            pl.BlockSpec((rows, tile), lambda i: (0, i)),
            pl.BlockSpec((width, tile), lambda i: (0, i)),
            pl.BlockSpec((8, tile), lambda i: (0, i)),
            pl.BlockSpec(shape, lambda i: (0, 0)),
        ],
        out_shape=[
            jax.ShapeDtypeStruct((rows, hidden_units), LOW),
            jax.ShapeDtypeStruct((width, hidden_units), LOW),
            jax.ShapeDtypeStruct((8, hidden_units), FULL),
            jax.ShapeDtypeStruct(shape, LOW),
        ],
        scratch_shapes=[pltpu.VMEM((width, rows), LOW)] + halve_scratch(shape, grid),
        compiler_params=pltpu.CompilerParams(
            collective_id=4, has_side_effects=True, vmem_limit_bytes=56 * 2**20
        ),
        cost_estimate=pl.CostEstimate(
            flops=4 * rows * width * hidden_units, bytes_accessed=6 * rows * hidden_units, transcendentals=0
        ),
        name="widen",
    )(second, hidden, down_matrix, slope, down_total)


def narrow_kernel(
    grad_ref, second_ref, normed_ref, inverse_ref, attended_ref, up_ref, out_ref, gain_ref, total_ref,
    first_ref, back_ref, out_total_ref, sums_ref, block_ref, held, *scratch, grid, whens,
):
    step = pl.program_id(0)
    final = pl.num_programs(0) - 1
    carried = Halving(total_ref, block_ref, scratch, grid, whens)
    carried.before(step)

    @pl.when(step == 0)
    def _():
        held[...] = jnp.zeros(held.shape, FULL)
        sums_ref[...] = jnp.zeros(sums_ref.shape, FULL)

    grad_hidden = nt(grad_ref[...], up_ref[...]) + second_ref[...].astype(FULL)
    normed = normed_ref[...].astype(FULL)
    grad_first = normalize_back(grad_hidden * gain_ref[...], normed, inverse_ref[...])
    low = grad_first.astype(LOW)
    first_ref[...] = low
    back_ref[...] = nt(low, out_ref[...]).astype(LOW)
    held[...] += tn(attended_ref[...], low)

    sums_ref[0:8] += folded(grad_first)
    sums_ref[8:16] += folded(grad_hidden * normed)
    sums_ref[16:24] += folded(grad_hidden)
    carried.after(step, final)

    @pl.when(step == final)
    def _():
        out_total_ref[...] = held[...].astype(LOW)


def narrow(grad, second, normed, inverse, attended, up_matrix, out_matrix, gain, up_total, shape, grid):
    rows, width = second.shape
    hidden_units = grad.shape[1]
    tile = 256
    once = pl.Buffered(buffer_count=1)

    def block(columns):
        return pl.BlockSpec((tile, columns), lambda i: (i, 0))

    def whole(shape, **more):
        return pl.BlockSpec(shape, lambda i: (0, 0), **more)

    return pl.pallas_call(
        functools.partial(narrow_kernel, grid=grid, whens=(0, 1, 5)),
        grid=(rows // tile,),
        in_specs=[
            block(hidden_units),
            block(width),
            block(width),
            block(1),
            block(width),
            whole(up_matrix.shape, pipeline_mode=once),
            whole(out_matrix.shape, pipeline_mode=once),
            whole(gain.shape),
            pl.BlockSpec(memory_space=pl.ANY),
        ],
        out_specs=[
            block(width), block(width), whole(out_matrix.shape), whole((24, width)), whole(shape),
        ],
        out_shape=[
            jax.ShapeDtypeStruct((rows, width), LOW),
            jax.ShapeDtypeStruct((rows, width), LOW),
            jax.ShapeDtypeStruct(out_matrix.shape, LOW),
            jax.ShapeDtypeStruct((24, width), FULL),
            jax.ShapeDtypeStruct(shape, LOW),
        ],
        scratch_shapes=[pltpu.VMEM(out_matrix.shape, FULL)] + halve_scratch(shape, grid),
        compiler_params=pltpu.CompilerParams(
            collective_id=5, has_side_effects=True, vmem_limit_bytes=56 * 2**20
        ),
        cost_estimate=pl.CostEstimate(
            flops=2 * rows * width * (hidden_units + 2 * width),
            bytes_accessed=2 * rows * hidden_units,
            transcendentals=0,
        ),
        name="narrow",
    )(grad, second, normed, inverse, attended, up_matrix, out_matrix, gain, up_total)


def reduce_scratch(blocks, grid, hops):
    count = grid[0] * grid[1]
    shapes = []
    for depth, columns in blocks:
        shapes += [
            pltpu.VMEM((count // 2, depth, columns), LOW),
            pltpu.VMEM((count - 1, depth, columns), LOW),
            pltpu.VMEM((2 * hops, depth, columns), LOW),
            pltpu.SemaphoreType.DMA((count - 1 + hops,)),
            pltpu.SemaphoreType.DMA((count - 1 + hops,)),
            pltpu.SemaphoreType.DMA((count // 2,)),
        ]
    return shapes


def greet_all(row_bits, col_bits, across):
    barrier = pltpu.get_barrier_semaphore()
    targets = [flipped(here((axis,)), axis, mask) for axis, mask in row_bits + col_bits]
    targets += [across_target(axis, mask) for axis, mask in across]
    for target in targets:
        pl.semaphore_signal(barrier, inc=1, device_id=target, device_id_type=pl.DeviceIdType.MESH)
    pl.semaphore_wait(barrier, len(targets))


def end_kernel(
    own_ref, matrix_ref, first_ref, total_ref, sent_ref, pair_ref, norm_ref, bias_ref, last_ref,
    tokens_ref, out_ref, all_ref, came_ref, *scratch, grid, dp,
):
    step = pl.program_id(0)
    final = pl.num_programs(0) - 1
    rows, columns = grid
    row_bits, col_bits = bits_of("row", rows), bits_of("col", columns)
    across = across_bits("dp", dp)
    first, later = tuple(row_bits[:1]), tuple(row_bits[1:])
    orders = [first + later + tuple(col_bits[::-1]), first + tuple(col_bits[::-1]) + later]
    depth = out_ref.shape[0]
    part_depth = depth // 4
    parts = []
    for number in range(4):
        acc, arrived, chain, sends, arrivals, loads = scratch[6 * number : 6 * number + 6]
        part = Reduce(
            total_ref, number * part_depth, acc, arrived, chain, sends, arrivals, loads,
            orders[number % 2], tuple(across),
        )
        part.size = depth
        parts.append(part)
    running, came, small_sends, small_arrivals, sent_sem, came_sem = scratch[24:]
    exchange = pltpu.make_async_remote_copy(
        src_ref=sent_ref,
        dst_ref=came_ref,
        send_sem=sent_sem,
        recv_sem=came_sem,
        device_id=flipped(here(("col",)), "col", 1),
        device_id_type=pl.DeviceIdType.MESH,
    )
    targets = [flipped(here((axis,)), axis, mask) for axis, mask in row_bits + col_bits]
    targets += [across_target(axis, mask) for axis, mask in across]

    def small(stage):
        return pltpu.make_async_remote_copy(
            src_ref=running.at[stage],
            dst_ref=came.at[stage],
            send_sem=small_sends.at[stage],
            recv_sem=small_arrivals.at[stage],
            device_id=targets[stage],
            device_id_type=pl.DeviceIdType.MESH,
        )

    stages = len(targets)
    events = []
    for number, part in enumerate(parts):
        for stage in range(1, stages):
            late = 0 if number < 2 else (1.1 if stage == 1 else 2.1)
            events.append((stage + late, number, stage))
    whens = {1: 2, 2: 5, 3: 5}
    batches = {}
    for key, number, stage in sorted(events):
        batches.setdefault(min(whens.get(int(key), final), final), []).append((number, stage))

    def advance(batch):
        for number, stage in batch:
            parts[number].prepare(stage)
            parts[number].launch(stage)
            if number == 3 and stage == len(orders[0]) - 1:
                exchange.start()
            if number == 1:
                small(stage - 1).wait_recv()
                running[stage] = running[stage - 1] + came[stage - 1]
                small(stage).start()

    @pl.when(step == 0)
    def _():
        greet_all(row_bits, col_bits, across)
        for part in parts:
            part.begin(depth)
        running[0] = jnp.zeros(running.shape[1:], FULL)

        def column_sums(value):
            return jnp.sum(value, axis=0, keepdims=True)

        width = running.shape[2]
        tiles = pair_ref.shape[1]
        for kind in range(2):
            lines = slice(8 * kind, 8 * kind + 8)
            for tile in range(tiles):
                value = sum(pair_ref[m, tile, lines] for m in range(pair_ref.shape[0]))
                running[0, kind : kind + 1, tile * LANES : (tile + 1) * LANES] = column_sums(value)
        for number in range(3):
            running[0, 2 + number : 3 + number] = column_sums(norm_ref[8 * number : 8 * number + 8])
            running[0, 5 + number : 6 + number] = last_ref[number : number + 1]
        for number in range(bias_ref.shape[1] // width):
            value = bias_ref[:, number * width : (number + 1) * width]
            running[0, 8 + number : 9 + number] = column_sums(value)
        small(0).start()

    for when in sorted(batches):
        if when < final:
            pl.when(step == when)(functools.partial(advance, batches[when]))

    grad = nt(own_ref[...], matrix_ref[...]) + first_ref[...].astype(FULL)
    tokens_ref[...] = grad.astype(LOW)

    @pl.when(step == final)
    def _():
        advance(batches.get(final, []))
        for number, part in enumerate(parts):
            part.finish(out_ref.at[pl.ds(number * part_depth, part_depth)])
        small(stages - 1).wait_recv()
        all_ref[...] = running[stages - 1] + came[stages - 1]
        for stage in range(stages):
            small(stage).wait_send()
        exchange.wait()


def end(own, matrix, first, total, sent, sums, shape, grid, dp):
    lines = 8 + sums[2].shape[1] // first.shape[1]
    lines = (lines + -lines % 8, first.shape[1])
    hops = dp.bit_length() - 1
    stages = (grid[0] * grid[1] * dp).bit_length() - 1
    rows, width = first.shape
    tile = 256

    def block(columns):
        return pl.BlockSpec((tile, columns), lambda i: (i, 0))

    def whole(shape, **more):
        return pl.BlockSpec(shape, lambda i: (0, 0), **more)

    return pl.pallas_call(
        functools.partial(end_kernel, grid=grid, dp=dp),
        grid=(rows // tile,),
        in_specs=[
            block(own.shape[1]),
            whole(matrix.shape, pipeline_mode=pl.Buffered(buffer_count=1)),
            block(width),
            pl.BlockSpec(memory_space=pl.ANY),
            pl.BlockSpec(memory_space=pl.ANY),
            pl.BlockSpec(sums[0].shape, lambda i: (0, 0, 0, 0)),
            *(whole(value.shape) for value in sums[1:]),
        ],
        out_specs=[block(width), whole(shape), whole(lines), pl.BlockSpec(memory_space=pl.ANY)],
        out_shape=[
            jax.ShapeDtypeStruct((rows, width), LOW),
            jax.ShapeDtypeStruct(shape, FULL),
            jax.ShapeDtypeStruct(lines, FULL),
            jax.ShapeDtypeStruct(sent.shape, LOW),
        ],
        scratch_shapes=reduce_scratch([(shape[0] // 4, shape[1])] * 4, grid, hops)
        + [
            pltpu.VMEM((stages,) + lines, FULL),
            pltpu.VMEM((stages,) + lines, FULL),
            pltpu.SemaphoreType.DMA((stages,)),
            pltpu.SemaphoreType.DMA((stages,)),
            pltpu.SemaphoreType.DMA,
            pltpu.SemaphoreType.DMA,
        ],
        compiler_params=pltpu.CompilerParams(
            collective_id=3, has_side_effects=True, vmem_limit_bytes=56 * 2**20
        ),
        cost_estimate=pl.CostEstimate(
            flops=2 * rows * width * own.shape[1], bytes_accessed=8 * own.size, transcendentals=0
        ),
        name="end",
    )(own, matrix, first, total, sent, *sums)


def attend_step(q_ref, k_ref, v_ref, ok_ref, ov_ref, mask_ref, out_ref, lse_ref, *, head, exact):
    rows = q_ref.shape[1]
    half = rows // 2
    heads = LANES // head
    scale = jnp.asarray(head**-0.5, LOW)
    queries = q_ref[0]
    own_keys = k_ref[0] * scale
    own_values = v_ref[0]
    keys = cat([own_keys[:half], ok_ref[0] * scale], axis=0)
    near = own_keys[half:]
    values_t = cat([own_values[:half], ov_ref[0]], axis=0).T
    near_values_t = own_values[half:].T
    lane = lax.broadcasted_iota(jnp.int32, (1, LANES), 1) // head
    spans = [(start, start + CLEN) for start in range(0, half, CLEN)]
    picked = lax.broadcasted_iota(jnp.int32, (8, LANES), 0) == lane
    chooser = jnp.where(picked, 1.0, 0.0).astype(LOW)

    def with_ones(value):
        return cat([value, jnp.ones((16, value.shape[1]), LOW)], axis=0)

    def squares(value):
        return nt(chooser, value * value)

    flags = []
    if not exact:
        largest = jnp.maximum(
            jnp.max(squares(keys), axis=1, keepdims=True),
            jnp.max(squares(near), axis=1, keepdims=True),
        )
        bound = jnp.sqrt(squares(queries) * largest) * LOG2E
    for part in range(2):
        span = slice(part * half, (part + 1) * half)
        query = queries[span]
        outs = []
        for h in range(heads):
            pick = lane == h
            lines = slice(h * head, (h + 1) * head)
            scores = nt(only(pick, keys), query)
            if part:
                near_keys = only(pick, near)
                local = cat([nt(near_keys[a:b], query[a:b]) for a, b in spans], axis=1)
                local = local + mask_ref[0]
            if exact:
                top = jnp.max(scores, axis=0, keepdims=True)
                if part:
                    top = jnp.maximum(top, jnp.max(local, axis=0, keepdims=True))
                top = top * LOG2E
            else:
                top = bound[h : h + 1, span]
            weights = jnp.exp2(scores * LOG2E - top).astype(LOW)
            mixed = nn(with_ones(values_t[lines]), weights)
            if part:
                weights = jnp.exp2(local * LOG2E - top).astype(LOW)
                value = with_ones(near_values_t[lines])
                mixed = mixed + cat([nn(value[:, a:b], weights[:, a:b]) for a, b in spans], axis=1)
            total = mixed[head : head + 1]
            fine = jnp.logical_and(total > 1e-25, total < 1e30)
            flags.append(jnp.where(fine, 0.0, 1.0))
            outs.append(mixed[:head] / total)
            lse_ref[0, 0, h : h + 1, span] = top + jnp.log2(total)
        out_ref[0, span] = cat(outs, axis=0).T.astype(LOW)
    return sum(flags[1:], flags[0])


def attend_again_kernel(*refs, head):
    attend_step(*refs, head=head, exact=True)


def attend_kernel(
    q_ref, k_ref, v_ref, ok_ref, ov_ref, mask_ref, out_block, up_block, down_block, moved_block,
    out_ref, lse_ref, flag_ref, out_whole, up_whole, down_whole,
    sends, arrivals, placed, *held, head, grid,
):
    rows, columns = grid
    steps = pl.num_programs(1)
    step = pl.program_id(0) * steps + pl.program_id(1)
    final = 2 * steps - 1
    row_bits, col_bits = bits_of("row", rows), bits_of("col", columns)
    first_order = tuple(col_bits + row_bits[::-1])
    second_order = tuple(row_bits[:0:-1] + col_bits + row_bits[:1])
    per = len(spread(first_order))
    half = up_block.shape[0] // 2
    down_moved = (row_bits[-1], moved_block)
    parts = [
        Gather(out_block, out_whole, first_order, sends, arrivals, 0),
        Gather(down_block, down_whole, first_order, sends, arrivals, per, moved=down_moved),
        Gather(up_block, up_whole, second_order, sends, arrivals, 2 * per, (0, half)),
        Gather(up_block, up_whole, first_order, sends, arrivals, 3 * per, (half, half)),
    ]
    locals_ = [pair for part in parts for pair in part.placed()]

    def load(number):
        return pltpu.make_async_copy(locals_[number][0], held[number], placed.at[number, 0])

    def store(number):
        return pltpu.make_async_copy(held[number], locals_[number][1], placed.at[number, 1])

    @pl.when(step == 0)
    def _():
        greet(row_bits + col_bits)
        for index in range(per):
            for part in parts:
                if index in part.first():
                    part.copy(index).start()
        for number in range(len(held)):
            load(number).start()

    @pl.when(step == 1)
    def _():
        for number in range(len(held)):
            load(number).wait()
            store(number).start()

    reached = (
        {("col",): 2, ("row",): 4, ("col", "row"): 7},
        {("col",): 6, ("row",): 1},
        {("row",): 3, ("col",): 10},
        {("col",): 8, ("row",): 6},
    )
    events = {}
    for number, part in enumerate(parts):
        for index in part.later():
            crossed = tuple(axis for axis, mask in part.copies[index][1])
            when = min(reached[number].get(crossed, final), final)
            events.setdefault(when, []).append((part, index))
    waited = set()

    def forward(batch):
        for part, index in batch:
            origin = part.source(index)
            if origin is not None and (part.base, origin) not in waited:
                waited.add((part.base, origin))
                part.arrival(origin).wait_recv()
            part.copy(index).start()

    for when in sorted(events):
        if when < final:
            pl.when(step == when)(functools.partial(forward, events[when]))

    flags = attend_step(
        q_ref, k_ref, v_ref, ok_ref, ov_ref, mask_ref, out_ref, lse_ref, head=head, exact=False
    )
    flag_ref[0, 0] = jnp.broadcast_to(flags, flag_ref.shape[2:])

    @pl.when(step == final)
    def _():
        forward(events.get(final, []))
        for number in range(len(held)):
            store(number).wait()
        for part in parts:
            for index in part.used():
                if (part.base, index) not in waited:
                    part.arrival(index).wait_recv()
                part.copy(index).wait_send()


def attend_specs(own, other, mask):
    batch, rows, columns = own.shape
    steps = columns // (3 * LANES)

    def spec(count, offset):
        return pl.BlockSpec((1, count, LANES), lambda m, p: (m, 0, offset * steps + p))

    ins = [
        spec(rows, 0),
        spec(rows, 1),
        spec(rows, 2),
        spec(rows // 2, 0),
        spec(rows // 2, 1),
        pl.BlockSpec((1,) + mask.shape[1:], lambda m, p: (m, 0, 0)),
    ]
    return batch, rows, steps, spec, ins


def attend_again(own, other, mask, head):
    batch, rows, steps, spec, ins = attend_specs(own, other, mask)
    heads = LANES // head
    return pl.pallas_call(
        functools.partial(attend_again_kernel, head=head),
        grid=(batch, steps),
        in_specs=ins,
        out_specs=[spec(rows, 0), pl.BlockSpec((1, 1, heads, rows), lambda m, p: (m, p, 0, 0))],
        out_shape=[
            jax.ShapeDtypeStruct((batch, rows, steps * LANES), LOW),
            jax.ShapeDtypeStruct((batch, steps, heads, rows), FULL),
        ],
        name="attend_again",
    )(own, own, own, other, other, mask)


def attend(own, other, mask, blocks, moved, grid, head):
    batch, rows, steps, spec, ins = attend_specs(own, other, mask)
    heads = LANES // head
    half = rows // 2
    anywhere = pl.BlockSpec(memory_space=pl.ANY)
    copies = 4 * (grid[0] * grid[1] - 1)
    out_shape, up_shape, down_shape = (block.shape for block in blocks)
    half_shape = (up_shape[0] // 2, up_shape[1])
    held = [out_shape, down_shape, down_shape, half_shape, half_shape]
    work = batch * rows * (rows + CLEN) * steps * LANES
    wholes = [
        jax.ShapeDtypeStruct((block.shape[0] * grid[0], block.shape[1] * grid[1]), LOW)
        for block in blocks
    ]
    out, lse, flags, *wholes = pl.pallas_call(
        functools.partial(attend_kernel, head=head, grid=grid),
        grid=(batch, steps),
        in_specs=ins + [anywhere] * 4,
        out_specs=[
            spec(rows, 0),
            pl.BlockSpec((1, 1, heads, rows), lambda m, p: (m, p, 0, 0)),
            pl.BlockSpec((1, 1, 8, half), lambda m, p: (m, p, 0, 0)),
        ]
        + [anywhere] * 3,
        out_shape=[
            jax.ShapeDtypeStruct((batch, rows, steps * LANES), LOW),
            jax.ShapeDtypeStruct((batch, steps, heads, rows), FULL),
            jax.ShapeDtypeStruct((batch, steps, 8, half), FULL),
        ]
        + wholes,
        scratch_shapes=[
            pltpu.SemaphoreType.DMA((copies,)),
            pltpu.SemaphoreType.DMA((copies,)),
            pltpu.SemaphoreType.DMA((len(held), 2)),
        ]
        + [pltpu.VMEM(shape, LOW) for shape in held],
        compiler_params=pltpu.CompilerParams(collective_id=1, has_side_effects=True),
        cost_estimate=pl.CostEstimate(
            flops=16 * work, bytes_accessed=own.size * 4, transcendentals=work // head
        ),
        name="attend",
    )(own, own, own, other, other, mask, *blocks, moved)
    _, out, lse = lax.while_loop(
        lambda state: state[0] > 0.5,
        lambda state: (jnp.zeros((), FULL), *attend_again(own, other, mask, head)),
        (jnp.max(flags), out, lse),
    )
    return out, lse, wholes


def begin_kernel(tokens_ref, block_ref, other_ref, whole_ref, sends, arrivals, placed, held, *, grid):
    rows, columns = grid
    row_bits, col_bits = bits_of("row", rows), bits_of("col", columns)
    order = tuple(col_bits + row_bits[::-1])
    part = Gather(block_ref, whole_ref, order, sends, arrivals, 0)
    per = len(part.copies)
    exchange = pltpu.make_async_remote_copy(
        src_ref=tokens_ref.at[0, pl.ds(0, other_ref.shape[0])],
        dst_ref=other_ref,
        send_sem=sends.at[per],
        recv_sem=arrivals.at[per],
        device_id=flipped(here(("col",)), "col", 1),
        device_id_type=pl.DeviceIdType.MESH,
    )
    greet(row_bits + col_bits)
    for index in part.first():
        part.copy(index).start()
    exchange.start()
    source, slot = part.placed()[0]
    load = pltpu.make_async_copy(source, held, placed.at[0])
    store = pltpu.make_async_copy(held, slot, placed.at[1])
    load.start()
    load.wait()
    store.start()
    waited = set()
    for index in part.later():
        origin = part.source(index)
        if origin not in waited:
            waited.add(origin)
            part.arrival(origin).wait_recv()
        part.copy(index).start()
    for index in range(per):
        if index not in waited:
            part.arrival(index).wait_recv()
        part.copy(index).wait_send()
    store.wait()
    exchange.wait()


def begin(tokens, block, grid):
    batch, rows, width = tokens.shape
    copies = grid[0] * grid[1]
    anywhere = pl.BlockSpec(memory_space=pl.ANY)
    return pl.pallas_call(
        functools.partial(begin_kernel, grid=grid),
        in_specs=[anywhere] * 2,
        out_specs=[anywhere] * 2,
        out_shape=[
            jax.ShapeDtypeStruct((rows // 2, width), LOW),
            jax.ShapeDtypeStruct((block.shape[0] * grid[0], block.shape[1] * grid[1]), LOW),
        ],
        scratch_shapes=[
            pltpu.SemaphoreType.DMA((copies,)),
            pltpu.SemaphoreType.DMA((copies,)),
            pltpu.SemaphoreType.DMA((2,)),
            pltpu.VMEM(block.shape, LOW),
        ],
        compiler_params=pltpu.CompilerParams(collective_id=0, has_side_effects=True),
        cost_estimate=pl.CostEstimate(
            flops=0, bytes_accessed=block.size * copies * 16, transcendentals=0
        ),
        name="begin",
    )(tokens, block)


def attend_back_kernel(
    q_ref, k_ref, v_ref, ok_ref, ov_ref, mask_ref, out_ref, grad_ref, lse_ref,
    *rest, head, scale, grid, dp,
):
    if grid is not None:
        totals_in, matrices_in, rest = rest[:3], rest[3:5], rest[5:]
    own_grad_ref, other_grad_ref, sums_ref, *rest = rest
    if grid is not None:
        blocks_out, early_ref, rest = rest[:3], rest[3], rest[4:]
    own_scratch, other_scratch, stored, *scratch = rest
    rows = q_ref.shape[1]
    half = rows // 2
    heads = LANES // head
    steps = pl.num_programs(1)
    group, tile = pl.program_id(0), pl.program_id(1)
    step = group * steps + tile
    slot = step % 2

    def stores(group, tile, slot):
        copies = []
        for part in range(3):
            lanes = pl.ds(pl.multiple_of((part * steps + tile) * LANES, LANES), LANES)
            copies.append(
                pltpu.make_async_copy(
                    own_scratch.at[slot, part], own_grad_ref.at[group, :, lanes], stored.at[slot, part]
                )
            )
        for part in range(2):
            lanes = pl.ds(pl.multiple_of((part * steps + tile) * LANES, LANES), LANES)
            copies.append(
                pltpu.make_async_copy(
                    other_scratch.at[slot, part],
                    other_grad_ref.at[group, :, lanes],
                    stored.at[slot, 3 + part],
                )
            )
        return copies

    @pl.when(step >= 2)
    def _():
        for copy in stores((step - 2) // steps, (step - 2) % steps, slot):
            copy.wait()

    launches = {}
    if grid is not None:
        final = pl.num_programs(0) * steps - 1
        row_bits, col_bits = bits_of("row", grid[0]), bits_of("col", grid[1])
        across = across_bits("dp", dp)
        by_row = tuple(row_bits + col_bits[::-1])
        parts = []
        for number, hops in enumerate((tuple(across), tuple(across))):
            buffers, sends, arrivals = scratch[3 * number : 3 * number + 3]
            parts.append(Chain(totals_in[number], buffers, sends, arrivals, hops))
        acc, arrived, chain, sends, arrivals, loads = scratch[6:12]
        last = Reduce(
            totals_in[2], 0, acc, arrived, chain, sends, arrivals, loads, by_row, tuple(across)
        )
        last.size = blocks_out[2].shape[0]
        parts.append(last)

        @pl.when(step == 0)
        def _():
            greet_all(row_bits, col_bits, across)
            for part in parts[:2]:
                part.launch(0)
            last.begin(last.size)

        kept, sent, sent_sem, early_sem = scratch[12:]
        exchange = pltpu.make_async_remote_copy(
            src_ref=sent,
            dst_ref=early_ref,
            send_sem=sent_sem,
            recv_sem=early_sem,
            device_id=flipped(here(("col",)), "col", 1),
            device_id_type=pl.DeviceIdType.MESH,
        )

        @pl.when(step == steps)
        def _():
            width = kept.shape[1] // 2
            value = nt(kept[:, :width], matrices_in[0][...]) + nt(kept[:, width:], matrices_in[1][...])
            sent[...] = value.astype(LOW)
            exchange.start()

        for hop in range(1, len(across)):
            launches.setdefault(min(2 * hop, final), []).append((parts[0], hop))
            launches.setdefault(min(2 * hop + 2, final), []).append((parts[1], hop))
        for stage in range(1, last.stages()):
            when = min((0, 1, 3, 5, 9)[stage] if stage < 5 else final, final)
            launches.setdefault(when, []).append((last, stage))
        for when in sorted(launches):

            @pl.when(step == when)
            def _(batch=launches[when]):
                for part, stage in batch:
                    part.prepare(stage)
                    part.launch(stage)

    own_keys = k_ref[0] * jnp.asarray(scale, LOW)
    own_values = v_ref[0]
    keys = cat([own_keys[:half], ok_ref[0] * jnp.asarray(scale, LOW)], axis=0)
    near = own_keys[half:]
    values = cat([own_values[:half], ov_ref[0]], axis=0)
    near_values = own_values[half:]
    keys_t = keys.T
    near_t = near.T
    lane = lax.broadcasted_iota(jnp.int32, (1, LANES), 1) // head
    spans = [(start, start + CLEN) for start in range(0, half, CLEN)]
    totals = [None, None, None, None]
    query_sums = []

    def add(place, value):
        totals[place] = value if totals[place] is None else totals[place] + value

    for part in range(2):
        span = slice(part * half, (part + 1) * half)
        query = q_ref[0, span]
        grad = grad_ref[0, span]
        dots = (grad.astype(FULL) * out_ref[0, span].astype(FULL)).T
        query_grads = []
        for h in range(heads):
            pick = lane == h
            lines = slice(h * head, (h + 1) * head)
            lse = lse_ref[0, 0, h : h + 1, span]
            delta = jnp.sum(dots[lines], axis=0, keepdims=True)
            query_h = only(pick, query)
            grad_h = only(pick, grad)
            probs = jnp.exp2(nt(only(pick, keys), query) * LOG2E - lse)
            slopes = (probs * (nt(only(pick, values), grad) - delta)).astype(LOW)
            probs = probs.astype(LOW)
            query_grad = nn(keys_t[lines], slopes)
            add(0, nn(slopes, query_h))
            add(1, nn(probs, grad_h))
            if part:
                near_h = only(pick, near)
                near_values_h = only(pick, near_values)
                local = cat([nt(near_h[a:b], query[a:b]) for a, b in spans], axis=1)
                dlocal = cat([nt(near_values_h[a:b], grad[a:b]) for a, b in spans], axis=1)
                probs = jnp.exp2((local + mask_ref[0]) * LOG2E - lse)
                slopes = (probs * (dlocal - delta)).astype(LOW)
                probs = probs.astype(LOW)
                query_grad = query_grad + cat(
                    [nn(near_t[lines, a:b], slopes[:, a:b]) for a, b in spans], axis=1
                )
                add(2, cat([nn(slopes[:, a:b], query_h[a:b]) for a, b in spans], axis=0))
                add(3, cat([nn(probs[:, a:b], grad_h[a:b]) for a, b in spans], axis=0))
            query_grads.append(query_grad)
        query_grad = cat(query_grads, axis=0).T
        query_sums.append(folded(query_grad))
        own_scratch[slot, 0, span] = query_grad.astype(LOW)
    key_grad = (totals[0] * scale).astype(LOW)
    value_grad = totals[1].astype(LOW)
    own_scratch[slot, 1, :half] = key_grad[:half]
    own_scratch[slot, 2, :half] = value_grad[:half]
    own_scratch[slot, 1, half:] = (totals[2] * scale).astype(LOW)
    own_scratch[slot, 2, half:] = totals[3].astype(LOW)
    other_scratch[slot, 0] = key_grad[half:]
    other_scratch[slot, 1] = value_grad[half:]
    if grid is not None:
        for part in range(2):
            lanes = pl.ds(pl.multiple_of((part * steps + tile) * LANES, LANES), LANES)
            kept[:, lanes] = other_scratch[slot, part]
    sums_ref[0, 0, 0:8] = query_sums[0] + query_sums[1]
    sums_ref[0, 0, 8:16] = folded(totals[1]) + folded(totals[3])
    for copy in stores(group, tile, slot):
        copy.start()
    if grid is not None:

        @pl.when(step == final)
        def _():
            for part, block in zip(parts, blocks_out):
                part.finish(block)
            exchange.wait()

    @pl.when(step == pl.num_programs(0) * steps - 1)
    def _():
        for copy in stores((step - 1) // steps, (step - 1) % steps, 1 - slot):
            copy.wait()
        for copy in stores(group, tile, slot):
            copy.wait()


def attend_back(
    own, other, mask, out, grad, lse, head, sums=None, matrix=None, shapes=None, grid=None, dp=1
):
    batch, rows, steps, spec, ins = attend_specs(own, other, mask)
    work = batch * rows * (rows + CLEN) * steps * LANES
    anywhere = pl.BlockSpec(memory_space=pl.ANY)
    more_in, more_out, more_shapes, more_scratch, operands = [], [], [], [], []
    params = None
    if grid is not None:
        width = steps * LANES
        once = pl.Buffered(buffer_count=1)
        more_in = [pl.BlockSpec(shape, lambda m, p: (0, 0)) for shape in shapes[:2]] + [anywhere]
        more_in += [
            pl.BlockSpec((width, width), lambda m, p: (0, 1), pipeline_mode=once),
            pl.BlockSpec((width, width), lambda m, p: (0, 2), pipeline_mode=once),
        ]
        more_out = [pl.BlockSpec(shape, lambda m, p: (0, 0)) for shape in shapes] + [anywhere]
        more_shapes = [jax.ShapeDtypeStruct(shape, FULL) for shape in shapes]
        more_shapes += [jax.ShapeDtypeStruct((rows // 2, width), LOW)]
        hops = dp.bit_length() - 1
        more_scratch = chain_scratch(shapes[:2], hops) + reduce_scratch(shapes[2:], grid, hops)
        more_scratch += [
            pltpu.VMEM((rows // 2, 2 * width), LOW),
            pltpu.VMEM((rows // 2, width), LOW),
            pltpu.SemaphoreType.DMA,
            pltpu.SemaphoreType.DMA,
        ]
        operands = list(sums) + [matrix, matrix]
        params = pltpu.CompilerParams(
            collective_id=2, has_side_effects=True, vmem_limit_bytes=60 * 2**20
        )
    return pl.pallas_call(
        functools.partial(attend_back_kernel, head=head, scale=head**-0.5, grid=grid, dp=dp),
        grid=(batch, steps),
        in_specs=ins
        + [
            spec(rows, 0),
            spec(rows, 0),
            pl.BlockSpec((1, 1) + lse.shape[2:], lambda m, p: (m, p, 0, 0)),
        ]
        + more_in,
        out_specs=[anywhere] * 2
        + [pl.BlockSpec((1, 1, 16, LANES), lambda m, p: (m, p, 0, 0))]
        + more_out,
        out_shape=[
            jax.ShapeDtypeStruct(own.shape, LOW),
            jax.ShapeDtypeStruct(other.shape, LOW),
            jax.ShapeDtypeStruct((batch, steps, 16, LANES), FULL),
        ]
        + more_shapes,
        scratch_shapes=[
            pltpu.VMEM((2, 3, rows, LANES), LOW),
            pltpu.VMEM((2, 2, rows // 2, LANES), LOW),
            pltpu.SemaphoreType.DMA((2, 5)),
        ]
        + more_scratch,
        compiler_params=params,
        cost_estimate=pl.CostEstimate(
            flops=40 * work, bytes_accessed=own.size * 10, transcendentals=work // head
        ),
        name="attend_back",
    )(own, own, own, other, other, mask, out, grad, lse, *operands)


def swapped(value, axis, mask):
    pairs = [(source, source ^ mask) for source in range(lax.axis_size(axis))]
    return lax.ppermute(value, axis, pairs)


def masks_of(axis):
    return [1 << bit for bit in range(lax.axis_size(axis).bit_length() - 1)]


def bit_of(axis, mask):
    return jnp.where(lax.axis_index(axis) & mask == 0, 0, 1)


def joined(value, axis, mask, dim):
    other = swapped(value, axis, mask)
    first = bit_of(axis, mask) == 0
    return jnp.stack([jnp.where(first, value, other), jnp.where(first, other, value)], axis=dim)


def gathered(block):
    for mask in masks_of("col"):
        block = joined(block, "col", mask, 1).reshape(block.shape[0], -1)
    depth, columns = block.shape
    value = block[None]
    for mask in masks_of("row")[::-1]:
        value = joined(value, "row", mask, 1).reshape(-1, depth, columns)
    return value.reshape(-1, columns)


def parted(value, axis, mask, dim):
    bit = bit_of(axis, mask)
    keep = lax.dynamic_index_in_dim(value, bit, dim, keepdims=False)
    send = lax.dynamic_index_in_dim(value, 1 - bit, dim, keepdims=False)
    return keep + swapped(send.astype(LOW), axis, mask).astype(FULL)


def scattered(total, shape):
    value = total.reshape(-1, shape[0], total.shape[1])
    for mask in masks_of("row"):
        value = parted(value.reshape(-1, 2, *value.shape[1:]), "row", mask, 1)
    value = value.reshape(shape[0], -1)
    for mask in masks_of("col")[::-1]:
        value = parted(value.reshape(shape[0], 2, -1), "col", mask, 1)
    return over_dp(value)


def over_dp(value):
    for mask in masks_of("dp"):
        low = value.astype(LOW)
        value = low.astype(FULL) + swapped(low, "dp", 2 * mask - 1).astype(FULL)
    return value


def normalize(value):
    average = jnp.mean(value, axis=-1, keepdims=True)
    centred = value - average
    spread = jnp.mean(centred * centred, axis=-1, keepdims=True)
    inverse = lax.rsqrt(spread + EPSILON)
    return (centred * inverse, inverse)


def normalize_back(grad_normed, normed, inverse):
    first = jnp.mean(grad_normed, axis=-1, keepdims=True)
    second = jnp.mean(grad_normed * normed, axis=-1, keepdims=True)
    return inverse * (grad_normed - first - normed * second)


def near_mask(lengths, half):
    place = jnp.arange(CLEN, dtype=jnp.int32)[:, None]
    query = jnp.arange(half, dtype=jnp.int32)[None, :]
    limit = jnp.repeat(lengths, CLEN, axis=1)[:, None, :]
    seen = jnp.logical_and((place <= query % CLEN)[None], place[None] < limit)
    return jnp.where(seen, 0.0, -jnp.inf).astype(FULL)


def local(
    inputs,
    qkv_weight,
    out_weight,
    up_weight,
    down_weight,
    vectors,
    up_bias,
    cont_lengths,
    out_cotangent,
):
    grid_rows = lax.axis_size("row")
    grid_cols = lax.axis_size("col")
    place = lax.axis_index("col")
    side = place % 2
    batch, rows, width = inputs.shape
    half = rows // 2
    head = width // H
    half_conts = cont_lengths.shape[2] // 2
    group_lengths = lax.dynamic_index_in_dim(cont_lengths, place // 2, 1, keepdims=False)
    lengths = lax.dynamic_slice_in_dim(group_lengths, side * half_conts, half_conts, 1)
    mask = near_mask(lengths, half)

    grid = (grid_rows, grid_cols)
    direct = out_weight.shape[1] % LANES == 0 and qkv_weight.shape[1] % LANES == 0
    blocks = (out_weight, up_weight, down_weight)
    tokens = inputs.reshape(batch * rows, width)
    if direct:
        early, qkv_matrix = begin(inputs, qkv_weight, grid)
        late, moved, qkv_matrix = lax.optimization_barrier(
            (inputs[1:, :half], down_weight, qkv_matrix)
        )
        moved = swapped(moved, "row", masks_of("row")[-1])
        other_tokens = cat([early[None], swapped(late, "col", 1)], axis=0)
    else:
        other_tokens = swapped(inputs[:, :half], "col", 1)
        qkv_matrix = gathered(qkv_weight)
    other_tokens = other_tokens.reshape(batch * half, width)
    pair_matrix = qkv_matrix[:, width:]
    shift = cat([vectors[:, 0], jnp.zeros((width,), FULL), vectors[:, 1]])
    pair_shift = shift[width:]
    own = (nn(tokens, qkv_matrix) + shift).astype(LOW).reshape(batch, rows, 3 * width)
    other = (nn(other_tokens, pair_matrix) + pair_shift).astype(LOW)
    other = other.reshape(batch, half, 2 * width)
    if direct:
        attended, lse, (out_matrix, up_matrix, down_matrix) = attend(
            own, other, mask, blocks, moved, grid, head
        )
    else:
        attended, lse = attend_again(own, other, mask, head)
        out_matrix, up_matrix, down_matrix = (gathered(block) for block in blocks)
    attended = attended.reshape(batch * rows, width)
    first_sum = tokens.astype(FULL) + nn(attended, out_matrix) + vectors[:, 2]
    first_normed, first_inverse = normalize(first_sum)
    hidden = first_normed * vectors[:, 3] + vectors[:, 4]
    hidden_low = hidden.astype(LOW)
    pre_act = nn(hidden_low, up_matrix) + up_bias
    phi = 0.5 + 0.5 * lax.erf(pre_act * (0.5**0.5))
    slope = phi + pre_act * (jnp.exp(-0.5 * pre_act * pre_act) * ((2 * math.pi) ** -0.5))
    act_low = (pre_act * phi).astype(LOW)
    slope_low = slope.astype(LOW)
    second_sum = hidden + nn(act_low, down_matrix) + vectors[:, 5]
    second_normed, second_inverse = normalize(second_sum)
    result = (second_normed * vectors[:, 6] + vectors[:, 7]).astype(LOW)

    grad_out = out_cotangent.reshape(batch * rows, width).astype(FULL)
    grad_second = normalize_back(grad_out * vectors[:, 6], second_normed, second_inverse)
    grad_second_low = grad_second.astype(LOW)
    shapes = (down_weight.shape, up_weight.shape, out_weight.shape)
    down_total = tn(act_low, grad_second_low)
    if direct:
        grad_pre_low, up_total, bias_sums, down_block = widen(
            grad_second_low, hidden_low, down_matrix, slope_low, down_total.astype(LOW), shapes[0], grid
        )
        grad_first, grad_attended, out_total, norm_sums, up_block = narrow(
            grad_pre_low, grad_second_low, first_normed.astype(LOW), first_inverse, attended,
            up_matrix, out_matrix, vectors[:, 3][None], up_total, shapes[1], grid,
        )
        totals = [down_block, up_block, out_total]
    else:
        grad_pre = nt(grad_second_low, down_matrix) * slope_low.astype(FULL)
        grad_pre_low = grad_pre.astype(LOW)
        grad_hidden = grad_second + nt(grad_pre_low, up_matrix)
        grad_first = normalize_back(grad_hidden * vectors[:, 3], first_normed, first_inverse)
        grad_first_low = grad_first.astype(LOW)
        grad_attended = nt(grad_first_low, out_matrix).astype(LOW)
        totals = (down_total, tn(hidden_low, grad_pre_low), tn(attended, grad_first_low))
        first_sums = [
            jnp.sum(grad_first, axis=0),
            jnp.sum(grad_hidden * first_normed, axis=0),
            jnp.sum(grad_hidden, axis=0),
        ]
        bias_sum = jnp.sum(grad_pre, axis=0)
    operands = (
        own,
        other,
        mask,
        attended.reshape(batch, rows, width),
        grad_attended.reshape(batch, rows, width),
        lse,
        head,
    )
    if direct:
        own_grad, other_grad, pair_sums, down_grad, up_grad, out_grad, received = attend_back(
            *operands, totals, qkv_matrix, shapes, grid, lax.axis_size("dp")
        )
        sent = nt(other_grad[1:].reshape(-1, 2 * width), pair_matrix).astype(LOW)
        own_grad = own_grad.reshape(batch * rows, 3 * width)
        other_grad = other_grad.reshape(batch * half, 2 * width)
    else:
        own_grad, other_grad, pair_sums = attend_back(*operands)
        down_grad, up_grad, out_grad = (
            scattered(total, shape) for total, shape in zip(totals, shapes)
        )
        own_grad = own_grad.reshape(batch * rows, 3 * width)
        other_grad = other_grad.reshape(batch * half, 2 * width)
        sent = nt(other_grad, pair_matrix).astype(LOW).reshape(batch, half, width)
        received = swapped(sent, "col", 1).astype(FULL)
        grad_tokens = (grad_first + nt(own_grad, qkv_matrix)).reshape(batch, rows, width)
        grad_tokens = cat([grad_tokens[:, :half] + received, grad_tokens[:, half:]], axis=1)
        grad_tokens = grad_tokens.astype(LOW)
    qkv_total = tn(tokens, own_grad)
    pair_total = tn(other_tokens, other_grad)
    qkv_total = cat([qkv_total[:, :width], qkv_total[:, width:] + pair_total], axis=1)
    last_sums = [
        jnp.sum(grad_second, axis=0),
        jnp.sum(grad_out * second_normed, axis=0),
        jnp.sum(grad_out, axis=0),
    ]
    if direct:
        grad_tokens, qkv_grad, sums, late = end(
            own_grad, qkv_matrix, grad_first, qkv_total.astype(LOW), sent,
            (pair_sums, norm_sums, bias_sums, jnp.stack(last_sums)),
            qkv_weight.shape, grid, lax.axis_size("dp"),
        )
        received = cat([received[None], late.reshape(batch - 1, half, width)], axis=0)
        received = jnp.pad(received, ((0, 0), (0, rows - half), (0, 0))).astype(FULL)
        grad_tokens = (grad_tokens.reshape(batch, rows, width).astype(FULL) + received).astype(LOW)
        sums = sums.reshape(-1)[: 8 * width + up_bias.shape[0]]
    else:
        qkv_grad = scattered(qkv_total, qkv_weight.shape)
        pair_sums = jnp.sum(pair_sums, axis=0)
        pair_sums = [jnp.sum(pair_sums[:, i : i + 8], axis=1).reshape(width) for i in (0, 8)]
        sums = lax.psum(cat([*pair_sums, *first_sums, *last_sums, bias_sum]), ("dp", "row", "col"))
    index = lax.axis_index("row") * grid_cols + place
    devices = grid_rows * grid_cols
    split = sums[: 8 * width].reshape(8, width)
    vector_grad = lax.dynamic_slice_in_dim(split, index * (width // devices), width // devices, 1).T
    bias = sums[8 * width :]
    count = bias.shape[0] // devices
    bias_grad = lax.dynamic_slice_in_dim(bias, index * count, count, 0)
    return (
        result.reshape(batch, rows, width),
        grad_tokens,
        qkv_grad,
        out_grad,
        up_grad,
        down_grad,
        vector_grad,
        bias_grad,
    )


def solution(mesh):
    everywhere = ("dp", "row", "col")
    tokens = P(None, everywhere, None)
    matrix = P("row", "col")
    return jax.shard_map(
        local,
        mesh=mesh,
        in_specs=(
            tokens, matrix, matrix, matrix, matrix, P(), P(), P(None, ("dp", "row"), None), tokens,
        ),
        out_specs=(
            tokens, tokens, matrix, matrix, matrix, matrix, P(("row", "col"), None), P(("row", "col")),
        ),
        check_vma=False,
    )
```
